128 devices in a mesh: cam: 16 (over x, y_hi, core), fsdp: 8 (over z, y_lo).
Axes of the slice: x: 4, y: 4 (y_hi: 2, y_lo: 2; y = y_hi * 2 + y_lo), z: 4, core: 2. Of those that a mesh axis runs over, the one named last changes fastest.
Arguments:
- queries: bfloat16 [8, 2560, 4096], P('fsdp', 'cam'), may hold values from -16 to 16
- keys: bfloat16 [8, 2560, 4096], P('fsdp', 'cam'), may hold values from -16 to 16
- values: bfloat16 [8, 2560, 4096], P('fsdp', 'cam'), may hold values from -6 to 6
- out_weight: bfloat16 [4096, 5120], P('fsdp'), may hold values from -0.09375 to 0.09375
- block_counts: int32 [8, 16], P('fsdp', 'cam'), may hold values from 1 to 5, as said below
- row_mask: int32 [8, 2560], P('fsdp', 'cam'), may hold values from 0 to 1, as said below
Outputs:
- projected: bfloat16 [8, 2560, 5120], P('fsdp', 'cam')
The draws below stay inside these ranges and needn't reach their ends.
Inputs may be any that keep to these rules, and one draw needn't show every extreme that they name: `block_counts`: every view uses at least one block; in every clip one view uses all 5 blocks. `row_mask`: 0 or 1; the first two rows of every block are 1.
All inputs are finite; a program needn't handle non-finite values.
Results may differ from the reference program's by a relative error of at most 0.0057.
Values may be sent and summed in bfloat16 or wider, within the bound.
A program may use at most 128 MiB of HBM per device.

```python
import math
import jax
import jax.numpy as jnp
from jax import lax

D = 5120
HEADS = 32
HEAD_DIM = 128
BLOCK = 32
NB = 5
VIEWS = 16
CLIPS = 8
ROWS = 160
TOK = 2560
HD = 4096


def pair_draw(key):
    full_shape = (CLIPS, TOK, HD)
    key_a = jax.random.fold_in(key, 101)
    key_b = jax.random.fold_in(key, 102)
    query_draw = jnp.clip(jax.random.normal(key_a, full_shape, jnp.float32), -4.0, 4.0)
    key_draw = jnp.clip(jax.random.normal(key_b, full_shape, jnp.float32), -4.0, 4.0)
    return (query_draw, key_draw)


def draw_queries(key, part):
    return pair_draw(key)[0].astype(jnp.bfloat16)


def draw_keys(key, part):
    return pair_draw(key)[1].astype(jnp.bfloat16)


def draw_block_counts(key, part):
    pick = jax.random.randint(jax.random.fold_in(key, 201), (CLIPS, VIEWS), 0, 3) == 0
    extra = jax.random.randint(jax.random.fold_in(key, 202), (CLIPS, VIEWS), 0, NB)
    counts = jnp.where(pick, 1 + extra, 1)
    fullest = jax.random.randint(jax.random.fold_in(key, 203), (CLIPS,), 0, VIEWS)
    view_ids = jnp.arange(VIEWS, dtype=jnp.int32)[None, :]
    return jnp.where(view_ids == fullest[:, None], NB, counts).astype(jnp.int32)


def draw_row_mask(key, part):
    coins = jax.random.randint(jax.random.fold_in(key, 301), (CLIPS, TOK), 0, 5) > 0
    inside = jnp.arange(TOK, dtype=jnp.int32) % BLOCK < 2
    return jnp.where(inside[None, :], 1, coins.astype(jnp.int32)).astype(jnp.int32)


def shard_levels(own_key, dims, cuts, least, largest):
    loudness, own = 1.0, jax.random.fold_in(own_key, 6)
    for position, shards_of in cuts:
        heights = jnp.exp(jax.random.uniform(jax.random.fold_in(own, position), (shards_of,), jnp.float32, least / len(cuts), largest / len(cuts)))
        loudness = loudness * jnp.repeat(heights, dims[position] // shards_of).reshape([-1 if axis == position else 1 for axis in range(len(dims))])
    return loudness


def bell_draw(key, extent, deviation, most, split=(), kind=jnp.bfloat16):
    level = shard_levels(key, extent, split, -0.22, 0.18) if split else 1.0
    entries = jax.random.normal(key, extent, jnp.float32) * deviation * level
    return jnp.minimum(jnp.maximum(entries, -most), most).astype(kind)


def setup_inputs(seed: int = 0) -> dict:
    streams_of = jax.random.split(jax.random.key(seed), 7)
    queries = draw_queries(jax.random.fold_in(streams_of[6], 71), 0)
    keys = draw_keys(jax.random.fold_in(streams_of[6], 71), 0)
    values = bell_draw(streams_of[2], (CLIPS, TOK, HD), 1.0, 6.0, ((0, 8), (1, 16)))
    out_weight = bell_draw(streams_of[3], (HD, D), HD ** -0.5, 0.09375, ((0, 8),))
    block_counts = draw_block_counts(jax.random.fold_in(streams_of[6], 71), 0)
    row_mask = draw_row_mask(jax.random.fold_in(streams_of[6], 71), 0)
    return dict(queries=queries, keys=keys, values=values, out_weight=out_weight, block_counts=block_counts, row_mask=row_mask)


def reference(queries, keys, values, out_weight, block_counts, row_mask):
    score_scale = 1.0 / math.sqrt(HEAD_DIM)
    positions = jnp.arange(TOK, dtype=jnp.int32)
    which_view = positions // ROWS
    which_block = positions % ROWS // BLOCK
    row_valid = (row_mask == 1) & (which_block[None, :] < block_counts[:, which_view])

    def split_heads(tensor):
        return tensor.reshape(CLIPS, TOK, HEADS, HEAD_DIM).transpose(0, 2, 1, 3).reshape(CLIPS * HEADS, TOK, HEAD_DIM)
    head_masks = jnp.repeat(row_valid, HEADS, axis=0)

    def one_head(pieces):
        query_h, key_h, value_h, key_ok = pieces
        scores = jnp.dot(query_h, key_h.T, preferred_element_type=jnp.float32) * score_scale
        scores = jnp.where(key_ok[None, :], scores, jnp.float32(-1e+30))
        row_top = lax.optimization_barrier(jnp.max(scores, axis=1, keepdims=True))
        raised = jnp.exp(scores - row_top)
        weights = (raised / lax.optimization_barrier(jnp.sum(raised, axis=1, keepdims=True))).astype(jnp.bfloat16)
        return jnp.dot(weights, value_h, preferred_element_type=jnp.float32).astype(jnp.bfloat16)
    heads_out = lax.map(one_head, (split_heads(queries), split_heads(keys), split_heads(values), head_masks))
    attended = heads_out.reshape(CLIPS, HEADS, TOK, HEAD_DIM).transpose(0, 2, 1, 3).reshape(CLIPS * TOK, HD)
    projected = jnp.dot(attended, out_weight, preferred_element_type=jnp.float32).reshape(CLIPS, TOK, D)
    return jnp.where(row_valid[:, :, None], projected, jnp.float32(0.0)).astype(jnp.bfloat16)
```

```python
import math

import jax
import jax.numpy as jnp
from jax import lax
from jax.sharding import Mesh
from jax.sharding import PartitionSpec as P

HEAD_DIM = 128
BLOCK = 32

CAM = ("x", "y_hi", "core")
FSDP = ("z", "y_lo")
Y = ("y_hi", "y_lo")


def attend(query_rows, key_rows, value_rows, key_ok):
    score_scale = 1.0 / math.sqrt(HEAD_DIM)
    count_all = query_rows.shape[0]
    head_count = query_rows.shape[1] // HEAD_DIM
    block_rows = 512
    outputs = []
    for head_number in range(head_count):
        column = head_number * HEAD_DIM
        query_h = query_rows[:, column : column + HEAD_DIM].reshape(
            count_all // block_rows, block_rows, HEAD_DIM
        )
        key_h = key_rows[:, column : column + HEAD_DIM]
        value_h = value_rows[:, column : column + HEAD_DIM]

        def one_block(query_block):
            scores = (
                jnp.einsum("qd,kd->qk", query_block, key_h, preferred_element_type=jnp.float32)
                * score_scale
            )
            scores = jnp.where(key_ok[None, :], scores, jnp.float32(-1e30))
            row_top = jnp.max(scores, axis=1, keepdims=True)
            raised = jnp.exp(scores - row_top)
            weights = (raised / jnp.sum(raised, axis=1, keepdims=True)).astype(jnp.bfloat16)
            return jnp.dot(weights, value_h, preferred_element_type=jnp.float32).astype(
                jnp.bfloat16
            )

        outputs.append(lax.map(one_block, query_h).reshape(count_all, HEAD_DIM))
    return jnp.concatenate(outputs, axis=1)


def shift(x, axes, size, step):
    return lax.ppermute(x, axes, perm=[(i, (i + step) % size) for i in range(size)])


def gather_pieces(weight):
    rows, cols = weight.shape
    core = lax.axis_index("core")
    half_cols = cols // 2
    half_rows = rows // 2
    own = lax.dynamic_slice_in_dim(weight, core * half_cols, half_cols, axis=1)
    z_size = lax.axis_size("z")
    y_size = lax.axis_size("y_hi") * lax.axis_size("y_lo")
    from_below = shift(own, "z", z_size, 1)
    from_above = shift(own, "z", z_size, -1)
    far_top = shift(from_below[:half_rows], "z", z_size, 1)
    far_bottom = shift(from_above[half_rows:], "z", z_size, -1)
    pieces = [
        (from_below, -1, 0, 0),
        (from_above, 1, 0, 0),
        (far_top, 2, 0, 0),
        (far_bottom, 2, 0, half_rows),
    ]
    for held, dz in ((own, 0), (from_below, -1), (from_above, 1)):
        pieces.append((shift(held[:half_rows], Y, y_size, 1), dz, 1, 0))
        pieces.append((shift(held[half_rows:], Y, y_size, -1), dz, 1, half_rows))
    pieces.append((shift(far_top, Y, y_size, 1), 2, 1, 0))
    pieces.append((shift(far_bottom, Y, y_size, -1), 2, 1, half_rows))
    return pieces


def local(queries, keys, values, out_weight, block_counts, row_mask):
    query_rows = queries[0]
    row_count = query_rows.shape[0]
    cam_count = lax.axis_size(CAM)
    offsets = jnp.arange(row_count, dtype=jnp.int32)
    row_valid = (row_mask[0] == 1) & (offsets // BLOCK < block_counts[0, 0])
    key_flag = jnp.broadcast_to(row_valid.astype(jnp.bfloat16)[:, None], (row_count, cam_count))
    query_all, key_all, value_all, flag_all = (
        lax.all_to_all(query_rows, CAM, split_axis=1, concat_axis=0, tiled=True),
        lax.all_to_all(keys[0], CAM, split_axis=1, concat_axis=0, tiled=True),
        lax.all_to_all(values[0], CAM, split_axis=1, concat_axis=0, tiled=True),
        lax.all_to_all(key_flag, CAM, split_axis=1, concat_axis=0, tiled=True),
    )
    head_rows = attend(query_all, key_all, value_all, flag_all[:, 0] > 0.5)
    attended = lax.all_to_all(head_rows, CAM, split_axis=0, concat_axis=1, tiled=True)

    shard_rows = out_weight.shape[0]
    z = lax.axis_index("z")
    y_lo = lax.axis_index("y_lo")
    z_size = lax.axis_size("z")
    y_lo_size = lax.axis_size("y_lo")
    core = lax.axis_index("core")
    own_block = (z * y_lo_size + y_lo) * shard_rows
    total = jnp.dot(
        lax.dynamic_slice_in_dim(attended, own_block, shard_rows, axis=1),
        out_weight,
        preferred_element_type=jnp.float32,
    )
    mine = None
    theirs = None
    for piece, dz, flip, first_row in gather_pieces(out_weight):
        block = (((z + dz) % z_size) * y_lo_size + (y_lo + flip) % y_lo_size) * shard_rows
        lhs = lax.dynamic_slice_in_dim(attended, block + first_row, piece.shape[0], axis=1)
        partner = lax.ppermute(piece, "core", perm=[(0, 1), (1, 0)])
        part_mine = jnp.dot(lhs, piece, preferred_element_type=jnp.float32)
        part_theirs = jnp.dot(lhs, partner, preferred_element_type=jnp.float32)
        mine = part_mine if mine is None else mine + part_mine
        theirs = part_theirs if theirs is None else theirs + part_theirs
    split = jnp.where(core == 0, jnp.concatenate([mine, theirs], axis=1), jnp.concatenate([theirs, mine], axis=1))
    projected = total + split
    result = jnp.where(row_valid[:, None], projected, jnp.float32(0.0)).astype(jnp.bfloat16)
    return result[None]


def solution(mesh):
    sub_mesh = Mesh(mesh.devices.reshape(4, 2, 2, 4, 2), CAM + FSDP)
    in_specs = (
        P(FSDP, CAM, None),
        P(FSDP, CAM, None),
        P(FSDP, CAM, None),
        P(FSDP, None),
        P(FSDP, CAM),
        P(FSDP, CAM),
    )
    out_specs = P(FSDP, CAM, None)
    return jax.shard_map(local, mesh=sub_mesh, in_specs=in_specs, out_specs=out_specs, check_vma=False)
```

```python
import math

import jax
import jax.numpy as jnp
from jax import lax
from jax.experimental import pallas as pl
from jax.experimental.pallas import tpu as pltpu
from jax.sharding import Mesh
from jax.sharding import PartitionSpec as P

HEAD_DIM = 128
BLOCK = 32

CAM = ("x", "y_hi", "core")
FSDP = ("z", "y_lo")
Y = ("y_hi", "y_lo")


def attend(query_rows, key_rows, value_rows, key_ok):
    score_scale = 1.0 / math.sqrt(HEAD_DIM)
    count_all = query_rows.shape[0]
    head_count = query_rows.shape[1] // HEAD_DIM
    block_rows = 512
    outputs = []
    for head_number in range(head_count):
        column = head_number * HEAD_DIM
        query_h = query_rows[:, column : column + HEAD_DIM].reshape(
            count_all // block_rows, block_rows, HEAD_DIM
        )
        key_h = key_rows[:, column : column + HEAD_DIM]
        value_h = value_rows[:, column : column + HEAD_DIM]

        def one_block(query_block):
            scores = (
                jnp.einsum("qd,kd->qk", query_block, key_h, preferred_element_type=jnp.float32)
                * score_scale
            )
            scores = jnp.where(key_ok[None, :], scores, jnp.float32(-1e30))
            row_top = jnp.max(scores, axis=1, keepdims=True)
            raised = jnp.exp(scores - row_top)
            weights = (raised / jnp.sum(raised, axis=1, keepdims=True)).astype(jnp.bfloat16)
            return jnp.dot(weights, value_h, preferred_element_type=jnp.float32).astype(
                jnp.bfloat16
            )

        outputs.append(lax.map(one_block, query_h).reshape(count_all, HEAD_DIM))
    return jnp.concatenate(outputs, axis=1)


MESH_IDS = pl.DeviceIdType.MESH


def gather_kernel(w_ref, out_ref, send, recv):
    k = lax.axis_index("core")
    z = lax.axis_index("z")
    yl = lax.axis_index("y_lo")
    y = lax.axis_index("y_hi") * 2 + yl
    shard = w_ref.shape[0]
    half = shard // 2
    quarter = half // 2

    def zdev(dz):
        return {"z": (z + dz) % 4}

    def ydev(dy):
        yy = (y + dy) % 4
        return {"y_hi": yy // 2, "y_lo": yy % 2}

    partner = {"core": 1 - k}
    neighbours = (zdev(1), zdev(-1), ydev(1), ydev(-1), partner)

    def shard_of(dz, flip):
        return ((z + dz) % 4) * 2 + (yl + flip) % 2

    def region(f, kk, part):
        start = f * shard + kk * half + (quarter if part == "bot" else 0)
        size = half if part == "all" else quarter
        return out_ref.at[pl.ds(pl.multiple_of(start, quarter), size)]

    barrier = pltpu.get_barrier_semaphore()
    for dev in neighbours:
        pl.semaphore_signal(barrier, inc=1, device_id=dev, device_id_type=MESH_IDS)
    pl.semaphore_wait(barrier, len(neighbours))

    sent = []

    def send_piece(src, dst, t, dev):
        copy = pltpu.make_async_remote_copy(
            src_ref=src, dst_ref=dst, send_sem=send.at[t], recv_sem=recv.at[t],
            device_id=dev, device_id_type=MESH_IDS,
        )
        copy.start()
        sent.append(copy)

    def forward(dz, flip, part, t, dev):
        piece = region(shard_of(dz, flip), k, part)
        send_piece(piece, piece, t, dev)

    def arrive(ref, t, dev):
        pltpu.make_async_remote_copy(
            src_ref=ref, dst_ref=ref, send_sem=send.at[t], recv_sem=recv.at[t],
            device_id=dev, device_id_type=MESH_IDS,
        ).wait_recv()

    own = shard_of(0, 0)
    mine = w_ref.at[pl.ds(pl.multiple_of(k * half, quarter), half)]
    mine_top = w_ref.at[pl.ds(pl.multiple_of(k * half, quarter), quarter)]
    mine_bot = w_ref.at[pl.ds(pl.multiple_of(k * half + quarter, quarter), quarter)]
    send_piece(mine, region(own, k, "all"), 0, zdev(1))
    send_piece(mine, region(own, k, "all"), 1, zdev(-1))
    send_piece(mine_top, region(own, k, "top"), 2, ydev(1))
    send_piece(mine_bot, region(own, k, "bot"), 3, ydev(-1))

    arrive(region(shard_of(-1, 0), k, "all"), 0, zdev(-1))
    forward(-1, 0, "top", 4, zdev(1))
    forward(-1, 0, "top", 5, ydev(1))
    forward(-1, 0, "bot", 6, ydev(-1))
    forward(-1, 0, "all", 7, partner)
    arrive(region(shard_of(1, 0), k, "all"), 1, zdev(1))
    forward(1, 0, "bot", 8, zdev(-1))
    forward(1, 0, "top", 9, ydev(1))
    forward(1, 0, "bot", 10, ydev(-1))
    forward(1, 0, "all", 11, partner)
    arrive(region(shard_of(0, 1), k, "top"), 2, ydev(-1))
    forward(0, 1, "top", 12, partner)
    arrive(region(shard_of(0, 1), k, "bot"), 3, ydev(1))
    forward(0, 1, "bot", 13, partner)

    arrive(region(shard_of(2, 0), k, "top"), 4, zdev(-1))
    forward(2, 0, "top", 14, ydev(1))
    forward(2, 0, "top", 15, partner)
    arrive(region(shard_of(2, 0), k, "bot"), 8, zdev(1))
    forward(2, 0, "bot", 16, ydev(-1))
    forward(2, 0, "bot", 17, partner)
    arrive(region(shard_of(-1, 1), k, "top"), 5, ydev(-1))
    forward(-1, 1, "top", 18, partner)
    arrive(region(shard_of(-1, 1), k, "bot"), 6, ydev(1))
    forward(-1, 1, "bot", 19, partner)
    arrive(region(shard_of(1, 1), k, "top"), 9, ydev(-1))
    forward(1, 1, "top", 20, partner)
    arrive(region(shard_of(1, 1), k, "bot"), 10, ydev(1))
    forward(1, 1, "bot", 21, partner)

    arrive(region(shard_of(2, 1), k, "top"), 14, ydev(-1))
    forward(2, 1, "top", 22, partner)
    arrive(region(shard_of(2, 1), k, "bot"), 16, ydev(1))
    forward(2, 1, "bot", 23, partner)

    other = 1 - k
    for dz, flip, part, t in (
        (-1, 0, "all", 7), (1, 0, "all", 11), (0, 1, "top", 12), (0, 1, "bot", 13),
        (2, 0, "top", 15), (2, 0, "bot", 17), (-1, 1, "top", 18), (-1, 1, "bot", 19),
        (1, 1, "top", 20), (1, 1, "bot", 21), (2, 1, "top", 22), (2, 1, "bot", 23),
    ):
        arrive(region(shard_of(dz, flip), other, part), t, partner)
    for copy in sent:
        copy.wait_send()


def gather_weight(out_weight):
    rows, cols = out_weight.shape
    fsdp = lax.axis_size("z") * lax.axis_size("y_lo")
    gathered = pl.pallas_call(
        gather_kernel,
        out_shape=jax.ShapeDtypeStruct((rows * fsdp, cols), out_weight.dtype),
        in_specs=[pl.BlockSpec(memory_space=pl.ANY)],
        out_specs=pl.BlockSpec(memory_space=pl.ANY),
        scratch_shapes=[pltpu.SemaphoreType.DMA((24,)), pltpu.SemaphoreType.DMA((24,))],
        compiler_params=pltpu.CompilerParams(collective_id=0, has_side_effects=True),
    )(out_weight)
    own = lax.axis_index("z") * lax.axis_size("y_lo") + lax.axis_index("y_lo")
    return lax.dynamic_update_slice_in_dim(gathered, out_weight, own * rows, axis=0)


def local(queries, keys, values, out_weight, block_counts, row_mask):
    query_rows = queries[0]
    row_count = query_rows.shape[0]
    cam_count = lax.axis_size(CAM)
    offsets = jnp.arange(row_count, dtype=jnp.int32)
    row_valid = (row_mask[0] == 1) & (offsets // BLOCK < block_counts[0, 0])
    key_flag = jnp.broadcast_to(row_valid.astype(jnp.bfloat16)[:, None], (row_count, cam_count))
    query_all, key_all, value_all, flag_all = (
        lax.all_to_all(query_rows, CAM, split_axis=1, concat_axis=0, tiled=True),
        lax.all_to_all(keys[0], CAM, split_axis=1, concat_axis=0, tiled=True),
        lax.all_to_all(values[0], CAM, split_axis=1, concat_axis=0, tiled=True),
        lax.all_to_all(key_flag, CAM, split_axis=1, concat_axis=0, tiled=True),
    )
    head_rows = attend(query_all, key_all, value_all, flag_all[:, 0] > 0.5)
    attended = lax.all_to_all(head_rows, CAM, split_axis=0, concat_axis=1, tiled=True)

    projected = jnp.dot(attended, gather_weight(out_weight), preferred_element_type=jnp.float32)
    result = jnp.where(row_valid[:, None], projected, jnp.float32(0.0)).astype(jnp.bfloat16)
    return result[None]


def solution(mesh):
    sub_mesh = Mesh(mesh.devices.reshape(4, 2, 2, 4, 2), CAM + FSDP)
    in_specs = (
        P(FSDP, CAM, None),
        P(FSDP, CAM, None),
        P(FSDP, CAM, None),
        P(FSDP, None),
        P(FSDP, CAM),
        P(FSDP, CAM),
    )
    out_specs = P(FSDP, CAM, None)
    return jax.shard_map(local, mesh=sub_mesh, in_specs=in_specs, out_specs=out_specs, check_vma=False)
```

```python
import math

import jax
import jax.numpy as jnp
from jax import lax
from jax.experimental import pallas as pl
from jax.experimental.pallas import tpu as pltpu
from jax.sharding import Mesh
from jax.sharding import PartitionSpec as P

HEAD_DIM = 128
BLOCK = 32

CAM = ("x", "y_hi", "core")
FSDP = ("z", "y_lo")
Y = ("y_hi", "y_lo")


def attend(query_rows, key_rows, value_rows, key_ok):
    score_scale = 1.0 / math.sqrt(HEAD_DIM)
    count_all = query_rows.shape[0]
    head_count = query_rows.shape[1] // HEAD_DIM
    block_rows = 512
    outputs = []
    for head_number in range(head_count):
        column = head_number * HEAD_DIM
        query_h = query_rows[:, column : column + HEAD_DIM].reshape(
            count_all // block_rows, block_rows, HEAD_DIM
        )
        key_h = key_rows[:, column : column + HEAD_DIM]
        value_h = value_rows[:, column : column + HEAD_DIM]

        def one_block(query_block):
            scores = (
                jnp.einsum("qd,kd->qk", query_block, key_h, preferred_element_type=jnp.float32)
                * score_scale
            )
            scores = jnp.where(key_ok[None, :], scores, jnp.float32(-1e30))
            row_top = jnp.max(scores, axis=1, keepdims=True)
            raised = jnp.exp(scores - row_top)
            weights = (raised / jnp.sum(raised, axis=1, keepdims=True)).astype(jnp.bfloat16)
            return jnp.dot(weights, value_h, preferred_element_type=jnp.float32).astype(
                jnp.bfloat16
            )

        outputs.append(lax.map(one_block, query_h).reshape(count_all, HEAD_DIM))
    return jnp.concatenate(outputs, axis=1)


MESH_IDS = pl.DeviceIdType.MESH


def gather_kernel(w_ref, out_ref, send, recv):
    k = lax.axis_index("core")
    z = lax.axis_index("z")
    yl = lax.axis_index("y_lo")
    y = lax.axis_index("y_hi") * 2 + yl
    shard = w_ref.shape[0]
    half = shard // 2
    quarter = half // 2

    def zdev(dz):
        return {"z": (z + dz) % 4}

    def ydev(dy):
        yy = (y + dy) % 4
        return {"y_hi": yy // 2, "y_lo": yy % 2}

    partner = {"core": 1 - k}
    neighbours = (zdev(1), zdev(-1), ydev(1), ydev(-1), partner)

    def shard_of(dz, flip):
        return ((z + dz) % 4) * 2 + (yl + flip) % 2

    def region(f, kk, part):
        start = f * shard + kk * half + (quarter if part == "bot" else 0)
        size = half if part == "all" else quarter
        return out_ref.at[pl.ds(pl.multiple_of(start, quarter), size)]

    barrier = pltpu.get_barrier_semaphore()
    for dev in neighbours:
        pl.semaphore_signal(barrier, inc=1, device_id=dev, device_id_type=MESH_IDS)
    pl.semaphore_wait(barrier, len(neighbours))

    sent = []

    def send_piece(src, dst, t, dev):
        copy = pltpu.make_async_remote_copy(
            src_ref=src, dst_ref=dst, send_sem=send.at[t], recv_sem=recv.at[t],
            device_id=dev, device_id_type=MESH_IDS,
        )
        copy.start()
        sent.append(copy)

    def forward(dz, flip, part, t, dev):
        piece = region(shard_of(dz, flip), k, part)
        send_piece(piece, piece, t, dev)

    def arrive(ref, t, dev):
        pltpu.make_async_remote_copy(
            src_ref=ref, dst_ref=ref, send_sem=send.at[t], recv_sem=recv.at[t],
            device_id=dev, device_id_type=MESH_IDS,
        ).wait_recv()

    own = shard_of(0, 0)
    mine = w_ref.at[pl.ds(pl.multiple_of(k * half, quarter), half)]
    mine_top = w_ref.at[pl.ds(pl.multiple_of(k * half, quarter), quarter)]
    mine_bot = w_ref.at[pl.ds(pl.multiple_of(k * half + quarter, quarter), quarter)]
    send_piece(mine, region(own, k, "all"), 0, zdev(1))
    send_piece(mine, region(own, k, "all"), 1, zdev(-1))
    send_piece(mine_top, region(own, k, "top"), 2, ydev(1))
    send_piece(mine_bot, region(own, k, "bot"), 3, ydev(-1))

    arrive(region(shard_of(-1, 0), k, "all"), 0, zdev(-1))
    forward(-1, 0, "top", 4, zdev(1))
    forward(-1, 0, "top", 5, ydev(1))
    forward(-1, 0, "bot", 6, ydev(-1))
    forward(-1, 0, "all", 7, partner)
    arrive(region(shard_of(1, 0), k, "all"), 1, zdev(1))
    forward(1, 0, "bot", 8, zdev(-1))
    forward(1, 0, "top", 9, ydev(1))
    forward(1, 0, "bot", 10, ydev(-1))
    forward(1, 0, "all", 11, partner)
    arrive(region(shard_of(0, 1), k, "top"), 2, ydev(-1))
    forward(0, 1, "top", 12, partner)
    arrive(region(shard_of(0, 1), k, "bot"), 3, ydev(1))
    forward(0, 1, "bot", 13, partner)

    arrive(region(shard_of(2, 0), k, "top"), 4, zdev(-1))
    forward(2, 0, "top", 14, ydev(1))
    forward(2, 0, "top", 15, partner)
    arrive(region(shard_of(2, 0), k, "bot"), 8, zdev(1))
    forward(2, 0, "bot", 16, ydev(-1))
    forward(2, 0, "bot", 17, partner)
    arrive(region(shard_of(-1, 1), k, "top"), 5, ydev(-1))
    forward(-1, 1, "top", 18, partner)
    arrive(region(shard_of(-1, 1), k, "bot"), 6, ydev(1))
    forward(-1, 1, "bot", 19, partner)
    arrive(region(shard_of(1, 1), k, "top"), 9, ydev(-1))
    forward(1, 1, "top", 20, partner)
    arrive(region(shard_of(1, 1), k, "bot"), 10, ydev(1))
    forward(1, 1, "bot", 21, partner)

    arrive(region(shard_of(2, 1), k, "top"), 14, ydev(-1))
    forward(2, 1, "top", 22, partner)
    arrive(region(shard_of(2, 1), k, "bot"), 16, ydev(1))
    forward(2, 1, "bot", 23, partner)

    other = 1 - k
    for dz, flip, part, t in (
        (-1, 0, "all", 7), (1, 0, "all", 11), (0, 1, "top", 12), (0, 1, "bot", 13),
        (2, 0, "top", 15), (2, 0, "bot", 17), (-1, 1, "top", 18), (-1, 1, "bot", 19),
        (1, 1, "top", 20), (1, 1, "bot", 21), (2, 1, "top", 22), (2, 1, "bot", 23),
    ):
        arrive(region(shard_of(dz, flip), other, part), t, partner)
    for copy in sent:
        copy.wait_send()


def gather_weight(out_weight):
    rows, cols = out_weight.shape
    fsdp = lax.axis_size("z") * lax.axis_size("y_lo")
    gathered = pl.pallas_call(
        gather_kernel,
        out_shape=jax.ShapeDtypeStruct((rows * fsdp, cols), out_weight.dtype),
        in_specs=[pl.BlockSpec(memory_space=pl.ANY)],
        out_specs=pl.BlockSpec(memory_space=pl.ANY),
        scratch_shapes=[pltpu.SemaphoreType.DMA((24,)), pltpu.SemaphoreType.DMA((24,))],
        compiler_params=pltpu.CompilerParams(collective_id=0, has_side_effects=True),
    )(out_weight)
    own = lax.axis_index("z") * lax.axis_size("y_lo") + lax.axis_index("y_lo")
    return lax.dynamic_update_slice_in_dim(gathered, out_weight, own * rows, axis=0)


def local(queries, keys, values, out_weight, block_counts, row_mask):
    query_rows = queries[0]
    row_count = query_rows.shape[0]
    cam_count = lax.axis_size(CAM)
    offsets = jnp.arange(row_count, dtype=jnp.int32)
    row_valid = (row_mask[0] == 1) & (offsets // BLOCK < block_counts[0, 0])
    width = query_rows.shape[1] // cam_count
    flag = jnp.broadcast_to(
        row_valid.astype(jnp.bfloat16)[:, None, None], (row_count, cam_count, 128)
    )
    packed = jnp.concatenate(
        [
            query_rows.reshape(row_count, cam_count, width),
            keys[0].reshape(row_count, cam_count, width),
            values[0].reshape(row_count, cam_count, width),
            flag,
        ],
        axis=2,
    )
    packed_all = lax.all_to_all(packed, CAM, split_axis=1, concat_axis=0, tiled=True)[:, 0]
    query_all = packed_all[:, :width]
    key_all = packed_all[:, width : 2 * width]
    value_all = packed_all[:, 2 * width : 3 * width]
    flag_all = packed_all[:, 3 * width :]
    weight_all = gather_weight(out_weight)
    query_all, key_all, value_all, flag_all, weight_all = lax.optimization_barrier(
        (query_all, key_all, value_all, flag_all, weight_all)
    )
    head_rows = attend(query_all, key_all, value_all, flag_all[:, 0] > 0.5)
    attended = lax.all_to_all(head_rows, CAM, split_axis=0, concat_axis=1, tiled=True)

    projected = jnp.dot(attended, weight_all, preferred_element_type=jnp.float32)
    result = jnp.where(row_valid[:, None], projected, jnp.float32(0.0)).astype(jnp.bfloat16)
    return result[None]


def solution(mesh):
    sub_mesh = Mesh(mesh.devices.reshape(4, 2, 2, 4, 2), CAM + FSDP)
    in_specs = (
        P(FSDP, CAM, None),
        P(FSDP, CAM, None),
        P(FSDP, CAM, None),
        P(FSDP, None),
        P(FSDP, CAM),
        P(FSDP, CAM),
    )
    out_specs = P(FSDP, CAM, None)
    return jax.shard_map(local, mesh=sub_mesh, in_specs=in_specs, out_specs=out_specs, check_vma=False)
```

```python
import math

import jax
import jax.numpy as jnp
from jax import lax
from jax.experimental import pallas as pl
from jax.experimental.pallas import tpu as pltpu
from jax.sharding import Mesh
from jax.sharding import PartitionSpec as P

HEAD_DIM = 128
BLOCK = 32

CAM = ("x", "y_hi", "core")
FSDP = ("z", "y_lo")
Y = ("y_hi", "y_lo")


def attend(query_rows, key_rows, value_rows, key_ok):
    score_scale = 1.0 / math.sqrt(HEAD_DIM)
    count_all = query_rows.shape[0]
    head_count = query_rows.shape[1] // HEAD_DIM
    block_rows = 512
    outputs = []
    for head_number in range(head_count):
        column = head_number * HEAD_DIM
        query_h = query_rows[:, column : column + HEAD_DIM].reshape(
            count_all // block_rows, block_rows, HEAD_DIM
        )
        key_h = key_rows[:, column : column + HEAD_DIM]
        value_h = value_rows[:, column : column + HEAD_DIM]

        def one_block(query_block):
            scores = (
                jnp.einsum("qd,kd->qk", query_block, key_h, preferred_element_type=jnp.float32)
                * score_scale
            )
            scores = jnp.where(key_ok[None, :], scores, jnp.float32(-1e30))
            row_top = jnp.max(scores, axis=1, keepdims=True)
            raised = jnp.exp(scores - row_top)
            weights = (raised / jnp.sum(raised, axis=1, keepdims=True)).astype(jnp.bfloat16)
            return jnp.dot(weights, value_h, preferred_element_type=jnp.float32).astype(
                jnp.bfloat16
            )

        outputs.append(lax.map(one_block, query_h).reshape(count_all, HEAD_DIM))
    return jnp.concatenate(outputs, axis=1)


MESH_IDS = pl.DeviceIdType.MESH


def gather_kernel(w_ref, out_ref, send, recv, local_sem):
    k = lax.axis_index("core")
    z = lax.axis_index("z")
    yl = lax.axis_index("y_lo")
    y = lax.axis_index("y_hi") * 2 + yl
    shard = w_ref.shape[0]
    half = shard // 2
    quarter = half // 2

    def zdev(dz):
        return {"z": (z + dz) % 4}

    def ydev(dy):
        yy = (y + dy) % 4
        return {"y_hi": yy // 2, "y_lo": yy % 2}

    partner = {"core": 1 - k}
    neighbours = (zdev(1), zdev(-1), ydev(1), ydev(-1), partner)

    def shard_of(dz, flip):
        return ((z + dz) % 4) * 2 + (yl + flip) % 2

    parts = {"all": (0, half), "top": (0, quarter), "bot": (quarter, quarter)}
    for e in range(4):
        parts["e%d" % e] = (e * quarter // 2, quarter // 2)

    def region(f, kk, part):
        offset, size = parts[part]
        start = f * shard + kk * half + offset
        return out_ref.at[pl.ds(pl.multiple_of(start, quarter // 2), size)]

    barrier = pltpu.get_barrier_semaphore()
    for dev in neighbours:
        pl.semaphore_signal(barrier, inc=1, device_id=dev, device_id_type=MESH_IDS)
    pl.semaphore_wait(barrier, len(neighbours))

    sent = []

    def send_piece(src, dst, t, dev):
        copy = pltpu.make_async_remote_copy(
            src_ref=src, dst_ref=dst, send_sem=send.at[t], recv_sem=recv.at[t],
            device_id=dev, device_id_type=MESH_IDS,
        )
        copy.start()
        sent.append(copy)

    def forward(dz, flip, part, t, dev):
        piece = region(shard_of(dz, flip), k, part)
        send_piece(piece, piece, t, dev)

    def arrive(ref, t, dev):
        pltpu.make_async_remote_copy(
            src_ref=ref, dst_ref=ref, send_sem=send.at[t], recv_sem=recv.at[t],
            device_id=dev, device_id_type=MESH_IDS,
        ).wait_recv()

    own = shard_of(0, 0)
    local_copy = pltpu.make_async_copy(
        w_ref, out_ref.at[pl.ds(pl.multiple_of(own * shard, shard), shard)], local_sem
    )
    local_copy.start()
    mine = w_ref.at[pl.ds(pl.multiple_of(k * half, quarter), half)]
    mine_top = w_ref.at[pl.ds(pl.multiple_of(k * half, quarter), quarter)]
    mine_bot = w_ref.at[pl.ds(pl.multiple_of(k * half + quarter, quarter), quarter)]
    send_piece(mine, region(own, k, "all"), 0, zdev(1))
    send_piece(mine, region(own, k, "all"), 1, zdev(-1))
    send_piece(mine_top, region(own, k, "top"), 2, ydev(1))
    send_piece(mine_bot, region(own, k, "bot"), 3, ydev(-1))

    arrive(region(shard_of(-1, 0), k, "all"), 0, zdev(-1))
    forward(-1, 0, "top", 4, zdev(1))
    forward(-1, 0, "top", 5, ydev(1))
    forward(-1, 0, "bot", 6, ydev(-1))
    forward(-1, 0, "all", 7, partner)
    arrive(region(shard_of(1, 0), k, "all"), 1, zdev(1))
    forward(1, 0, "bot", 8, zdev(-1))
    forward(1, 0, "top", 9, ydev(1))
    forward(1, 0, "bot", 10, ydev(-1))
    forward(1, 0, "all", 11, partner)
    arrive(region(shard_of(0, 1), k, "top"), 2, ydev(-1))
    forward(0, 1, "top", 12, partner)
    arrive(region(shard_of(0, 1), k, "bot"), 3, ydev(1))
    forward(0, 1, "bot", 13, partner)

    arrive(region(shard_of(2, 0), k, "top"), 4, zdev(-1))
    forward(2, 0, "e0", 14, ydev(1))
    forward(2, 0, "top", 15, partner)
    arrive(region(shard_of(2, 0), k, "bot"), 8, zdev(1))
    forward(2, 0, "e3", 16, ydev(-1))
    forward(2, 0, "bot", 17, partner)
    arrive(region(shard_of(-1, 1), k, "top"), 5, ydev(-1))
    forward(-1, 1, "e1", 24, zdev(1))
    forward(-1, 1, "top", 18, partner)
    arrive(region(shard_of(-1, 1), k, "bot"), 6, ydev(1))
    forward(-1, 1, "bot", 19, partner)
    arrive(region(shard_of(1, 1), k, "top"), 9, ydev(-1))
    forward(1, 1, "top", 20, partner)
    arrive(region(shard_of(1, 1), k, "bot"), 10, ydev(1))
    forward(1, 1, "e2", 25, zdev(-1))
    forward(1, 1, "bot", 21, partner)

    arrive(region(shard_of(2, 1), k, "e0"), 14, ydev(-1))
    arrive(region(shard_of(2, 1), k, "e1"), 24, zdev(-1))
    forward(2, 1, "top", 22, partner)
    arrive(region(shard_of(2, 1), k, "e3"), 16, ydev(1))
    arrive(region(shard_of(2, 1), k, "e2"), 25, zdev(1))
    forward(2, 1, "bot", 23, partner)

    other = 1 - k
    for dz, flip, part, t in (
        (-1, 0, "all", 7), (1, 0, "all", 11), (0, 1, "top", 12), (0, 1, "bot", 13),
        (2, 0, "top", 15), (2, 0, "bot", 17), (-1, 1, "top", 18), (-1, 1, "bot", 19),
        (1, 1, "top", 20), (1, 1, "bot", 21), (2, 1, "top", 22), (2, 1, "bot", 23),
    ):
        arrive(region(shard_of(dz, flip), other, part), t, partner)
    for copy in sent:
        copy.wait_send()
    local_copy.wait()


def gather_weight(out_weight):
    rows, cols = out_weight.shape
    fsdp = lax.axis_size("z") * lax.axis_size("y_lo")
    gathered = pl.pallas_call(
        gather_kernel,
        out_shape=jax.ShapeDtypeStruct((rows * fsdp, cols), out_weight.dtype),
        in_specs=[pl.BlockSpec(memory_space=pl.ANY)],
        out_specs=pl.BlockSpec(memory_space=pl.ANY),
        scratch_shapes=[
            pltpu.SemaphoreType.DMA((26,)),
            pltpu.SemaphoreType.DMA((26,)),
            pltpu.SemaphoreType.DMA(()),
        ],
        compiler_params=pltpu.CompilerParams(collective_id=0, has_side_effects=True),
    )(out_weight)
    return gathered


def local(queries, keys, values, out_weight, block_counts, row_mask):
    query_rows = queries[0]
    row_count = query_rows.shape[0]
    cam_count = lax.axis_size(CAM)
    offsets = jnp.arange(row_count, dtype=jnp.int32)
    row_valid = (row_mask[0] == 1) & (offsets // BLOCK < block_counts[0, 0])
    width = query_rows.shape[1] // cam_count
    flag = jnp.broadcast_to(
        row_valid.astype(jnp.bfloat16)[:, None, None], (row_count, cam_count, 128)
    )
    packed = jnp.concatenate(
        [
            query_rows.reshape(row_count, cam_count, width),
            keys[0].reshape(row_count, cam_count, width),
            values[0].reshape(row_count, cam_count, width),
            flag,
        ],
        axis=2,
    )
    packed_all = lax.all_to_all(packed, CAM, split_axis=1, concat_axis=0, tiled=True)[:, 0]
    query_all = packed_all[:, :width]
    key_all = packed_all[:, width : 2 * width]
    value_all = packed_all[:, 2 * width : 3 * width]
    flag_all = packed_all[:, 3 * width :]
    weight_all = gather_weight(out_weight)
    query_all, key_all, value_all, flag_all, weight_all = lax.optimization_barrier(
        (query_all, key_all, value_all, flag_all, weight_all)
    )
    head_rows = attend(query_all, key_all, value_all, flag_all[:, 0] > 0.5)
    attended = lax.all_to_all(head_rows, CAM, split_axis=0, concat_axis=1, tiled=True)

    projected = jnp.dot(attended, weight_all, preferred_element_type=jnp.float32)
    result = jnp.where(row_valid[:, None], projected, jnp.float32(0.0)).astype(jnp.bfloat16)
    return result[None]


def solution(mesh):
    sub_mesh = Mesh(mesh.devices.reshape(4, 2, 2, 4, 2), CAM + FSDP)
    in_specs = (
        P(FSDP, CAM, None),
        P(FSDP, CAM, None),
        P(FSDP, CAM, None),
        P(FSDP, None),
        P(FSDP, CAM),
        P(FSDP, CAM),
    )
    out_specs = P(FSDP, CAM, None)
    return jax.shard_map(local, mesh=sub_mesh, in_specs=in_specs, out_specs=out_specs, check_vma=False)
```

```python
import functools
import math

import jax
import jax.numpy as jnp
from jax import lax
from jax.experimental import pallas as pl
from jax.experimental.pallas import tpu as pltpu
from jax.sharding import Mesh
from jax.sharding import PartitionSpec as P

HEAD_DIM = 128
BLOCK = 32

CAM = ("x", "y_hi", "core")
FSDP = ("z", "y_lo")
Y = ("y_hi", "y_lo")


def attend(query_rows, key_rows, value_rows, key_ok):
    score_scale = 1.0 / math.sqrt(HEAD_DIM)
    count_all = query_rows.shape[0]
    head_count = query_rows.shape[1] // HEAD_DIM
    block_rows = 512
    outputs = []
    for head_number in range(head_count):
        column = head_number * HEAD_DIM
        query_h = query_rows[:, column : column + HEAD_DIM].reshape(
            count_all // block_rows, block_rows, HEAD_DIM
        )
        key_h = key_rows[:, column : column + HEAD_DIM]
        value_h = value_rows[:, column : column + HEAD_DIM]

        def one_block(query_block):
            scores = (
                jnp.einsum("qd,kd->qk", query_block, key_h, preferred_element_type=jnp.float32)
                * score_scale
            )
            scores = jnp.where(key_ok[None, :], scores, jnp.float32(-1e30))
            row_top = jnp.max(scores, axis=1, keepdims=True)
            raised = jnp.exp(scores - row_top)
            weights = (raised / jnp.sum(raised, axis=1, keepdims=True)).astype(jnp.bfloat16)
            return jnp.dot(weights, value_h, preferred_element_type=jnp.float32).astype(
                jnp.bfloat16
            )

        outputs.append(lax.map(one_block, query_h).reshape(count_all, HEAD_DIM))
    return jnp.concatenate(outputs, axis=1)


MESH_IDS = pl.DeviceIdType.MESH


def gather_kernel(col0, w_ref, out_ref, send, recv, local_sem):
    k = lax.axis_index("core")
    z = lax.axis_index("z")
    yl = lax.axis_index("y_lo")
    y = lax.axis_index("y_hi") * 2 + yl
    shard = w_ref.shape[0]
    half = shard // 2
    quarter = half // 2

    def zdev(dz):
        return {"z": (z + dz) % 4}

    def ydev(dy):
        yy = (y + dy) % 4
        return {"y_hi": yy // 2, "y_lo": yy % 2}

    partner = {"core": 1 - k}
    neighbours = (zdev(1), zdev(-1), ydev(1), ydev(-1), partner)

    def shard_of(dz, flip):
        return ((z + dz) % 4) * 2 + (yl + flip) % 2

    parts = {"all": (0, half), "top": (0, quarter), "bot": (quarter, quarter)}
    for e in range(4):
        parts["e%d" % e] = (e * quarter // 2, quarter // 2)

    def region(f, kk, part):
        offset, size = parts[part]
        start = f * shard + kk * half + offset
        return out_ref.at[pl.ds(pl.multiple_of(start, quarter // 2), size)]

    barrier = pltpu.get_barrier_semaphore()
    for dev in neighbours:
        pl.semaphore_signal(barrier, inc=1, device_id=dev, device_id_type=MESH_IDS)
    pl.semaphore_wait(barrier, len(neighbours))

    sent = []

    def send_piece(src, dst, t, dev):
        copy = pltpu.make_async_remote_copy(
            src_ref=src, dst_ref=dst, send_sem=send.at[t], recv_sem=recv.at[t],
            device_id=dev, device_id_type=MESH_IDS,
        )
        copy.start()
        sent.append(copy)

    def forward(dz, flip, part, t, dev):
        piece = region(shard_of(dz, flip), k, part)
        send_piece(piece, piece, t, dev)

    def arrive(ref, t, dev):
        pltpu.make_async_remote_copy(
            src_ref=ref, dst_ref=ref, send_sem=send.at[t], recv_sem=recv.at[t],
            device_id=dev, device_id_type=MESH_IDS,
        ).wait_recv()

    own = shard_of(0, 0)
    ncols = out_ref.shape[1]
    cols = pl.ds(col0, ncols)
    local_copy = pltpu.make_async_copy(
        w_ref.at[:, cols], out_ref.at[pl.ds(pl.multiple_of(own * shard, shard), shard)], local_sem
    )
    local_copy.start()
    mine = w_ref.at[pl.ds(pl.multiple_of(k * half, quarter), half), cols]
    mine_top = w_ref.at[pl.ds(pl.multiple_of(k * half, quarter), quarter), cols]
    mine_bot = w_ref.at[pl.ds(pl.multiple_of(k * half + quarter, quarter), quarter), cols]
    send_piece(mine, region(own, k, "all"), 0, zdev(1))
    send_piece(mine, region(own, k, "all"), 1, zdev(-1))
    send_piece(mine_top, region(own, k, "top"), 2, ydev(1))
    send_piece(mine_bot, region(own, k, "bot"), 3, ydev(-1))

    arrive(region(shard_of(-1, 0), k, "all"), 0, zdev(-1))
    forward(-1, 0, "top", 4, zdev(1))
    forward(-1, 0, "top", 5, ydev(1))
    forward(-1, 0, "bot", 6, ydev(-1))
    forward(-1, 0, "all", 7, partner)
    arrive(region(shard_of(1, 0), k, "all"), 1, zdev(1))
    forward(1, 0, "bot", 8, zdev(-1))
    forward(1, 0, "top", 9, ydev(1))
    forward(1, 0, "bot", 10, ydev(-1))
    forward(1, 0, "all", 11, partner)
    arrive(region(shard_of(0, 1), k, "top"), 2, ydev(-1))
    forward(0, 1, "top", 12, partner)
    arrive(region(shard_of(0, 1), k, "bot"), 3, ydev(1))
    forward(0, 1, "bot", 13, partner)

    arrive(region(shard_of(2, 0), k, "top"), 4, zdev(-1))
    forward(2, 0, "e0", 14, ydev(1))
    forward(2, 0, "top", 15, partner)
    arrive(region(shard_of(2, 0), k, "bot"), 8, zdev(1))
    forward(2, 0, "e3", 16, ydev(-1))
    forward(2, 0, "bot", 17, partner)
    arrive(region(shard_of(-1, 1), k, "top"), 5, ydev(-1))
    forward(-1, 1, "e1", 24, zdev(1))
    forward(-1, 1, "top", 18, partner)
    arrive(region(shard_of(-1, 1), k, "bot"), 6, ydev(1))
    forward(-1, 1, "bot", 19, partner)
    arrive(region(shard_of(1, 1), k, "top"), 9, ydev(-1))
    forward(1, 1, "top", 20, partner)
    arrive(region(shard_of(1, 1), k, "bot"), 10, ydev(1))
    forward(1, 1, "e2", 25, zdev(-1))
    forward(1, 1, "bot", 21, partner)

    arrive(region(shard_of(2, 1), k, "e0"), 14, ydev(-1))
    arrive(region(shard_of(2, 1), k, "e1"), 24, zdev(-1))
    forward(2, 1, "top", 22, partner)
    arrive(region(shard_of(2, 1), k, "e3"), 16, ydev(1))
    arrive(region(shard_of(2, 1), k, "e2"), 25, zdev(1))
    forward(2, 1, "bot", 23, partner)

    other = 1 - k
    for dz, flip, part, t in (
        (-1, 0, "all", 7), (1, 0, "all", 11), (0, 1, "top", 12), (0, 1, "bot", 13),
        (2, 0, "top", 15), (2, 0, "bot", 17), (-1, 1, "top", 18), (-1, 1, "bot", 19),
        (1, 1, "top", 20), (1, 1, "bot", 21), (2, 1, "top", 22), (2, 1, "bot", 23),
    ):
        arrive(region(shard_of(dz, flip), other, part), t, partner)
    for copy in sent:
        copy.wait_send()
    local_copy.wait()


def gather_weight(out_weight, col0, ncols, call_id):
    rows = out_weight.shape[0]
    fsdp = lax.axis_size("z") * lax.axis_size("y_lo")
    return pl.pallas_call(
        functools.partial(gather_kernel, col0),
        out_shape=jax.ShapeDtypeStruct((rows * fsdp, ncols), out_weight.dtype),
        in_specs=[pl.BlockSpec(memory_space=pl.ANY)],
        out_specs=pl.BlockSpec(memory_space=pl.ANY),
        scratch_shapes=[
            pltpu.SemaphoreType.DMA((26,)),
            pltpu.SemaphoreType.DMA((26,)),
            pltpu.SemaphoreType.DMA(()),
        ],
        compiler_params=pltpu.CompilerParams(collective_id=call_id, has_side_effects=True),
    )(out_weight)


def local(queries, keys, values, out_weight, block_counts, row_mask):
    query_rows = queries[0]
    row_count = query_rows.shape[0]
    cam_count = lax.axis_size(CAM)
    offsets = jnp.arange(row_count, dtype=jnp.int32)
    row_valid = (row_mask[0] == 1) & (offsets // BLOCK < block_counts[0, 0])
    width = query_rows.shape[1] // cam_count
    flag = jnp.broadcast_to(
        row_valid.astype(jnp.bfloat16)[:, None, None], (row_count, cam_count, 128)
    )
    packed = jnp.concatenate(
        [
            query_rows.reshape(row_count, cam_count, width),
            keys[0].reshape(row_count, cam_count, width),
            values[0].reshape(row_count, cam_count, width),
            flag,
        ],
        axis=2,
    )
    packed_all = lax.all_to_all(packed, CAM, split_axis=1, concat_axis=0, tiled=True)[:, 0]
    query_all = packed_all[:, :width]
    key_all = packed_all[:, width : 2 * width]
    value_all = packed_all[:, 2 * width : 3 * width]
    flag_all = packed_all[:, 3 * width :]
    split = out_weight.shape[1] // 2
    weight_left = gather_weight(out_weight, 0, split, 0)
    query_all, key_all, value_all, flag_all, weight_left = lax.optimization_barrier(
        (query_all, key_all, value_all, flag_all, weight_left)
    )
    head_rows = attend(query_all, key_all, value_all, flag_all[:, 0] > 0.5)
    head_rows, weight_late = lax.optimization_barrier((head_rows, out_weight))
    attended = lax.all_to_all(head_rows, CAM, split_axis=0, concat_axis=1, tiled=True)
    weight_right = gather_weight(weight_late, split, out_weight.shape[1] - split, 1)
    attended, weight_right = lax.optimization_barrier((attended, weight_right))
    projected = jnp.concatenate(
        [
            jnp.dot(attended, weight_left, preferred_element_type=jnp.float32),
            jnp.dot(attended, weight_right, preferred_element_type=jnp.float32),
        ],
        axis=1,
    )
    result = jnp.where(row_valid[:, None], projected, jnp.float32(0.0)).astype(jnp.bfloat16)
    return result[None]


def solution(mesh):
    sub_mesh = Mesh(mesh.devices.reshape(4, 2, 2, 4, 2), CAM + FSDP)
    in_specs = (
        P(FSDP, CAM, None),
        P(FSDP, CAM, None),
        P(FSDP, CAM, None),
        P(FSDP, None),
        P(FSDP, CAM),
        P(FSDP, CAM),
    )
    out_specs = P(FSDP, CAM, None)
    return jax.shard_map(local, mesh=sub_mesh, in_specs=in_specs, out_specs=out_specs, check_vma=False)
```

```python
import functools
import math

import jax
import jax.numpy as jnp
from jax import lax
from jax.experimental import pallas as pl
from jax.experimental.pallas import tpu as pltpu
from jax.sharding import Mesh
from jax.sharding import PartitionSpec as P

HEAD_DIM = 128
BLOCK = 32

CAM = ("x", "y_hi", "core")
FSDP = ("z", "y_lo")
Y = ("y_hi", "y_lo")


def attend(query_rows, key_rows, value_rows, key_ok):
    score_scale = 1.0 / math.sqrt(HEAD_DIM)
    count_all = query_rows.shape[0]
    head_count = query_rows.shape[1] // HEAD_DIM
    block_rows = 512
    outputs = []
    for head_number in range(head_count):
        column = head_number * HEAD_DIM
        query_h = query_rows[:, column : column + HEAD_DIM].reshape(
            count_all // block_rows, block_rows, HEAD_DIM
        )
        key_h = key_rows[:, column : column + HEAD_DIM]
        value_h = value_rows[:, column : column + HEAD_DIM]

        def one_block(query_block):
            scores = (
                jnp.einsum("qd,kd->qk", query_block, key_h, preferred_element_type=jnp.float32)
                * score_scale
            )
            scores = jnp.where(key_ok[None, :], scores, jnp.float32(-1e30))
            row_top = jnp.max(scores, axis=1, keepdims=True)
            raised = jnp.exp(scores - row_top)
            weights = (raised / jnp.sum(raised, axis=1, keepdims=True)).astype(jnp.bfloat16)
            return jnp.dot(weights, value_h, preferred_element_type=jnp.float32).astype(
                jnp.bfloat16
            )

        outputs.append(lax.map(one_block, query_h).reshape(count_all, HEAD_DIM))
    return jnp.concatenate(outputs, axis=1)


MESH_IDS = pl.DeviceIdType.MESH


RELATIVE = ((-1, 0), (1, 0), (0, 1), (2, 0), (-1, 1), (1, 1), (2, 1))
ROUTES = {
    (0, 0): (("z", 1, (0, 1, 2, 3)), ("z", -1, (0, 1, 2, 3)), ("y", 1, (0, 1)), ("y", -1, (2, 3))),
    (-1, 0): (("z", 1, (0, 1)), ("y", 1, (0, 1)), ("y", -1, (2, 3))),
    (1, 0): (("z", -1, (2, 3)), ("y", 1, (0, 1)), ("y", -1, (2, 3))),
    (0, 1): (),
    (2, 0): (("y", 1, (0,)), ("y", -1, (3,))),
    (-1, 1): (("z", 1, (1,)),),
    (1, 1): (("z", -1, (2,)),),
    (2, 1): (),
}
SOURCES = {
    (-1, 0): (("z", -1),) * 4,
    (1, 0): (("z", 1),) * 4,
    (0, 1): (("y", -1),) * 2 + (("y", 1),) * 2,
    (2, 0): (("z", -1),) * 2 + (("z", 1),) * 2,
    (-1, 1): (("y", -1),) * 2 + (("y", 1),) * 2,
    (1, 1): (("y", -1),) * 2 + (("y", 1),) * 2,
    (2, 1): (("y", -1), ("z", -1), ("z", 1), ("y", 1)),
}
ARRIVALS = (
    ((-1, 0), 0), ((1, 0), 0), ((0, 1), 0), ((0, 1), 2),
    ((-1, 0), 1), ((1, 0), 1), ((0, 1), 1), ((0, 1), 3),
    ((-1, 0), 2), ((1, 0), 2), ((-1, 1), 0),
    ((-1, 0), 3), ((1, 0), 3), ((1, 1), 0), ((-1, 1), 2),
    ((2, 0), 0), ((2, 0), 2), ((-1, 1), 1), ((1, 1), 2),
    ((2, 0), 1), ((2, 0), 3), ((1, 1), 1), ((-1, 1), 3),
    ((1, 1), 3), ((2, 1), 0), ((2, 1), 1), ((2, 1), 2),
    ((2, 1), 3),
)
CHUNKS = 4
SENDS = sum(len(c) for routes in ROUTES.values() for _, _, c in routes) + CHUNKS * len(RELATIVE)


def gather_kernel(col0, w_ref, out_ref, send, recv, local_sem):
    k = lax.axis_index("core")
    z = lax.axis_index("z")
    yl = lax.axis_index("y_lo")
    y = lax.axis_index("y_hi") * 2 + yl
    shard = w_ref.shape[0]
    half = shard // 2
    chunk = half // CHUNKS
    ncols = out_ref.shape[1]
    cols = pl.ds(col0, ncols)

    def device(axis, step):
        if axis == "z":
            return {"z": (z + step) % 4}
        yy = (y + step) % 4
        return {"y_hi": yy // 2, "y_lo": yy % 2}

    partner = {"core": 1 - k}
    neighbours = (device("z", 1), device("z", -1), device("y", 1), device("y", -1), partner)

    def shard_of(rel):
        dz, flip = rel
        return ((z + dz) % 4) * 2 + (yl + flip) % 2

    def region(rel, kk, c):
        start = shard_of(rel) * shard + kk * half + c * chunk
        return out_ref.at[pl.ds(pl.multiple_of(start, chunk), chunk)]

    def seen_by(rel, axis, step):
        dz, flip = rel
        if axis == "z":
            return ((dz - step + 1) % 4 - 1, flip)
        return (dz, 1 - flip)

    def recv_slot(rel, c, from_partner):
        return (len(RELATIVE) if from_partner else 0) * CHUNKS + RELATIVE.index(rel) * CHUNKS + c

    barrier = pltpu.get_barrier_semaphore()
    for dev in neighbours:
        pl.semaphore_signal(barrier, inc=1, device_id=dev, device_id_type=MESH_IDS)
    pl.semaphore_wait(barrier, len(neighbours))

    own = shard_of((0, 0))
    local_copy = pltpu.make_async_copy(
        w_ref.at[:, cols], out_ref.at[pl.ds(pl.multiple_of(own * shard, shard), shard)], local_sem
    )
    local_copy.start()

    sent = []

    def pass_on(rel, c):
        for axis, step, chunks in ROUTES[rel]:
            if c in chunks:
                src = region(rel, k, c)
                slot = recv_slot(seen_by(rel, axis, step), c, False)
                copy = pltpu.make_async_remote_copy(
                    src_ref=src, dst_ref=src, send_sem=send.at[len(sent)], recv_sem=recv.at[slot],
                    device_id=device(axis, step), device_id_type=MESH_IDS,
                )
                copy.start()
                sent.append(copy)
        if rel != (0, 0):
            piece = region(rel, k, c)
            copy = pltpu.make_async_remote_copy(
                src_ref=piece, dst_ref=piece, send_sem=send.at[len(sent)],
                recv_sem=recv.at[recv_slot(rel, c, True)],
                device_id=partner, device_id_type=MESH_IDS,
            )
            copy.start()
            sent.append(copy)

    def arrive(rel, kk, c, dev, from_partner):
        piece = region(rel, kk, c)
        pltpu.make_async_remote_copy(
            src_ref=piece, dst_ref=piece, send_sem=send.at[0],
            recv_sem=recv.at[recv_slot(rel, c, from_partner)],
            device_id=dev, device_id_type=MESH_IDS,
        ).wait_recv()

    for axis, step, chunks in ROUTES[(0, 0)]:
        for c in chunks:
            src = w_ref.at[pl.ds(pl.multiple_of(k * half + c * chunk, chunk), chunk), cols]
            there = seen_by((0, 0), axis, step)
            copy = pltpu.make_async_remote_copy(
                src_ref=src, dst_ref=region((0, 0), k, c), send_sem=send.at[len(sent)],
                recv_sem=recv.at[recv_slot(there, c, False)],
                device_id=device(axis, step), device_id_type=MESH_IDS,
            )
            copy.start()
            sent.append(copy)

    for rel, c in ARRIVALS:
        axis, step = SOURCES[rel][c]
        arrive(rel, k, c, device(axis, step), False)
        pass_on(rel, c)
    for rel in RELATIVE:
        for c in range(CHUNKS):
            arrive(rel, 1 - k, c, partner, True)
    assert len(sent) == SENDS
    for copy in sent:
        copy.wait_send()
    local_copy.wait()


def gather_weight(out_weight, col0, ncols, call_id):
    rows = out_weight.shape[0]
    fsdp = lax.axis_size("z") * lax.axis_size("y_lo")
    return pl.pallas_call(
        functools.partial(gather_kernel, col0),
        out_shape=jax.ShapeDtypeStruct((rows * fsdp, ncols), out_weight.dtype),
        in_specs=[pl.BlockSpec(memory_space=pl.ANY)],
        out_specs=pl.BlockSpec(memory_space=pl.ANY),
        scratch_shapes=[
            pltpu.SemaphoreType.DMA((SENDS,)),
            pltpu.SemaphoreType.DMA((2 * CHUNKS * len(RELATIVE),)),
            pltpu.SemaphoreType.DMA(()),
        ],
        compiler_params=pltpu.CompilerParams(collective_id=call_id, has_side_effects=True),
    )(out_weight)


def local(queries, keys, values, out_weight, block_counts, row_mask):
    query_rows = queries[0]
    row_count = query_rows.shape[0]
    cam_count = lax.axis_size(CAM)
    offsets = jnp.arange(row_count, dtype=jnp.int32)
    row_valid = (row_mask[0] == 1) & (offsets // BLOCK < block_counts[0, 0])
    width = query_rows.shape[1] // cam_count
    flag = jnp.broadcast_to(
        row_valid.astype(jnp.bfloat16)[:, None, None], (row_count, cam_count, 128)
    )
    packed = jnp.concatenate(
        [
            query_rows.reshape(row_count, cam_count, width),
            keys[0].reshape(row_count, cam_count, width),
            values[0].reshape(row_count, cam_count, width),
            flag,
        ],
        axis=2,
    )
    packed_all = lax.all_to_all(packed, CAM, split_axis=1, concat_axis=0, tiled=True)[:, 0]
    query_all = packed_all[:, :width]
    key_all = packed_all[:, width : 2 * width]
    value_all = packed_all[:, 2 * width : 3 * width]
    flag_all = packed_all[:, 3 * width :]
    weight_all = gather_weight(out_weight, 0, out_weight.shape[1], 0)
    query_all, key_all, value_all, flag_all, weight_all = lax.optimization_barrier(
        (query_all, key_all, value_all, flag_all, weight_all)
    )
    head_rows = attend(query_all, key_all, value_all, flag_all[:, 0] > 0.5)
    attended = lax.all_to_all(head_rows, CAM, split_axis=0, concat_axis=1, tiled=True)
    projected = jnp.dot(attended, weight_all, preferred_element_type=jnp.float32)
    result = jnp.where(row_valid[:, None], projected, jnp.float32(0.0)).astype(jnp.bfloat16)
    return result[None]


def solution(mesh):
    sub_mesh = Mesh(mesh.devices.reshape(4, 2, 2, 4, 2), CAM + FSDP)
    in_specs = (
        P(FSDP, CAM, None),
        P(FSDP, CAM, None),
        P(FSDP, CAM, None),
        P(FSDP, None),
        P(FSDP, CAM),
        P(FSDP, CAM),
    )
    out_specs = P(FSDP, CAM, None)
    return jax.shard_map(local, mesh=sub_mesh, in_specs=in_specs, out_specs=out_specs, check_vma=False)
```

```python
import functools
import math

import jax
import jax.numpy as jnp
from jax import lax
from jax.experimental import pallas as pl
from jax.experimental.pallas import tpu as pltpu
from jax.sharding import Mesh
from jax.sharding import PartitionSpec as P

HEAD_DIM = 128
BLOCK = 32

CAM = ("x", "y_hi", "core")
FSDP = ("z", "y_lo")
Y = ("y_hi", "y_lo")


MESH_IDS = pl.DeviceIdType.MESH


RELATIVE = ((-1, 0), (1, 0), (0, 1), (2, 0), (-1, 1), (1, 1), (2, 1))
ROUTES = {
    (0, 0): (("z", 1, (0, 1, 2, 3)), ("z", -1, (0, 1, 2, 3)), ("y", 1, (0, 1)), ("y", -1, (2, 3))),
    (-1, 0): (("z", 1, (0, 1)), ("y", 1, (0, 1)), ("y", -1, (2, 3))),
    (1, 0): (("z", -1, (2, 3)), ("y", 1, (0, 1)), ("y", -1, (2, 3))),
    (0, 1): (),
    (2, 0): (("y", 1, (0,)), ("y", -1, (3,))),
    (-1, 1): (("z", 1, (1,)),),
    (1, 1): (("z", -1, (2,)),),
    (2, 1): (),
}
SOURCES = {
    (-1, 0): (("z", -1),) * 4,
    (1, 0): (("z", 1),) * 4,
    (0, 1): (("y", -1),) * 2 + (("y", 1),) * 2,
    (2, 0): (("z", -1),) * 2 + (("z", 1),) * 2,
    (-1, 1): (("y", -1),) * 2 + (("y", 1),) * 2,
    (1, 1): (("y", -1),) * 2 + (("y", 1),) * 2,
    (2, 1): (("y", -1), ("z", -1), ("z", 1), ("y", 1)),
}
ARRIVALS = (
    ((-1, 0), 0), ((1, 0), 0), ((0, 1), 0), ((0, 1), 2),
    ((-1, 0), 1), ((1, 0), 1), ((0, 1), 1), ((0, 1), 3),
    ((-1, 0), 2), ((1, 0), 2), ((-1, 1), 0),
    ((-1, 0), 3), ((1, 0), 3), ((1, 1), 0), ((-1, 1), 2),
    ((2, 0), 0), ((2, 0), 2), ((-1, 1), 1), ((1, 1), 2),
    ((2, 0), 1), ((2, 0), 3), ((1, 1), 1), ((-1, 1), 3),
    ((1, 1), 3), ((2, 1), 0), ((2, 1), 1), ((2, 1), 2),
    ((2, 1), 3),
)
CHUNKS = 4
SENDS = sum(len(c) for routes in ROUTES.values() for _, _, c in routes) + CHUNKS * len(RELATIVE)


class WeightGather:
    def __init__(self, w_ref, out_ref, send, recv, local_sem):
        self.w_ref, self.out_ref, self.send, self.recv = w_ref, out_ref, send, recv
        self.local_sem = local_sem
        self.k = lax.axis_index("core")
        self.z = lax.axis_index("z")
        self.yl = lax.axis_index("y_lo")
        self.y = lax.axis_index("y_hi") * 2 + self.yl
        self.shard = w_ref.shape[0]
        self.half = self.shard // 2
        self.chunk = self.half // CHUNKS
        self.partner = {"core": 1 - self.k}
        self.sent = []

    def device(self, axis, step):
        if axis == "z":
            return {"z": (self.z + step) % 4}
        yy = (self.y + step) % 4
        return {"y_hi": yy // 2, "y_lo": yy % 2}

    def neighbours(self):
        return (self.device("z", 1), self.device("z", -1), self.device("y", 1), self.device("y", -1))

    def shard_of(self, rel):
        dz, flip = rel
        return ((self.z + dz) % 4) * 2 + (self.yl + flip) % 2

    def region(self, rel, kk, c):
        start = self.shard_of(rel) * self.shard + kk * self.half + c * self.chunk
        return self.out_ref.at[pl.ds(pl.multiple_of(start, self.chunk), self.chunk)]

    @staticmethod
    def seen_by(rel, axis, step):
        dz, flip = rel
        if axis == "z":
            return ((dz - step + 1) % 4 - 1, flip)
        return (dz, 1 - flip)

    @staticmethod
    def recv_slot(rel, c, from_partner):
        return (len(RELATIVE) if from_partner else 0) * CHUNKS + RELATIVE.index(rel) * CHUNKS + c

    def copy(self, src, dst, slot, dev):
        copy = pltpu.make_async_remote_copy(
            src_ref=src, dst_ref=dst, send_sem=self.send.at[len(self.sent)],
            recv_sem=self.recv.at[slot], device_id=dev, device_id_type=MESH_IDS,
        )
        copy.start()
        self.sent.append(copy)

    def start(self):
        k, shard, half, chunk = self.k, self.shard, self.half, self.chunk
        own = self.shard_of((0, 0))
        self.local_copy = pltpu.make_async_copy(
            self.w_ref, self.out_ref.at[pl.ds(pl.multiple_of(own * shard, shard), shard)],
            self.local_sem,
        )
        self.local_copy.start()
        for axis, step, chunks in ROUTES[(0, 0)]:
            for c in chunks:
                src = self.w_ref.at[pl.ds(pl.multiple_of(k * half + c * chunk, chunk), chunk)]
                slot = self.recv_slot(self.seen_by((0, 0), axis, step), c, False)
                self.copy(src, self.region((0, 0), k, c), slot, self.device(axis, step))

    def arrive(self, rel, kk, c, dev, from_partner):
        piece = self.region(rel, kk, c)
        pltpu.make_async_remote_copy(
            src_ref=piece, dst_ref=piece, send_sem=self.send.at[0],
            recv_sem=self.recv.at[self.recv_slot(rel, c, from_partner)],
            device_id=dev, device_id_type=MESH_IDS,
        ).wait_recv()

    def step(self, index):
        rel, c = ARRIVALS[index]
        axis, step = SOURCES[rel][c]
        self.arrive(rel, self.k, c, self.device(axis, step), False)
        piece = self.region(rel, self.k, c)
        for axis, step, chunks in ROUTES[rel]:
            if c in chunks:
                slot = self.recv_slot(self.seen_by(rel, axis, step), c, False)
                self.copy(piece, piece, slot, self.device(axis, step))
        self.copy(piece, piece, self.recv_slot(rel, c, True), self.partner)

    def finish(self):
        for rel in RELATIVE:
            for c in range(CHUNKS):
                self.arrive(rel, 1 - self.k, c, self.partner, True)
        assert len(self.sent) == SENDS
        for copy in self.sent:
            copy.wait_send()
        self.local_copy.wait()


def cam_device(j):
    return {"x": j // 4, "y_hi": (j // 2) % 2, "core": j % 2}


def fused_kernel(
    packed_ref, w_ref, weight_ref, attended_ref,
    inbox, heads, send, recv, local_sem, a2a_send, a2a_recv, back_send, back_recv, own_sems,
):
    cams = packed_ref.shape[0]
    rows = packed_ref.shape[1]
    width = heads.shape[2]
    head_count = width // HEAD_DIM
    me = (lax.axis_index("x") * 2 + lax.axis_index("y_hi")) * 2 + lax.axis_index("core")
    gather = WeightGather(w_ref, weight_ref, send, recv, local_sem)

    barrier = pltpu.get_barrier_semaphore()
    peers = [cam_device((me + d) % cams) for d in range(1, cams)]
    for dev in peers + list(gather.neighbours()):
        pl.semaphore_signal(barrier, inc=1, device_id=dev, device_id_type=MESH_IDS)
    pl.semaphore_wait(barrier, len(peers) + 4)

    gather.start()
    own_in = pltpu.make_async_copy(packed_ref.at[me], inbox.at[me], own_sems.at[0])
    own_in.start()
    outgoing = []
    for d in range(1, cams):
        peer = (me + d) % cams
        copy = pltpu.make_async_remote_copy(
            src_ref=packed_ref.at[peer], dst_ref=inbox.at[me], send_sem=a2a_send.at[d - 1],
            recv_sem=a2a_recv.at[d - 1], device_id=cam_device(peer), device_id_type=MESH_IDS,
        )
        copy.start()
        outgoing.append(copy)

    arrivals = iter(range(len(ARRIVALS)))
    gather.step(next(arrivals))
    own_in.wait()
    for d in range(1, cams):
        source = (me - d + cams) % cams
        pltpu.make_async_remote_copy(
            src_ref=inbox.at[source], dst_ref=inbox.at[source], send_sem=a2a_send.at[d - 1],
            recv_sem=a2a_recv.at[d - 1], device_id=cam_device(source), device_id_type=MESH_IDS,
        ).wait_recv()

    total = cams * rows
    flags = inbox[:, :, 3 * width : 3 * width + 128].reshape(total, 128)
    counted = lax.dot_general(
        jnp.ones((8, 128), flags.dtype), flags, (((1,), (1,)), ((), ())),
        preferred_element_type=jnp.float32,
    )
    key_ok = counted[0:1, :] > 64.0
    score_scale = 1.0 / math.sqrt(HEAD_DIM)
    group = 2
    for h in range(head_count):
        column = h * HEAD_DIM
        key_h = inbox[:, :, width + column : width + column + HEAD_DIM].reshape(total, HEAD_DIM)
        value_h = inbox[:, :, 2 * width + column : 2 * width + column + HEAD_DIM].reshape(
            total, HEAD_DIM
        )
        for g in range(cams // group):
            query_block = inbox[g * group : (g + 1) * group, :, column : column + HEAD_DIM].reshape(
                group * rows, HEAD_DIM
            )
            scores = lax.dot_general(
                query_block, key_h, (((1,), (1,)), ((), ())), preferred_element_type=jnp.float32
            ) * score_scale
            scores = jnp.where(key_ok, scores, jnp.float32(-1e30))
            row_top = jnp.max(scores, axis=1, keepdims=True)
            raised = jnp.exp(scores - row_top)
            weights = (raised / jnp.sum(raised, axis=1, keepdims=True)).astype(jnp.bfloat16)
            out = jnp.dot(weights, value_h, preferred_element_type=jnp.float32).astype(jnp.bfloat16)
            heads[g * group : (g + 1) * group, :, column : column + HEAD_DIM] = out.reshape(
                group, rows, HEAD_DIM
            )
            if g % 2 == 1:
                gather.step(next(arrivals))

    for copy in outgoing:
        copy.wait_send()
    own_back = pltpu.make_async_copy(
        heads.at[me], attended_ref.at[:, pl.ds(pl.multiple_of(me * width, width), width)],
        own_sems.at[1],
    )
    own_back.start()
    returning = []
    for d in range(1, cams):
        peer = (me + d) % cams
        copy = pltpu.make_async_remote_copy(
            src_ref=heads.at[peer],
            dst_ref=attended_ref.at[:, pl.ds(pl.multiple_of(me * width, width), width)],
            send_sem=back_send.at[d - 1], recv_sem=back_recv.at[d - 1],
            device_id=cam_device(peer), device_id_type=MESH_IDS,
        )
        copy.start()
        returning.append(copy)
    for index in arrivals:
        gather.step(index)
    gather.finish()
    for d in range(1, cams):
        source = (me - d + cams) % cams
        region = attended_ref.at[:, pl.ds(pl.multiple_of(source * width, width), width)]
        pltpu.make_async_remote_copy(
            src_ref=region, dst_ref=region, send_sem=back_send.at[d - 1],
            recv_sem=back_recv.at[d - 1], device_id=cam_device(source), device_id_type=MESH_IDS,
        ).wait_recv()
    for copy in returning:
        copy.wait_send()
    own_back.wait()


def fused(packed, out_weight):
    cams, rows, packed_width = packed.shape
    width = (packed_width - 128) // 3
    shard, cols = out_weight.shape
    fsdp = lax.axis_size("z") * lax.axis_size("y_lo")
    return pl.pallas_call(
        fused_kernel,
        out_shape=(
            jax.ShapeDtypeStruct((shard * fsdp, cols), out_weight.dtype),
            jax.ShapeDtypeStruct((rows, cams * width), packed.dtype),
        ),
        in_specs=[pl.BlockSpec(memory_space=pl.ANY), pl.BlockSpec(memory_space=pl.ANY)],
        out_specs=(pl.BlockSpec(memory_space=pl.ANY), pl.BlockSpec(memory_space=pl.ANY)),
        scratch_shapes=[
            pltpu.VMEM((cams, rows, packed_width), packed.dtype),
            pltpu.VMEM((cams, rows, width), packed.dtype),
            pltpu.SemaphoreType.DMA((SENDS,)),
            pltpu.SemaphoreType.DMA((2 * CHUNKS * len(RELATIVE),)),
            pltpu.SemaphoreType.DMA(()),
            pltpu.SemaphoreType.DMA((cams - 1,)),
            pltpu.SemaphoreType.DMA((cams - 1,)),
            pltpu.SemaphoreType.DMA((cams - 1,)),
            pltpu.SemaphoreType.DMA((cams - 1,)),
            pltpu.SemaphoreType.DMA((2,)),
        ],
        compiler_params=pltpu.CompilerParams(
            collective_id=0, has_side_effects=True, vmem_limit_bytes=60 * 1024 * 1024
        ),
    )(packed, out_weight)


def local(queries, keys, values, out_weight, block_counts, row_mask):
    query_rows = queries[0]
    row_count = query_rows.shape[0]
    cam_count = lax.axis_size(CAM)
    offsets = jnp.arange(row_count, dtype=jnp.int32)
    row_valid = (row_mask[0] == 1) & (offsets // BLOCK < block_counts[0, 0])
    width = query_rows.shape[1] // cam_count

    def by_head(x):
        return x.reshape(row_count, cam_count, width).transpose(1, 0, 2)

    flag = jnp.broadcast_to(
        row_valid.astype(jnp.bfloat16)[None, :, None], (cam_count, row_count, 128)
    )
    packed = jnp.concatenate([by_head(query_rows), by_head(keys[0]), by_head(values[0]), flag], axis=2)
    weight_all, attended = fused(packed, out_weight)
    projected = jnp.dot(attended, weight_all, preferred_element_type=jnp.float32)
    result = jnp.where(row_valid[:, None], projected, jnp.float32(0.0)).astype(jnp.bfloat16)
    return result[None]


def solution(mesh):
    sub_mesh = Mesh(mesh.devices.reshape(4, 2, 2, 4, 2), CAM + FSDP)
    in_specs = (
        P(FSDP, CAM, None),
        P(FSDP, CAM, None),
        P(FSDP, CAM, None),
        P(FSDP, None),
        P(FSDP, CAM),
        P(FSDP, CAM),
    )
    out_specs = P(FSDP, CAM, None)
    return jax.shard_map(local, mesh=sub_mesh, in_specs=in_specs, out_specs=out_specs, check_vma=False)
```

```python
import functools
import math

import jax
import jax.numpy as jnp
from jax import lax
from jax.experimental import pallas as pl
from jax.experimental.pallas import tpu as pltpu
from jax.sharding import Mesh
from jax.sharding import PartitionSpec as P

HEAD_DIM = 128
BLOCK = 32

CAM = ("x", "y_hi", "core")
FSDP = ("z", "y_lo")
Y = ("y_hi", "y_lo")


MESH_IDS = pl.DeviceIdType.MESH


RELATIVE = ((-1, 0), (1, 0), (0, 1), (2, 0), (-1, 1), (1, 1), (2, 1))
ROUTES = {
    (0, 0): (("z", 1, (0, 1, 2, 3)), ("z", -1, (0, 1, 2, 3)), ("y", 1, (0, 1)), ("y", -1, (2, 3))),
    (-1, 0): (("z", 1, (0, 1)), ("y", 1, (0, 1)), ("y", -1, (2, 3))),
    (1, 0): (("z", -1, (2, 3)), ("y", 1, (0, 1)), ("y", -1, (2, 3))),
    (0, 1): (),
    (2, 0): (("y", 1, (0,)), ("y", -1, (3,))),
    (-1, 1): (("z", 1, (1,)),),
    (1, 1): (("z", -1, (2,)),),
    (2, 1): (),
}
SOURCES = {
    (-1, 0): (("z", -1),) * 4,
    (1, 0): (("z", 1),) * 4,
    (0, 1): (("y", -1),) * 2 + (("y", 1),) * 2,
    (2, 0): (("z", -1),) * 2 + (("z", 1),) * 2,
    (-1, 1): (("y", -1),) * 2 + (("y", 1),) * 2,
    (1, 1): (("y", -1),) * 2 + (("y", 1),) * 2,
    (2, 1): (("y", -1), ("z", -1), ("z", 1), ("y", 1)),
}
ARRIVALS = (
    ((-1, 0), 0), ((1, 0), 0), ((0, 1), 0), ((0, 1), 2),
    ((-1, 0), 1), ((1, 0), 1), ((0, 1), 1), ((0, 1), 3),
    ((-1, 0), 2), ((1, 0), 2), ((-1, 1), 0),
    ((-1, 0), 3), ((1, 0), 3), ((1, 1), 0), ((-1, 1), 2),
    ((2, 0), 0), ((2, 0), 2), ((-1, 1), 1), ((1, 1), 2),
    ((2, 0), 1), ((2, 0), 3), ((1, 1), 1), ((-1, 1), 3),
    ((1, 1), 3), ((2, 1), 0), ((2, 1), 1), ((2, 1), 2),
    ((2, 1), 3),
)
CHUNKS = 4
SENDS = sum(len(c) for routes in ROUTES.values() for _, _, c in routes) + CHUNKS * len(RELATIVE)


class WeightGather:
    def __init__(self, w_ref, out_ref, send, recv, local_sem):
        self.w_ref, self.out_ref, self.send, self.recv = w_ref, out_ref, send, recv
        self.local_sem = local_sem
        self.k = lax.axis_index("core")
        self.z = lax.axis_index("z")
        self.yl = lax.axis_index("y_lo")
        self.y = lax.axis_index("y_hi") * 2 + self.yl
        self.shard = w_ref.shape[0]
        self.half = self.shard // 2
        self.chunk = self.half // CHUNKS
        self.partner = {"core": 1 - self.k}
        self.sent = []

    def device(self, axis, step):
        if axis == "z":
            return {"z": (self.z + step) % 4}
        yy = (self.y + step) % 4
        return {"y_hi": yy // 2, "y_lo": yy % 2}

    def neighbours(self):
        return (self.device("z", 1), self.device("z", -1), self.device("y", 1), self.device("y", -1))

    def shard_of(self, rel):
        dz, flip = rel
        return ((self.z + dz) % 4) * 2 + (self.yl + flip) % 2

    def region(self, rel, kk, c):
        start = self.shard_of(rel) * self.shard + kk * self.half + c * self.chunk
        return self.out_ref.at[pl.ds(pl.multiple_of(start, self.chunk), self.chunk)]

    @staticmethod
    def seen_by(rel, axis, step):
        dz, flip = rel
        if axis == "z":
            return ((dz - step + 1) % 4 - 1, flip)
        return (dz, 1 - flip)

    @staticmethod
    def recv_slot(rel, c, from_partner):
        return (len(RELATIVE) if from_partner else 0) * CHUNKS + RELATIVE.index(rel) * CHUNKS + c

    def copy(self, src, dst, slot, dev):
        copy = pltpu.make_async_remote_copy(
            src_ref=src, dst_ref=dst, send_sem=self.send.at[len(self.sent)],
            recv_sem=self.recv.at[slot], device_id=dev, device_id_type=MESH_IDS,
        )
        copy.start()
        self.sent.append(copy)

    def start(self):
        k, shard, half, chunk = self.k, self.shard, self.half, self.chunk
        own = self.shard_of((0, 0))
        self.local_copy = pltpu.make_async_copy(
            self.w_ref, self.out_ref.at[pl.ds(pl.multiple_of(own * shard, shard), shard)],
            self.local_sem,
        )
        self.local_copy.start()
        for axis, step, chunks in ROUTES[(0, 0)]:
            for c in chunks:
                src = self.w_ref.at[pl.ds(pl.multiple_of(k * half + c * chunk, chunk), chunk)]
                slot = self.recv_slot(self.seen_by((0, 0), axis, step), c, False)
                self.copy(src, self.region((0, 0), k, c), slot, self.device(axis, step))

    def arrive(self, rel, kk, c, dev, from_partner):
        piece = self.region(rel, kk, c)
        pltpu.make_async_remote_copy(
            src_ref=piece, dst_ref=piece, send_sem=self.send.at[0],
            recv_sem=self.recv.at[self.recv_slot(rel, c, from_partner)],
            device_id=dev, device_id_type=MESH_IDS,
        ).wait_recv()

    def step(self, index):
        rel, c = ARRIVALS[index]
        axis, step = SOURCES[rel][c]
        self.arrive(rel, self.k, c, self.device(axis, step), False)
        piece = self.region(rel, self.k, c)
        for axis, step, chunks in ROUTES[rel]:
            if c in chunks:
                slot = self.recv_slot(self.seen_by(rel, axis, step), c, False)
                self.copy(piece, piece, slot, self.device(axis, step))
        self.copy(piece, piece, self.recv_slot(rel, c, True), self.partner)

    def finish(self):
        for rel in RELATIVE:
            for c in range(CHUNKS):
                self.arrive(rel, 1 - self.k, c, self.partner, True)
        assert len(self.sent) == SENDS
        for copy in self.sent:
            copy.wait_send()
        self.local_copy.wait()


def cam_device(j):
    return {"x": j // 4, "y_hi": (j // 2) % 2, "core": j % 2}


def fused_kernel(
    packed_ref, w_ref, weight_ref, attended_ref,
    inbox, heads, send, recv, local_sem, a2a_send, a2a_recv, back_send, back_recv, own_sems,
):
    cams = packed_ref.shape[0]
    rows = packed_ref.shape[1]
    width = heads.shape[2]
    head_count = width // HEAD_DIM
    me = (lax.axis_index("x") * 2 + lax.axis_index("y_hi")) * 2 + lax.axis_index("core")
    gather = WeightGather(w_ref, weight_ref, send, recv, local_sem)

    barrier = pltpu.get_barrier_semaphore()
    peers = [cam_device((me + d) % cams) for d in range(1, cams)]
    for dev in peers + list(gather.neighbours()):
        pl.semaphore_signal(barrier, inc=1, device_id=dev, device_id_type=MESH_IDS)
    pl.semaphore_wait(barrier, len(peers) + 4)

    gather.start()
    own_in = pltpu.make_async_copy(packed_ref.at[me], inbox.at[me], own_sems.at[0])
    own_in.start()
    outgoing = []
    for d in range(1, cams):
        peer = (me + d) % cams
        copy = pltpu.make_async_remote_copy(
            src_ref=packed_ref.at[peer], dst_ref=inbox.at[me], send_sem=a2a_send.at[d - 1],
            recv_sem=a2a_recv.at[d - 1], device_id=cam_device(peer), device_id_type=MESH_IDS,
        )
        copy.start()
        outgoing.append(copy)

    arrivals = iter(range(len(ARRIVALS)))
    for _ in range(4):
        gather.step(next(arrivals))
    own_in.wait()
    for d in range(1, cams):
        source = (me - d + cams) % cams
        pltpu.make_async_remote_copy(
            src_ref=inbox.at[source], dst_ref=inbox.at[source], send_sem=a2a_send.at[d - 1],
            recv_sem=a2a_recv.at[d - 1], device_id=cam_device(source), device_id_type=MESH_IDS,
        ).wait_recv()

    total = cams * rows
    flags = inbox[:, :, 3 * width : 3 * width + 128].reshape(total, 128)
    counted = lax.dot_general(
        jnp.ones((8, 128), flags.dtype), flags, (((1,), (1,)), ((), ())),
        preferred_element_type=jnp.float32,
    )
    key_ok = counted[0:1, :] > 64.0
    score_scale = 1.0 / math.sqrt(HEAD_DIM)
    group = 2
    per_segment = 2
    for h in range(head_count):
        column = h * HEAD_DIM
        key_h = inbox[:, :, width + column : width + column + HEAD_DIM].reshape(total, HEAD_DIM)
        value_h = inbox[:, :, 2 * width + column : 2 * width + column + HEAD_DIM].reshape(
            total, HEAD_DIM
        )

        def attend_group(g, carry, column=column, key_h=key_h, value_h=value_h):
            first = pl.multiple_of(g * group, group)
            query_block = inbox[pl.ds(first, group), :, column : column + HEAD_DIM].reshape(
                group * rows, HEAD_DIM
            )
            scores = lax.dot_general(
                query_block, key_h, (((1,), (1,)), ((), ())), preferred_element_type=jnp.float32
            ) * score_scale
            scores = jnp.where(key_ok, scores, jnp.float32(-1e30))
            row_top = jnp.max(scores, axis=1, keepdims=True)
            raised = jnp.exp(scores - row_top)
            weights = (raised / jnp.sum(raised, axis=1, keepdims=True)).astype(jnp.bfloat16)
            out = jnp.dot(weights, value_h, preferred_element_type=jnp.float32).astype(jnp.bfloat16)
            heads[pl.ds(first, group), :, column : column + HEAD_DIM] = out.reshape(
                group, rows, HEAD_DIM
            )
            return carry

        for segment in range(cams // group // per_segment):
            lax.fori_loop(segment * per_segment, (segment + 1) * per_segment, attend_group, 0)
            gather.step(next(arrivals))

    for copy in outgoing:
        copy.wait_send()
    own_back = pltpu.make_async_copy(
        heads.at[me], attended_ref.at[:, pl.ds(pl.multiple_of(me * width, width), width)],
        own_sems.at[1],
    )
    own_back.start()
    returning = []
    for d in range(1, cams):
        peer = (me + d) % cams
        copy = pltpu.make_async_remote_copy(
            src_ref=heads.at[peer],
            dst_ref=attended_ref.at[:, pl.ds(pl.multiple_of(me * width, width), width)],
            send_sem=back_send.at[d - 1], recv_sem=back_recv.at[d - 1],
            device_id=cam_device(peer), device_id_type=MESH_IDS,
        )
        copy.start()
        returning.append(copy)
    for index in arrivals:
        gather.step(index)
    gather.finish()
    for d in range(1, cams):
        source = (me - d + cams) % cams
        region = attended_ref.at[:, pl.ds(pl.multiple_of(source * width, width), width)]
        pltpu.make_async_remote_copy(
            src_ref=region, dst_ref=region, send_sem=back_send.at[d - 1],
            recv_sem=back_recv.at[d - 1], device_id=cam_device(source), device_id_type=MESH_IDS,
        ).wait_recv()
    for copy in returning:
        copy.wait_send()
    own_back.wait()


def fused(packed, out_weight):
    cams, rows, packed_width = packed.shape
    width = (packed_width - 128) // 3
    shard, cols = out_weight.shape
    fsdp = lax.axis_size("z") * lax.axis_size("y_lo")
    return pl.pallas_call(
        fused_kernel,
        out_shape=(
            jax.ShapeDtypeStruct((shard * fsdp, cols), out_weight.dtype),
            jax.ShapeDtypeStruct((rows, cams * width), packed.dtype),
        ),
        in_specs=[pl.BlockSpec(memory_space=pl.ANY), pl.BlockSpec(memory_space=pl.ANY)],
        out_specs=(pl.BlockSpec(memory_space=pl.ANY), pl.BlockSpec(memory_space=pl.ANY)),
        scratch_shapes=[
            pltpu.VMEM((cams, rows, packed_width), packed.dtype),
            pltpu.VMEM((cams, rows, width), packed.dtype),
            pltpu.SemaphoreType.DMA((SENDS,)),
            pltpu.SemaphoreType.DMA((2 * CHUNKS * len(RELATIVE),)),
            pltpu.SemaphoreType.DMA(()),
            pltpu.SemaphoreType.DMA((cams - 1,)),
            pltpu.SemaphoreType.DMA((cams - 1,)),
            pltpu.SemaphoreType.DMA((cams - 1,)),
            pltpu.SemaphoreType.DMA((cams - 1,)),
            pltpu.SemaphoreType.DMA((2,)),
        ],
        compiler_params=pltpu.CompilerParams(
            collective_id=0, has_side_effects=True, vmem_limit_bytes=60 * 1024 * 1024
        ),
    )(packed, out_weight)


def local(queries, keys, values, out_weight, block_counts, row_mask):
    query_rows = queries[0]
    row_count = query_rows.shape[0]
    cam_count = lax.axis_size(CAM)
    offsets = jnp.arange(row_count, dtype=jnp.int32)
    row_valid = (row_mask[0] == 1) & (offsets // BLOCK < block_counts[0, 0])
    width = query_rows.shape[1] // cam_count

    def by_head(x):
        return x.reshape(row_count, cam_count, width).transpose(1, 0, 2)

    flag = jnp.broadcast_to(
        row_valid.astype(jnp.bfloat16)[None, :, None], (cam_count, row_count, 128)
    )
    packed = jnp.concatenate([by_head(query_rows), by_head(keys[0]), by_head(values[0]), flag], axis=2)
    weight_all, attended = fused(packed, out_weight)
    projected = jnp.dot(attended, weight_all, preferred_element_type=jnp.float32)
    result = jnp.where(row_valid[:, None], projected, jnp.float32(0.0)).astype(jnp.bfloat16)
    return result[None]


def solution(mesh):
    sub_mesh = Mesh(mesh.devices.reshape(4, 2, 2, 4, 2), CAM + FSDP)
    in_specs = (
        P(FSDP, CAM, None),
        P(FSDP, CAM, None),
        P(FSDP, CAM, None),
        P(FSDP, None),
        P(FSDP, CAM),
        P(FSDP, CAM),
    )
    out_specs = P(FSDP, CAM, None)
    return jax.shard_map(local, mesh=sub_mesh, in_specs=in_specs, out_specs=out_specs, check_vma=False)
```

```python
import functools
import math

import jax
import jax.numpy as jnp
from jax import lax
from jax.experimental import pallas as pl
from jax.experimental.pallas import tpu as pltpu
from jax.sharding import Mesh
from jax.sharding import PartitionSpec as P

HEAD_DIM = 128
BLOCK = 32

CAM = ("x", "y_hi", "core")
FSDP = ("z", "y_lo")
Y = ("y_hi", "y_lo")


MESH_IDS = pl.DeviceIdType.MESH


RELATIVE = ((-1, 0), (1, 0), (0, 1), (2, 0), (-1, 1), (1, 1), (2, 1))
ROUTES = {
    (0, 0): (("z", 1, (0, 1, 2, 3)), ("z", -1, (0, 1, 2, 3)), ("y", 1, (0, 1)), ("y", -1, (2, 3))),
    (-1, 0): (("z", 1, (0, 1)), ("y", 1, (0, 1)), ("y", -1, (2, 3))),
    (1, 0): (("z", -1, (2, 3)), ("y", 1, (0, 1)), ("y", -1, (2, 3))),
    (0, 1): (),
    (2, 0): (),
    (-1, 1): (("z", 1, (0, 1)),),
    (1, 1): (("z", -1, (2, 3)),),
    (2, 1): (),
}
SOURCES = {
    (-1, 0): (("z", -1),) * 4,
    (1, 0): (("z", 1),) * 4,
    (0, 1): (("y", -1),) * 2 + (("y", 1),) * 2,
    (2, 0): (("z", -1),) * 2 + (("z", 1),) * 2,
    (-1, 1): (("y", -1),) * 2 + (("y", 1),) * 2,
    (1, 1): (("y", -1),) * 2 + (("y", 1),) * 2,
    (2, 1): (("z", -1),) * 2 + (("z", 1),) * 2,
}
ARRIVALS = (
    ((-1, 0), 0), ((1, 0), 0), ((0, 1), 0), ((0, 1), 2),
    ((-1, 0), 1), ((1, 0), 1), ((0, 1), 1), ((0, 1), 3),
    ((-1, 0), 2), ((1, 0), 2), ((-1, 1), 0),
    ((-1, 0), 3), ((1, 0), 3), ((1, 1), 0), ((-1, 1), 2),
    ((2, 0), 0), ((2, 0), 2), ((-1, 1), 1), ((1, 1), 2),
    ((2, 0), 1), ((2, 0), 3), ((1, 1), 1), ((-1, 1), 3),
    ((1, 1), 3), ((2, 1), 0), ((2, 1), 2), ((2, 1), 1),
    ((2, 1), 3),
)
CHUNKS = 4
SENDS = sum(len(c) for routes in ROUTES.values() for _, _, c in routes) + CHUNKS * len(RELATIVE)


class WeightGather:
    def __init__(self, w_ref, out_ref, send, recv, local_sem):
        self.w_ref, self.out_ref, self.send, self.recv = w_ref, out_ref, send, recv
        self.local_sem = local_sem
        self.k = lax.axis_index("core")
        self.z = lax.axis_index("z")
        self.yl = lax.axis_index("y_lo")
        self.y = lax.axis_index("y_hi") * 2 + self.yl
        self.shard = w_ref.shape[0]
        self.half = self.shard // 2
        self.chunk = self.half // CHUNKS
        self.partner = {"core": 1 - self.k}
        self.sent = []

    def device(self, axis, step):
        if axis == "z":
            return {"z": (self.z + step) % 4}
        yy = (self.y + step) % 4
        return {"y_hi": yy // 2, "y_lo": yy % 2}

    def neighbours(self):
        return (self.device("z", 1), self.device("z", -1), self.device("y", 1), self.device("y", -1))

    def shard_of(self, rel):
        dz, flip = rel
        return ((self.z + dz) % 4) * 2 + (self.yl + flip) % 2

    def region(self, rel, kk, c):
        start = self.shard_of(rel) * self.shard + kk * self.half + c * self.chunk
        return self.out_ref.at[pl.ds(pl.multiple_of(start, self.chunk), self.chunk)]

    @staticmethod
    def seen_by(rel, axis, step):
        dz, flip = rel
        if axis == "z":
            return ((dz - step + 1) % 4 - 1, flip)
        return (dz, 1 - flip)

    @staticmethod
    def recv_slot(rel, c, from_partner):
        return (len(RELATIVE) if from_partner else 0) * CHUNKS + RELATIVE.index(rel) * CHUNKS + c

    def copy(self, src, dst, slot, dev):
        copy = pltpu.make_async_remote_copy(
            src_ref=src, dst_ref=dst, send_sem=self.send.at[len(self.sent)],
            recv_sem=self.recv.at[slot], device_id=dev, device_id_type=MESH_IDS,
        )
        copy.start()
        self.sent.append(copy)

    def start(self):
        k, shard, half, chunk = self.k, self.shard, self.half, self.chunk
        own = self.shard_of((0, 0))
        self.local_copy = pltpu.make_async_copy(
            self.w_ref, self.out_ref.at[pl.ds(pl.multiple_of(own * shard, shard), shard)],
            self.local_sem,
        )
        self.local_copy.start()
        for axis, step, chunks in ROUTES[(0, 0)]:
            for c in chunks:
                src = self.w_ref.at[pl.ds(pl.multiple_of(k * half + c * chunk, chunk), chunk)]
                slot = self.recv_slot(self.seen_by((0, 0), axis, step), c, False)
                self.copy(src, self.region((0, 0), k, c), slot, self.device(axis, step))

    def arrive(self, rel, kk, c, dev, from_partner):
        piece = self.region(rel, kk, c)
        pltpu.make_async_remote_copy(
            src_ref=piece, dst_ref=piece, send_sem=self.send.at[0],
            recv_sem=self.recv.at[self.recv_slot(rel, c, from_partner)],
            device_id=dev, device_id_type=MESH_IDS,
        ).wait_recv()

    def step(self, index):
        rel, c = ARRIVALS[index]
        axis, step = SOURCES[rel][c]
        self.arrive(rel, self.k, c, self.device(axis, step), False)
        piece = self.region(rel, self.k, c)
        for axis, step, chunks in ROUTES[rel]:
            if c in chunks:
                slot = self.recv_slot(self.seen_by(rel, axis, step), c, False)
                self.copy(piece, piece, slot, self.device(axis, step))
        self.copy(piece, piece, self.recv_slot(rel, c, True), self.partner)

    def finish(self):
        for rel in RELATIVE:
            for c in range(CHUNKS):
                self.arrive(rel, 1 - self.k, c, self.partner, True)
        assert len(self.sent) == SENDS
        for copy in self.sent:
            copy.wait_send()
        self.local_copy.wait()


def cam_device(j):
    return {"x": j // 4, "y_hi": (j // 2) % 2, "core": j % 2}


def fused_kernel(
    packed_ref, w_ref, weight_ref, attended_ref,
    inbox, heads, send, recv, local_sem, a2a_send, a2a_recv, back_send, back_recv, own_sems,
):
    cams = packed_ref.shape[0]
    rows = packed_ref.shape[1]
    width = heads.shape[2]
    head_count = width // HEAD_DIM
    me = (lax.axis_index("x") * 2 + lax.axis_index("y_hi")) * 2 + lax.axis_index("core")
    gather = WeightGather(w_ref, weight_ref, send, recv, local_sem)

    barrier = pltpu.get_barrier_semaphore()
    peers = [cam_device((me + d) % cams) for d in range(1, cams)]
    for dev in peers + list(gather.neighbours()):
        pl.semaphore_signal(barrier, inc=1, device_id=dev, device_id_type=MESH_IDS)
    pl.semaphore_wait(barrier, len(peers) + 4)

    gather.start()
    own_in = pltpu.make_async_copy(packed_ref.at[me], inbox.at[me], own_sems.at[0])
    own_in.start()
    outgoing = []
    for d in range(1, cams):
        peer = (me + d) % cams
        copy = pltpu.make_async_remote_copy(
            src_ref=packed_ref.at[peer], dst_ref=inbox.at[me], send_sem=a2a_send.at[d - 1],
            recv_sem=a2a_recv.at[d - 1], device_id=cam_device(peer), device_id_type=MESH_IDS,
        )
        copy.start()
        outgoing.append(copy)

    arrivals = iter(range(len(ARRIVALS)))
    for _ in range(4):
        gather.step(next(arrivals))
    own_in.wait()
    for d in range(1, cams):
        source = (me - d + cams) % cams
        pltpu.make_async_remote_copy(
            src_ref=inbox.at[source], dst_ref=inbox.at[source], send_sem=a2a_send.at[d - 1],
            recv_sem=a2a_recv.at[d - 1], device_id=cam_device(source), device_id_type=MESH_IDS,
        ).wait_recv()

    total = cams * rows
    flags = inbox[:, :, 3 * width : 3 * width + 128].reshape(total, 128)
    counted = lax.dot_general(
        jnp.ones((8, 128), flags.dtype), flags, (((1,), (1,)), ((), ())),
        preferred_element_type=jnp.float32,
    )
    key_ok = counted[0:1, :] > 64.0
    score_scale = 1.0 / math.sqrt(HEAD_DIM)
    group = 2
    per_segment = 2
    for h in range(head_count):
        column = h * HEAD_DIM
        key_h = inbox[:, :, width + column : width + column + HEAD_DIM].reshape(total, HEAD_DIM)
        value_h = inbox[:, :, 2 * width + column : 2 * width + column + HEAD_DIM].reshape(
            total, HEAD_DIM
        )

        def attend_group(g, carry, column=column, key_h=key_h, value_h=value_h):
            first = pl.multiple_of(g * group, group)
            query_block = inbox[pl.ds(first, group), :, column : column + HEAD_DIM].reshape(
                group * rows, HEAD_DIM
            )
            scores = lax.dot_general(
                query_block, key_h, (((1,), (1,)), ((), ())), preferred_element_type=jnp.float32
            ) * score_scale
            scores = jnp.where(key_ok, scores, jnp.float32(-1e30))
            row_top = jnp.max(scores, axis=1, keepdims=True)
            raised = jnp.exp(scores - row_top)
            weights = (raised / jnp.sum(raised, axis=1, keepdims=True)).astype(jnp.bfloat16)
            out = jnp.dot(weights, value_h, preferred_element_type=jnp.float32).astype(jnp.bfloat16)
            heads[pl.ds(first, group), :, column : column + HEAD_DIM] = out.reshape(
                group, rows, HEAD_DIM
            )
            return carry

        for segment in range(cams // group // per_segment):
            lax.fori_loop(segment * per_segment, (segment + 1) * per_segment, attend_group, 0)
            gather.step(next(arrivals))

    for copy in outgoing:
        copy.wait_send()
    own_back = pltpu.make_async_copy(
        heads.at[me], attended_ref.at[:, pl.ds(pl.multiple_of(me * width, width), width)],
        own_sems.at[1],
    )
    own_back.start()
    returning = []
    for d in range(1, cams):
        peer = (me + d) % cams
        copy = pltpu.make_async_remote_copy(
            src_ref=heads.at[peer],
            dst_ref=attended_ref.at[:, pl.ds(pl.multiple_of(me * width, width), width)],
            send_sem=back_send.at[d - 1], recv_sem=back_recv.at[d - 1],
            device_id=cam_device(peer), device_id_type=MESH_IDS,
        )
        copy.start()
        returning.append(copy)
    for index in arrivals:
        gather.step(index)
    gather.finish()
    for d in range(1, cams):
        source = (me - d + cams) % cams
        region = attended_ref.at[:, pl.ds(pl.multiple_of(source * width, width), width)]
        pltpu.make_async_remote_copy(
            src_ref=region, dst_ref=region, send_sem=back_send.at[d - 1],
            recv_sem=back_recv.at[d - 1], device_id=cam_device(source), device_id_type=MESH_IDS,
        ).wait_recv()
    for copy in returning:
        copy.wait_send()
    own_back.wait()


def fused(packed, out_weight):
    cams, rows, packed_width = packed.shape
    width = (packed_width - 128) // 3
    shard, cols = out_weight.shape
    fsdp = lax.axis_size("z") * lax.axis_size("y_lo")
    return pl.pallas_call(
        fused_kernel,
        out_shape=(
            jax.ShapeDtypeStruct((shard * fsdp, cols), out_weight.dtype),
            jax.ShapeDtypeStruct((rows, cams * width), packed.dtype),
        ),
        in_specs=[pl.BlockSpec(memory_space=pl.ANY), pl.BlockSpec(memory_space=pl.ANY)],
        out_specs=(pl.BlockSpec(memory_space=pl.ANY), pl.BlockSpec(memory_space=pl.ANY)),
        scratch_shapes=[
            pltpu.VMEM((cams, rows, packed_width), packed.dtype),
            pltpu.VMEM((cams, rows, width), packed.dtype),
            pltpu.SemaphoreType.DMA((SENDS,)),
            pltpu.SemaphoreType.DMA((2 * CHUNKS * len(RELATIVE),)),
            pltpu.SemaphoreType.DMA(()),
            pltpu.SemaphoreType.DMA((cams - 1,)),
            pltpu.SemaphoreType.DMA((cams - 1,)),
            pltpu.SemaphoreType.DMA((cams - 1,)),
            pltpu.SemaphoreType.DMA((cams - 1,)),
            pltpu.SemaphoreType.DMA((2,)),
        ],
        compiler_params=pltpu.CompilerParams(
            collective_id=0, has_side_effects=True, vmem_limit_bytes=60 * 1024 * 1024
        ),
    )(packed, out_weight)


def local(queries, keys, values, out_weight, block_counts, row_mask):
    query_rows = queries[0]
    row_count = query_rows.shape[0]
    cam_count = lax.axis_size(CAM)
    offsets = jnp.arange(row_count, dtype=jnp.int32)
    row_valid = (row_mask[0] == 1) & (offsets // BLOCK < block_counts[0, 0])
    width = query_rows.shape[1] // cam_count

    def by_head(x):
        return x.reshape(row_count, cam_count, width).transpose(1, 0, 2)

    flag = jnp.broadcast_to(
        row_valid.astype(jnp.bfloat16)[None, :, None], (cam_count, row_count, 128)
    )
    packed = jnp.concatenate([by_head(query_rows), by_head(keys[0]), by_head(values[0]), flag], axis=2)
    weight_all, attended = fused(packed, out_weight)
    projected = jnp.dot(attended, weight_all, preferred_element_type=jnp.float32)
    result = jnp.where(row_valid[:, None], projected, jnp.float32(0.0)).astype(jnp.bfloat16)
    return result[None]


def solution(mesh):
    sub_mesh = Mesh(mesh.devices.reshape(4, 2, 2, 4, 2), CAM + FSDP)
    in_specs = (
        P(FSDP, CAM, None),
        P(FSDP, CAM, None),
        P(FSDP, CAM, None),
        P(FSDP, None),
        P(FSDP, CAM),
        P(FSDP, CAM),
    )
    out_specs = P(FSDP, CAM, None)
    return jax.shard_map(local, mesh=sub_mesh, in_specs=in_specs, out_specs=out_specs, check_vma=False)
```

```python
import functools
import math

import jax
import jax.numpy as jnp
from jax import lax
from jax.experimental import pallas as pl
from jax.experimental.pallas import tpu as pltpu
from jax.sharding import Mesh
from jax.sharding import PartitionSpec as P

HEAD_DIM = 128
BLOCK = 32

CAM = ("x", "y_hi", "core")
FSDP = ("z", "y_lo")
Y = ("y_hi", "y_lo")


MESH_IDS = pl.DeviceIdType.MESH


RELATIVE = ((-1, 0), (1, 0), (0, 1), (2, 0), (-1, 1), (1, 1), (2, 1))
ROUTES = {
    (0, 0): (("z", 1, (0, 1, 2, 3)), ("z", -1, (0, 1, 2, 3)), ("y", 1, (0, 1)), ("y", -1, (2, 3))),
    (-1, 0): (("z", 1, (0, 1)), ("y", 1, (0, 1)), ("y", -1, (2, 3))),
    (1, 0): (("z", -1, (2, 3)), ("y", 1, (0, 1)), ("y", -1, (2, 3))),
    (0, 1): (),
    (2, 0): (),
    (-1, 1): (("z", 1, (0, 1)),),
    (1, 1): (("z", -1, (2, 3)),),
    (2, 1): (),
}
SOURCES = {
    (-1, 0): (("z", -1),) * 4,
    (1, 0): (("z", 1),) * 4,
    (0, 1): (("y", -1),) * 2 + (("y", 1),) * 2,
    (2, 0): (("z", -1),) * 2 + (("z", 1),) * 2,
    (-1, 1): (("y", -1),) * 2 + (("y", 1),) * 2,
    (1, 1): (("y", -1),) * 2 + (("y", 1),) * 2,
    (2, 1): (("z", -1),) * 2 + (("z", 1),) * 2,
}
ARRIVALS = (
    ((-1, 0), 0), ((1, 0), 0), ((0, 1), 0), ((0, 1), 2),
    ((-1, 0), 1), ((1, 0), 1), ((0, 1), 1), ((0, 1), 3),
    ((-1, 0), 2), ((1, 0), 2), ((-1, 1), 0),
    ((-1, 0), 3), ((1, 0), 3), ((1, 1), 0), ((-1, 1), 2),
    ((2, 0), 0), ((2, 0), 2), ((-1, 1), 1), ((1, 1), 2),
    ((2, 0), 1), ((2, 0), 3), ((1, 1), 1), ((-1, 1), 3),
    ((1, 1), 3), ((2, 1), 0), ((2, 1), 2), ((2, 1), 1),
    ((2, 1), 3),
)
CHUNKS = 4
SENDS = sum(len(c) for routes in ROUTES.values() for _, _, c in routes) + CHUNKS * len(RELATIVE)


class WeightGather:
    def __init__(self, w_ref, out_ref, send, recv, local_sem):
        self.w_ref, self.out_ref, self.send, self.recv = w_ref, out_ref, send, recv
        self.local_sem = local_sem
        self.k = lax.axis_index("core")
        self.z = lax.axis_index("z")
        self.yl = lax.axis_index("y_lo")
        self.y = lax.axis_index("y_hi") * 2 + self.yl
        self.shard = w_ref.shape[0]
        self.half = self.shard // 2
        self.chunk = self.half // CHUNKS
        self.partner = {"core": 1 - self.k}
        self.sent = []
        self.from_partner = set()

    def device(self, axis, step):
        if axis == "z":
            return {"z": (self.z + step) % 4}
        yy = (self.y + step) % 4
        return {"y_hi": yy // 2, "y_lo": yy % 2}

    def neighbours(self):
        return (self.device("z", 1), self.device("z", -1), self.device("y", 1), self.device("y", -1))

    def shard_of(self, rel):
        dz, flip = rel
        return ((self.z + dz) % 4) * 2 + (self.yl + flip) % 2

    def region(self, rel, kk, c):
        start = self.shard_of(rel) * self.shard + kk * self.half + c * self.chunk
        return self.out_ref.at[pl.ds(pl.multiple_of(start, self.chunk), self.chunk)]

    @staticmethod
    def seen_by(rel, axis, step):
        dz, flip = rel
        if axis == "z":
            return ((dz - step + 1) % 4 - 1, flip)
        return (dz, 1 - flip)

    @staticmethod
    def recv_slot(rel, c, from_partner):
        return (len(RELATIVE) if from_partner else 0) * CHUNKS + RELATIVE.index(rel) * CHUNKS + c

    def copy(self, src, dst, slot, dev):
        copy = pltpu.make_async_remote_copy(
            src_ref=src, dst_ref=dst, send_sem=self.send.at[len(self.sent)],
            recv_sem=self.recv.at[slot], device_id=dev, device_id_type=MESH_IDS,
        )
        copy.start()
        self.sent.append(copy)

    def start(self):
        k, shard, half, chunk = self.k, self.shard, self.half, self.chunk
        own = self.shard_of((0, 0))
        self.local_copy = pltpu.make_async_copy(
            self.w_ref, self.out_ref.at[pl.ds(pl.multiple_of(own * shard, shard), shard)],
            self.local_sem,
        )
        self.local_copy.start()
        for axis, step, chunks in ROUTES[(0, 0)]:
            for c in chunks:
                src = self.w_ref.at[pl.ds(pl.multiple_of(k * half + c * chunk, chunk), chunk)]
                slot = self.recv_slot(self.seen_by((0, 0), axis, step), c, False)
                self.copy(src, self.region((0, 0), k, c), slot, self.device(axis, step))

    def arrive(self, rel, kk, c, dev, from_partner):
        piece = self.region(rel, kk, c)
        pltpu.make_async_remote_copy(
            src_ref=piece, dst_ref=piece, send_sem=self.send.at[0],
            recv_sem=self.recv.at[self.recv_slot(rel, c, from_partner)],
            device_id=dev, device_id_type=MESH_IDS,
        ).wait_recv()

    def step(self, index):
        rel, c = ARRIVALS[index]
        axis, step = SOURCES[rel][c]
        self.arrive(rel, self.k, c, self.device(axis, step), False)
        piece = self.region(rel, self.k, c)
        for axis, step, chunks in ROUTES[rel]:
            if c in chunks:
                slot = self.recv_slot(self.seen_by(rel, axis, step), c, False)
                self.copy(piece, piece, slot, self.device(axis, step))
        self.copy(piece, piece, self.recv_slot(rel, c, True), self.partner)

    def partner_arrive(self, rel, c):
        if (rel, c) not in self.from_partner:
            self.from_partner.add((rel, c))
            self.arrive(rel, 1 - self.k, c, self.partner, True)

    def finish(self):
        for rel in RELATIVE:
            for c in range(CHUNKS):
                self.partner_arrive(rel, c)
        assert len(self.sent) == SENDS
        for copy in self.sent:
            copy.wait_send()
        self.local_copy.wait()


def cam_device(j):
    return {"x": j // 4, "y_hi": (j // 2) % 2, "core": j % 2}


def fused_kernel(
    packed_ref, w_ref, weight_ref, proj_ref,
    inbox, heads, attended, acc, wbuf, send, recv, local_sem, a2a_send, a2a_recv, back_send,
    back_recv, own_sems, wsems,
):
    cams = packed_ref.shape[0]
    rows = packed_ref.shape[1]
    width = heads.shape[2]
    head_count = width // HEAD_DIM
    me = (lax.axis_index("x") * 2 + lax.axis_index("y_hi")) * 2 + lax.axis_index("core")
    gather = WeightGather(w_ref, weight_ref, send, recv, local_sem)

    barrier = pltpu.get_barrier_semaphore()
    peers = [cam_device((me + d) % cams) for d in range(1, cams)]
    for dev in peers + list(gather.neighbours()):
        pl.semaphore_signal(barrier, inc=1, device_id=dev, device_id_type=MESH_IDS)
    pl.semaphore_wait(barrier, len(peers) + 4)

    gather.start()
    own_in = pltpu.make_async_copy(packed_ref.at[me], inbox.at[me], own_sems.at[0])
    own_in.start()
    outgoing = []
    for d in range(1, cams):
        peer = (me + d) % cams
        copy = pltpu.make_async_remote_copy(
            src_ref=packed_ref.at[peer], dst_ref=inbox.at[me], send_sem=a2a_send.at[d - 1],
            recv_sem=a2a_recv.at[d - 1], device_id=cam_device(peer), device_id_type=MESH_IDS,
        )
        copy.start()
        outgoing.append(copy)

    arrivals = iter(range(len(ARRIVALS)))
    for _ in range(4):
        gather.step(next(arrivals))
    own_in.wait()
    for d in range(1, cams):
        source = (me - d + cams) % cams
        pltpu.make_async_remote_copy(
            src_ref=inbox.at[source], dst_ref=inbox.at[source], send_sem=a2a_send.at[d - 1],
            recv_sem=a2a_recv.at[d - 1], device_id=cam_device(source), device_id_type=MESH_IDS,
        ).wait_recv()

    total = cams * rows
    flags = inbox[:, :, 3 * width : 3 * width + 128].reshape(total, 128)
    counted = lax.dot_general(
        jnp.ones((8, 128), flags.dtype), flags, (((1,), (1,)), ((), ())),
        preferred_element_type=jnp.float32,
    )
    key_ok = counted[0:1, :] > 64.0
    score_scale = 1.0 / math.sqrt(HEAD_DIM)
    group = 2
    per_segment = 2
    for h in range(head_count):
        column = h * HEAD_DIM
        key_h = inbox[:, :, width + column : width + column + HEAD_DIM].reshape(total, HEAD_DIM)
        value_h = inbox[:, :, 2 * width + column : 2 * width + column + HEAD_DIM].reshape(
            total, HEAD_DIM
        )

        def attend_group(g, carry, column=column, key_h=key_h, value_h=value_h):
            first = pl.multiple_of(g * group, group)
            query_block = inbox[pl.ds(first, group), :, column : column + HEAD_DIM].reshape(
                group * rows, HEAD_DIM
            )
            scores = lax.dot_general(
                query_block, key_h, (((1,), (1,)), ((), ())), preferred_element_type=jnp.float32
            ) * score_scale
            scores = jnp.where(key_ok, scores, jnp.float32(-1e30))
            row_top = jnp.max(scores, axis=1, keepdims=True)
            raised = jnp.exp(scores - row_top)
            weights = (raised / jnp.sum(raised, axis=1, keepdims=True)).astype(jnp.bfloat16)
            out = jnp.dot(weights, value_h, preferred_element_type=jnp.float32).astype(jnp.bfloat16)
            heads[pl.ds(first, group), :, column : column + HEAD_DIM] = out.reshape(
                group, rows, HEAD_DIM
            )
            return carry

        for segment in range(cams // group // per_segment):
            lax.fori_loop(segment * per_segment, (segment + 1) * per_segment, attend_group, 0)
            gather.step(next(arrivals))

    for copy in outgoing:
        copy.wait_send()

    def columns(j):
        return attended.at[:, pl.ds(pl.multiple_of(j * width, width), width)]

    own_back = pltpu.make_async_copy(heads.at[me], columns(me), own_sems.at[1])
    own_back.start()
    returning = []
    for d in range(1, cams):
        peer = (me + d) % cams
        copy = pltpu.make_async_remote_copy(
            src_ref=heads.at[peer], dst_ref=columns(me),
            send_sem=back_send.at[d - 1], recv_sem=back_recv.at[d - 1],
            device_id=cam_device(peer), device_id_type=MESH_IDS,
        )
        copy.start()
        returning.append(copy)
    remaining = list(arrivals)
    ready_at = len(ARRIVALS) - 12
    while remaining and remaining[0] < ready_at:
        gather.step(remaining.pop(0))
    for d in range(1, cams):
        source = (me - d + cams) % cams
        pltpu.make_async_remote_copy(
            src_ref=columns(source), dst_ref=columns(source), send_sem=back_send.at[d - 1],
            recv_sem=back_recv.at[d - 1], device_id=cam_device(source), device_id_type=MESH_IDS,
        ).wait_recv()
    own_back.wait()

    acc[...] = jnp.zeros_like(acc)
    shard = w_ref.shape[0]
    col_block = acc.shape[1] // 4
    loads = [0]

    def project(rows_ref, f):
        slot = loads[0] % 2
        loads[0] += 1
        load = pltpu.make_async_copy(rows_ref, wbuf.at[slot], wsems.at[slot])
        load.start()
        load.wait()
        lhs = attended[:, pl.ds(pl.multiple_of(f * shard, shard), shard)]
        for cb in range(4):
            block = pl.ds(cb * col_block, col_block)
            acc[:, block] += jnp.dot(
                lhs, wbuf[slot, :, block], preferred_element_type=jnp.float32
            )

    def project_shard(rel):
        for c in range(CHUNKS):
            gather.partner_arrive(rel, c)
        f = gather.shard_of(rel)
        project(weight_ref.at[pl.ds(pl.multiple_of(f * shard, shard), shard)], f)

    project(w_ref, gather.shard_of((0, 0)))
    last = {rel: max(i for i, (r, _) in enumerate(ARRIVALS) if r == rel) for rel in RELATIVE}
    for rel in sorted(RELATIVE, key=lambda r: last[r]):
        if last[rel] < ready_at:
            project_shard(rel)
    for index in remaining:
        gather.step(index)
        for rel in RELATIVE:
            if last[rel] == index:
                project_shard(rel)
    gather.finish()
    store = pltpu.make_async_copy(acc, proj_ref, own_sems.at[2])
    store.start()
    store.wait()
    for copy in returning:
        copy.wait_send()


def fused(packed, out_weight):
    cams, rows, packed_width = packed.shape
    width = (packed_width - 128) // 3
    shard, cols = out_weight.shape
    fsdp = lax.axis_size("z") * lax.axis_size("y_lo")
    _, projected = pl.pallas_call(
        fused_kernel,
        out_shape=(
            jax.ShapeDtypeStruct((shard * fsdp, cols), out_weight.dtype),
            jax.ShapeDtypeStruct((rows, cols), jnp.float32),
        ),
        in_specs=[pl.BlockSpec(memory_space=pl.ANY), pl.BlockSpec(memory_space=pl.ANY)],
        out_specs=(pl.BlockSpec(memory_space=pl.ANY), pl.BlockSpec(memory_space=pl.ANY)),
        scratch_shapes=[
            pltpu.VMEM((cams, rows, packed_width), packed.dtype),
            pltpu.VMEM((cams, rows, width), packed.dtype),
            pltpu.VMEM((rows, cams * width), packed.dtype),
            pltpu.VMEM((rows, cols), jnp.float32),
            pltpu.VMEM((2, shard, cols), out_weight.dtype),
            pltpu.SemaphoreType.DMA((SENDS,)),
            pltpu.SemaphoreType.DMA((2 * CHUNKS * len(RELATIVE),)),
            pltpu.SemaphoreType.DMA(()),
            pltpu.SemaphoreType.DMA((cams - 1,)),
            pltpu.SemaphoreType.DMA((cams - 1,)),
            pltpu.SemaphoreType.DMA((cams - 1,)),
            pltpu.SemaphoreType.DMA((cams - 1,)),
            pltpu.SemaphoreType.DMA((3,)),
            pltpu.SemaphoreType.DMA((2,)),
        ],
        compiler_params=pltpu.CompilerParams(
            collective_id=0, has_side_effects=True, vmem_limit_bytes=62 * 1024 * 1024
        ),
    )(packed, out_weight)
    return projected


def local(queries, keys, values, out_weight, block_counts, row_mask):
    query_rows = queries[0]
    row_count = query_rows.shape[0]
    cam_count = lax.axis_size(CAM)
    offsets = jnp.arange(row_count, dtype=jnp.int32)
    row_valid = (row_mask[0] == 1) & (offsets // BLOCK < block_counts[0, 0])
    width = query_rows.shape[1] // cam_count

    def by_head(x):
        return x.reshape(row_count, cam_count, width).transpose(1, 0, 2)

    flag = jnp.broadcast_to(
        row_valid.astype(jnp.bfloat16)[None, :, None], (cam_count, row_count, 128)
    )
    packed = jnp.concatenate([by_head(query_rows), by_head(keys[0]), by_head(values[0]), flag], axis=2)
    projected = fused(packed, out_weight)
    result = jnp.where(row_valid[:, None], projected, jnp.float32(0.0)).astype(jnp.bfloat16)
    return result[None]


def solution(mesh):
    sub_mesh = Mesh(mesh.devices.reshape(4, 2, 2, 4, 2), CAM + FSDP)
    in_specs = (
        P(FSDP, CAM, None),
        P(FSDP, CAM, None),
        P(FSDP, CAM, None),
        P(FSDP, None),
        P(FSDP, CAM),
        P(FSDP, CAM),
    )
    out_specs = P(FSDP, CAM, None)
    return jax.shard_map(local, mesh=sub_mesh, in_specs=in_specs, out_specs=out_specs, check_vma=False)
```

```python
import functools
import math

import jax
import jax.numpy as jnp
from jax import lax
from jax.experimental import pallas as pl
from jax.experimental.pallas import tpu as pltpu
from jax.sharding import Mesh
from jax.sharding import PartitionSpec as P

HEAD_DIM = 128
BLOCK = 32

CAM = ("x", "y_hi", "core")
FSDP = ("z", "y_lo")
Y = ("y_hi", "y_lo")


MESH_IDS = pl.DeviceIdType.MESH


RELATIVE = ((-1, 0), (1, 0), (0, 1), (2, 0), (-1, 1), (1, 1), (2, 1))
ROUTES = {
    (0, 0): (("z", 1, (0, 1, 2, 3)), ("z", -1, (0, 1, 2, 3)), ("y", 1, (0, 1)), ("y", -1, (2, 3))),
    (-1, 0): (("z", 1, (0, 1)), ("y", 1, (0, 1)), ("y", -1, (2, 3))),
    (1, 0): (("z", -1, (2, 3)), ("y", 1, (0, 1)), ("y", -1, (2, 3))),
    (0, 1): (),
    (2, 0): (),
    (-1, 1): (("z", 1, (0, 1)),),
    (1, 1): (("z", -1, (2, 3)),),
    (2, 1): (),
}
SOURCES = {
    (-1, 0): (("z", -1),) * 4,
    (1, 0): (("z", 1),) * 4,
    (0, 1): (("y", -1),) * 2 + (("y", 1),) * 2,
    (2, 0): (("z", -1),) * 2 + (("z", 1),) * 2,
    (-1, 1): (("y", -1),) * 2 + (("y", 1),) * 2,
    (1, 1): (("y", -1),) * 2 + (("y", 1),) * 2,
    (2, 1): (("z", -1),) * 2 + (("z", 1),) * 2,
}
ARRIVALS = (
    ((-1, 0), 0), ((1, 0), 0), ((0, 1), 0), ((0, 1), 2),
    ((-1, 0), 1), ((1, 0), 1), ((0, 1), 1), ((0, 1), 3),
    ((-1, 0), 2), ((1, 0), 2), ((-1, 1), 0),
    ((-1, 0), 3), ((1, 0), 3), ((1, 1), 0), ((-1, 1), 2),
    ((2, 0), 0), ((2, 0), 2), ((-1, 1), 1), ((1, 1), 2),
    ((2, 0), 1), ((2, 0), 3), ((1, 1), 1), ((-1, 1), 3),
    ((1, 1), 3), ((2, 1), 0), ((2, 1), 2), ((2, 1), 1),
    ((2, 1), 3),
)
CHUNKS = 4
SENDS = sum(len(c) for routes in ROUTES.values() for _, _, c in routes) + CHUNKS * len(RELATIVE)


class WeightGather:
    def __init__(self, w_ref, out_ref, send, recv, local_sem):
        self.w_ref, self.out_ref, self.send, self.recv = w_ref, out_ref, send, recv
        self.local_sem = local_sem
        self.k = lax.axis_index("core")
        self.z = lax.axis_index("z")
        self.yl = lax.axis_index("y_lo")
        self.y = lax.axis_index("y_hi") * 2 + self.yl
        self.shard = w_ref.shape[0]
        self.half = self.shard // 2
        self.chunk = self.half // CHUNKS
        self.partner = {"core": 1 - self.k}
        self.sent = []

    def device(self, axis, step):
        if axis == "z":
            return {"z": (self.z + step) % 4}
        yy = (self.y + step) % 4
        return {"y_hi": yy // 2, "y_lo": yy % 2}

    def neighbours(self):
        return (self.device("z", 1), self.device("z", -1), self.device("y", 1), self.device("y", -1))

    def shard_of(self, rel):
        dz, flip = rel
        return ((self.z + dz) % 4) * 2 + (self.yl + flip) % 2

    def region(self, rel, kk, c):
        start = self.shard_of(rel) * self.shard + kk * self.half + c * self.chunk
        return self.out_ref.at[pl.ds(pl.multiple_of(start, self.chunk), self.chunk)]

    @staticmethod
    def seen_by(rel, axis, step):
        dz, flip = rel
        if axis == "z":
            return ((dz - step + 1) % 4 - 1, flip)
        return (dz, 1 - flip)

    @staticmethod
    def recv_slot(rel, c, from_partner):
        return (len(RELATIVE) if from_partner else 0) * CHUNKS + RELATIVE.index(rel) * CHUNKS + c

    def copy(self, src, dst, slot, dev):
        copy = pltpu.make_async_remote_copy(
            src_ref=src, dst_ref=dst, send_sem=self.send.at[len(self.sent)],
            recv_sem=self.recv.at[slot], device_id=dev, device_id_type=MESH_IDS,
        )
        copy.start()
        self.sent.append(copy)

    def start(self):
        k, shard, half, chunk = self.k, self.shard, self.half, self.chunk
        own = self.shard_of((0, 0))
        self.local_copy = pltpu.make_async_copy(
            self.w_ref, self.out_ref.at[pl.ds(pl.multiple_of(own * shard, shard), shard)],
            self.local_sem,
        )
        self.local_copy.start()
        for axis, step, chunks in ROUTES[(0, 0)]:
            for c in chunks:
                src = self.w_ref.at[pl.ds(pl.multiple_of(k * half + c * chunk, chunk), chunk)]
                slot = self.recv_slot(self.seen_by((0, 0), axis, step), c, False)
                self.copy(src, self.region((0, 0), k, c), slot, self.device(axis, step))

    def arrive(self, rel, kk, c, dev, from_partner):
        piece = self.region(rel, kk, c)
        pltpu.make_async_remote_copy(
            src_ref=piece, dst_ref=piece, send_sem=self.send.at[0],
            recv_sem=self.recv.at[self.recv_slot(rel, c, from_partner)],
            device_id=dev, device_id_type=MESH_IDS,
        ).wait_recv()

    def step(self, index):
        rel, c = ARRIVALS[index]
        axis, step = SOURCES[rel][c]
        self.arrive(rel, self.k, c, self.device(axis, step), False)
        piece = self.region(rel, self.k, c)
        for axis, step, chunks in ROUTES[rel]:
            if c in chunks:
                slot = self.recv_slot(self.seen_by(rel, axis, step), c, False)
                self.copy(piece, piece, slot, self.device(axis, step))
        self.copy(piece, piece, self.recv_slot(rel, c, True), self.partner)

    def finish(self):
        for rel in RELATIVE:
            for c in range(CHUNKS):
                self.arrive(rel, 1 - self.k, c, self.partner, True)
        assert len(self.sent) == SENDS
        for copy in self.sent:
            copy.wait_send()
        self.local_copy.wait()


def cam_device(j):
    return {"x": j // 4, "y_hi": (j // 2) % 2, "core": j % 2}


def fused_kernel(
    q_ref, k_ref, v_ref, flag_ref, w_ref, weight_ref, attended_ref,
    inbox, heads, send, recv, local_sem, a2a_send, a2a_recv, back_send, back_recv, own_sems,
):
    cams = inbox.shape[0]
    rows = inbox.shape[1]
    width = heads.shape[2]
    head_count = width // HEAD_DIM
    sources = (q_ref, k_ref, v_ref, flag_ref)
    me = (lax.axis_index("x") * 2 + lax.axis_index("y_hi")) * 2 + lax.axis_index("core")
    gather = WeightGather(w_ref, weight_ref, send, recv, local_sem)

    barrier = pltpu.get_barrier_semaphore()
    peers = [cam_device((me + d) % cams) for d in range(1, cams)]
    for dev in peers + list(gather.neighbours()):
        pl.semaphore_signal(barrier, inc=1, device_id=dev, device_id_type=MESH_IDS)
    pl.semaphore_wait(barrier, len(peers) + 4)

    gather.start()
    def block(ref, part, j):
        if part == 3:
            return ref
        return ref.at[:, pl.ds(pl.multiple_of(j * width, width), width)]

    def slot_of(ref_inbox, part, j):
        return ref_inbox.at[j, :, pl.ds(part * width, width if part < 3 else 128)]

    own_in = []
    for part, ref in enumerate(sources):
        copy = pltpu.make_async_copy(block(ref, part, me), slot_of(inbox, part, me), own_sems.at[part])
        copy.start()
        own_in.append(copy)
    outgoing = []
    for d in range(1, cams):
        peer = (me + d) % cams
        for part, ref in enumerate(sources):
            copy = pltpu.make_async_remote_copy(
                src_ref=block(ref, part, peer), dst_ref=slot_of(inbox, part, me),
                send_sem=a2a_send.at[4 * (d - 1) + part], recv_sem=a2a_recv.at[4 * (d - 1) + part],
                device_id=cam_device(peer), device_id_type=MESH_IDS,
            )
            copy.start()
            outgoing.append(copy)

    arrivals = iter(range(len(ARRIVALS)))
    for _ in range(4):
        gather.step(next(arrivals))
    for copy in own_in:
        copy.wait()
    for d in range(1, cams):
        source = (me - d + cams) % cams
        for part in range(len(sources)):
            landing = slot_of(inbox, part, source)
            pltpu.make_async_remote_copy(
                src_ref=landing, dst_ref=landing, send_sem=a2a_send.at[4 * (d - 1) + part],
                recv_sem=a2a_recv.at[4 * (d - 1) + part], device_id=cam_device(source),
                device_id_type=MESH_IDS,
            ).wait_recv()

    total = cams * rows
    flags = inbox[:, :, 3 * width : 3 * width + 128].reshape(total, 128)
    counted = lax.dot_general(
        jnp.ones((8, 128), flags.dtype), flags, (((1,), (1,)), ((), ())),
        preferred_element_type=jnp.float32,
    )
    key_ok = counted[0:1, :] > 64.0
    score_scale = 1.0 / math.sqrt(HEAD_DIM)
    group = 2
    per_segment = 2
    for h in range(head_count):
        column = h * HEAD_DIM
        key_h = inbox[:, :, width + column : width + column + HEAD_DIM].reshape(total, HEAD_DIM)
        value_h = inbox[:, :, 2 * width + column : 2 * width + column + HEAD_DIM].reshape(
            total, HEAD_DIM
        )

        def attend_group(g, carry, column=column, key_h=key_h, value_h=value_h):
            first = pl.multiple_of(g * group, group)
            query_block = inbox[pl.ds(first, group), :, column : column + HEAD_DIM].reshape(
                group * rows, HEAD_DIM
            )
            scores = lax.dot_general(
                query_block, key_h, (((1,), (1,)), ((), ())), preferred_element_type=jnp.float32
            ) * score_scale
            scores = jnp.where(key_ok, scores, jnp.float32(-1e30))
            row_top = jnp.max(scores, axis=1, keepdims=True)
            raised = jnp.exp(scores - row_top)
            weights = (raised / jnp.sum(raised, axis=1, keepdims=True)).astype(jnp.bfloat16)
            out = jnp.dot(weights, value_h, preferred_element_type=jnp.float32).astype(jnp.bfloat16)
            heads[pl.ds(first, group), :, column : column + HEAD_DIM] = out.reshape(
                group, rows, HEAD_DIM
            )
            return carry

        for segment in range(cams // group // per_segment):
            lax.fori_loop(segment * per_segment, (segment + 1) * per_segment, attend_group, 0)
            gather.step(next(arrivals))

    for copy in outgoing:
        copy.wait_send()
    own_back = pltpu.make_async_copy(
        heads.at[me], attended_ref.at[:, pl.ds(pl.multiple_of(me * width, width), width)],
        own_sems.at[4],
    )
    own_back.start()
    returning = []
    for d in range(1, cams):
        peer = (me + d) % cams
        copy = pltpu.make_async_remote_copy(
            src_ref=heads.at[peer],
            dst_ref=attended_ref.at[:, pl.ds(pl.multiple_of(me * width, width), width)],
            send_sem=back_send.at[d - 1], recv_sem=back_recv.at[d - 1],
            device_id=cam_device(peer), device_id_type=MESH_IDS,
        )
        copy.start()
        returning.append(copy)
    for index in arrivals:
        gather.step(index)
    gather.finish()
    for d in range(1, cams):
        source = (me - d + cams) % cams
        region = attended_ref.at[:, pl.ds(pl.multiple_of(source * width, width), width)]
        pltpu.make_async_remote_copy(
            src_ref=region, dst_ref=region, send_sem=back_send.at[d - 1],
            recv_sem=back_recv.at[d - 1], device_id=cam_device(source), device_id_type=MESH_IDS,
        ).wait_recv()
    for copy in returning:
        copy.wait_send()
    own_back.wait()


def fused(query_rows, key_rows, value_rows, flag, out_weight):
    rows, features = query_rows.shape
    cams = lax.axis_size(CAM)
    width = features // cams
    shard, cols = out_weight.shape
    fsdp = lax.axis_size("z") * lax.axis_size("y_lo")
    any_spec = pl.BlockSpec(memory_space=pl.ANY)
    return pl.pallas_call(
        fused_kernel,
        out_shape=(
            jax.ShapeDtypeStruct((shard * fsdp, cols), out_weight.dtype),
            jax.ShapeDtypeStruct((rows, features), query_rows.dtype),
        ),
        in_specs=[any_spec] * 5,
        out_specs=(any_spec, any_spec),
        scratch_shapes=[
            pltpu.VMEM((cams, rows, 3 * width + 128), query_rows.dtype),
            pltpu.VMEM((cams, rows, width), query_rows.dtype),
            pltpu.SemaphoreType.DMA((SENDS,)),
            pltpu.SemaphoreType.DMA((2 * CHUNKS * len(RELATIVE),)),
            pltpu.SemaphoreType.DMA(()),
            pltpu.SemaphoreType.DMA((4 * (cams - 1),)),
            pltpu.SemaphoreType.DMA((4 * (cams - 1),)),
            pltpu.SemaphoreType.DMA((cams - 1,)),
            pltpu.SemaphoreType.DMA((cams - 1,)),
            pltpu.SemaphoreType.DMA((5,)),
        ],
        compiler_params=pltpu.CompilerParams(
            collective_id=0, has_side_effects=True, vmem_limit_bytes=60 * 1024 * 1024
        ),
    )(query_rows, key_rows, value_rows, flag, out_weight)


def local(queries, keys, values, out_weight, block_counts, row_mask):
    query_rows = queries[0]
    row_count = query_rows.shape[0]
    cam_count = lax.axis_size(CAM)
    offsets = jnp.arange(row_count, dtype=jnp.int32)
    row_valid = (row_mask[0] == 1) & (offsets // BLOCK < block_counts[0, 0])

    flag = jnp.broadcast_to(row_valid.astype(jnp.bfloat16)[:, None], (row_count, 128))
    weight_all, attended = fused(query_rows, keys[0], values[0], flag, out_weight)
    projected = jnp.dot(attended, weight_all, preferred_element_type=jnp.float32)
    result = jnp.where(row_valid[:, None], projected, jnp.float32(0.0)).astype(jnp.bfloat16)
    return result[None]


def solution(mesh):
    sub_mesh = Mesh(mesh.devices.reshape(4, 2, 2, 4, 2), CAM + FSDP)
    in_specs = (
        P(FSDP, CAM, None),
        P(FSDP, CAM, None),
        P(FSDP, CAM, None),
        P(FSDP, None),
        P(FSDP, CAM),
        P(FSDP, CAM),
    )
    out_specs = P(FSDP, CAM, None)
    return jax.shard_map(local, mesh=sub_mesh, in_specs=in_specs, out_specs=out_specs, check_vma=False)
```

```python
import functools
import math

import jax
import jax.numpy as jnp
from jax import lax
from jax.experimental import pallas as pl
from jax.experimental.pallas import tpu as pltpu
from jax.sharding import Mesh
from jax.sharding import PartitionSpec as P

HEAD_DIM = 128
BLOCK = 32

CAM = ("x", "y_hi", "core")
FSDP = ("z", "y_lo")
Y = ("y_hi", "y_lo")


MESH_IDS = pl.DeviceIdType.MESH


RELATIVE = ((-1, 0), (1, 0), (0, 1), (2, 0), (-1, 1), (1, 1), (2, 1))
ROUTES = {
    (0, 0): (("z", 1, (0, 1, 2, 3)), ("z", -1, (0, 1, 2, 3)), ("y", 1, (0, 1)), ("y", -1, (2, 3))),
    (-1, 0): (("z", 1, (0, 1)), ("y", -1, (2, 3))),
    (1, 0): (("z", -1, (2, 3)), ("y", 1, (0, 1))),
    (0, 1): (("z", 1, (0, 1)), ("z", -1, (2, 3))),
    (2, 0): (),
    (-1, 1): (("z", 1, (0, 1)),),
    (1, 1): (("z", -1, (2, 3)),),
    (2, 1): (),
}
SOURCES = {
    (-1, 0): (("z", -1),) * 4,
    (1, 0): (("z", 1),) * 4,
    (0, 1): (("y", -1),) * 2 + (("y", 1),) * 2,
    (2, 0): (("z", -1),) * 2 + (("z", 1),) * 2,
    (-1, 1): (("z", -1),) * 2 + (("y", 1),) * 2,
    (1, 1): (("y", -1),) * 2 + (("z", 1),) * 2,
    (2, 1): (("z", -1),) * 2 + (("z", 1),) * 2,
}
ARRIVALS = (
    ((-1, 0), 0), ((1, 0), 0), ((0, 1), 0), ((0, 1), 2),
    ((-1, 0), 1), ((1, 0), 1), ((0, 1), 1), ((0, 1), 3),
    ((-1, 0), 2), ((1, 0), 2), ((1, 1), 0), ((-1, 1), 2),
    ((-1, 0), 3), ((1, 0), 3), ((1, 1), 1), ((-1, 1), 3),
    ((2, 0), 0), ((2, 0), 2), ((-1, 1), 0), ((1, 1), 2),
    ((2, 0), 1), ((2, 0), 3), ((-1, 1), 1), ((1, 1), 3),
    ((2, 1), 0), ((2, 1), 2), ((2, 1), 1), ((2, 1), 3),
)
CHUNKS = 4
SENDS = sum(len(c) for routes in ROUTES.values() for _, _, c in routes) + CHUNKS * len(RELATIVE)


class WeightGather:
    def __init__(self, w_ref, out_ref, send, recv, local_sem):
        self.w_ref, self.out_ref, self.send, self.recv = w_ref, out_ref, send, recv
        self.local_sem = local_sem
        self.k = lax.axis_index("core")
        self.z = lax.axis_index("z")
        self.yl = lax.axis_index("y_lo")
        self.y = lax.axis_index("y_hi") * 2 + self.yl
        self.shard = w_ref.shape[0]
        self.half = self.shard // 2
        self.chunk = self.half // CHUNKS
        self.partner = {"core": 1 - self.k}
        self.sent = []

    def device(self, axis, step):
        if axis == "z":
            return {"z": (self.z + step) % 4}
        yy = (self.y + step) % 4
        return {"y_hi": yy // 2, "y_lo": yy % 2}

    def neighbours(self):
        return (self.device("z", 1), self.device("z", -1), self.device("y", 1), self.device("y", -1))

    def shard_of(self, rel):
        dz, flip = rel
        return ((self.z + dz) % 4) * 2 + (self.yl + flip) % 2

    def region(self, rel, kk, c):
        start = self.shard_of(rel) * self.shard + kk * self.half + c * self.chunk
        return self.out_ref.at[pl.ds(pl.multiple_of(start, self.chunk), self.chunk)]

    @staticmethod
    def seen_by(rel, axis, step):
        dz, flip = rel
        if axis == "z":
            return ((dz - step + 1) % 4 - 1, flip)
        return (dz, 1 - flip)

    @staticmethod
    def recv_slot(rel, c, from_partner):
        return (len(RELATIVE) if from_partner else 0) * CHUNKS + RELATIVE.index(rel) * CHUNKS + c

    def copy(self, src, dst, slot, dev):
        copy = pltpu.make_async_remote_copy(
            src_ref=src, dst_ref=dst, send_sem=self.send.at[len(self.sent)],
            recv_sem=self.recv.at[slot], device_id=dev, device_id_type=MESH_IDS,
        )
        copy.start()
        self.sent.append(copy)

    def start(self):
        k, shard, half, chunk = self.k, self.shard, self.half, self.chunk
        own = self.shard_of((0, 0))
        self.local_copy = pltpu.make_async_copy(
            self.w_ref, self.out_ref.at[pl.ds(pl.multiple_of(own * shard, shard), shard)],
            self.local_sem,
        )
        self.local_copy.start()
        for axis, step, chunks in ROUTES[(0, 0)]:
            for c in chunks:
                src = self.w_ref.at[pl.ds(pl.multiple_of(k * half + c * chunk, chunk), chunk)]
                slot = self.recv_slot(self.seen_by((0, 0), axis, step), c, False)
                self.copy(src, self.region((0, 0), k, c), slot, self.device(axis, step))

    def arrive(self, rel, kk, c, dev, from_partner):
        piece = self.region(rel, kk, c)
        pltpu.make_async_remote_copy(
            src_ref=piece, dst_ref=piece, send_sem=self.send.at[0],
            recv_sem=self.recv.at[self.recv_slot(rel, c, from_partner)],
            device_id=dev, device_id_type=MESH_IDS,
        ).wait_recv()

    def step(self, index):
        rel, c = ARRIVALS[index]
        axis, step = SOURCES[rel][c]
        self.arrive(rel, self.k, c, self.device(axis, step), False)
        piece = self.region(rel, self.k, c)
        for axis, step, chunks in ROUTES[rel]:
            if c in chunks:
                slot = self.recv_slot(self.seen_by(rel, axis, step), c, False)
                self.copy(piece, piece, slot, self.device(axis, step))
        self.copy(piece, piece, self.recv_slot(rel, c, True), self.partner)

    def finish(self):
        for rel in RELATIVE:
            for c in range(CHUNKS):
                self.arrive(rel, 1 - self.k, c, self.partner, True)
        assert len(self.sent) == SENDS
        for copy in self.sent:
            copy.wait_send()
        self.local_copy.wait()


def cam_device(j):
    return {"x": j // 4, "y_hi": (j // 2) % 2, "core": j % 2}


def fused_kernel(
    q_ref, k_ref, v_ref, flag_ref, w_ref, weight_ref, attended_ref,
    inbox, heads, send, recv, local_sem, a2a_send, a2a_recv, back_send, back_recv, own_sems,
):
    cams = inbox.shape[0]
    rows = inbox.shape[1]
    width = heads.shape[2]
    head_count = width // HEAD_DIM
    sources = (q_ref, k_ref, v_ref, flag_ref)
    me = (lax.axis_index("x") * 2 + lax.axis_index("y_hi")) * 2 + lax.axis_index("core")
    gather = WeightGather(w_ref, weight_ref, send, recv, local_sem)

    barrier = pltpu.get_barrier_semaphore()
    peers = [cam_device((me + d) % cams) for d in range(1, cams)]
    for dev in peers + list(gather.neighbours()):
        pl.semaphore_signal(barrier, inc=1, device_id=dev, device_id_type=MESH_IDS)
    pl.semaphore_wait(barrier, len(peers) + 4)

    gather.start()
    def block(ref, part, j):
        if part == 3:
            return ref
        return ref.at[:, pl.ds(pl.multiple_of(j * width, width), width)]

    def slot_of(ref_inbox, part, j):
        return ref_inbox.at[j, :, pl.ds(part * width, width if part < 3 else 128)]

    own_in = []
    for part, ref in enumerate(sources):
        copy = pltpu.make_async_copy(block(ref, part, me), slot_of(inbox, part, me), own_sems.at[part])
        copy.start()
        own_in.append(copy)
    outgoing = []
    for d in range(1, cams):
        peer = (me + d) % cams
        for part, ref in enumerate(sources):
            copy = pltpu.make_async_remote_copy(
                src_ref=block(ref, part, peer), dst_ref=slot_of(inbox, part, me),
                send_sem=a2a_send.at[4 * (d - 1) + part], recv_sem=a2a_recv.at[4 * (d - 1) + part],
                device_id=cam_device(peer), device_id_type=MESH_IDS,
            )
            copy.start()
            outgoing.append(copy)

    arrivals = iter(range(len(ARRIVALS)))
    for _ in range(4):
        gather.step(next(arrivals))
    for copy in own_in:
        copy.wait()
    for d in range(1, cams):
        source = (me - d + cams) % cams
        for part in range(len(sources)):
            landing = slot_of(inbox, part, source)
            pltpu.make_async_remote_copy(
                src_ref=landing, dst_ref=landing, send_sem=a2a_send.at[4 * (d - 1) + part],
                recv_sem=a2a_recv.at[4 * (d - 1) + part], device_id=cam_device(source),
                device_id_type=MESH_IDS,
            ).wait_recv()

    total = cams * rows
    flags = inbox[:, :, 3 * width : 3 * width + 128].reshape(total, 128)
    counted = lax.dot_general(
        jnp.ones((8, 128), flags.dtype), flags, (((1,), (1,)), ((), ())),
        preferred_element_type=jnp.float32,
    )
    key_ok = counted[0:1, :] > 64.0
    score_scale = 1.0 / math.sqrt(HEAD_DIM)
    group = 2
    per_segment = 2
    for h in range(head_count):
        column = h * HEAD_DIM
        key_h = inbox[:, :, width + column : width + column + HEAD_DIM].reshape(total, HEAD_DIM)
        value_h = inbox[:, :, 2 * width + column : 2 * width + column + HEAD_DIM].reshape(
            total, HEAD_DIM
        )

        def attend_group(g, carry, column=column, key_h=key_h, value_h=value_h):
            first = pl.multiple_of(g * group, group)
            query_block = inbox[pl.ds(first, group), :, column : column + HEAD_DIM].reshape(
                group * rows, HEAD_DIM
            )
            scores = lax.dot_general(
                query_block, key_h, (((1,), (1,)), ((), ())), preferred_element_type=jnp.float32
            ) * score_scale
            scores = jnp.where(key_ok, scores, jnp.float32(-1e30))
            row_top = jnp.max(scores, axis=1, keepdims=True)
            raised = jnp.exp(scores - row_top)
            weights = (raised / jnp.sum(raised, axis=1, keepdims=True)).astype(jnp.bfloat16)
            out = jnp.dot(weights, value_h, preferred_element_type=jnp.float32).astype(jnp.bfloat16)
            heads[pl.ds(first, group), :, column : column + HEAD_DIM] = out.reshape(
                group, rows, HEAD_DIM
            )
            return carry

        for segment in range(cams // group // per_segment):
            lax.fori_loop(segment * per_segment, (segment + 1) * per_segment, attend_group, 0)
            gather.step(next(arrivals))

    for copy in outgoing:
        copy.wait_send()
    own_back = pltpu.make_async_copy(
        heads.at[me], attended_ref.at[:, pl.ds(pl.multiple_of(me * width, width), width)],
        own_sems.at[4],
    )
    own_back.start()
    returning = []
    for d in range(1, cams):
        peer = (me + d) % cams
        copy = pltpu.make_async_remote_copy(
            src_ref=heads.at[peer],
            dst_ref=attended_ref.at[:, pl.ds(pl.multiple_of(me * width, width), width)],
            send_sem=back_send.at[d - 1], recv_sem=back_recv.at[d - 1],
            device_id=cam_device(peer), device_id_type=MESH_IDS,
        )
        copy.start()
        returning.append(copy)
    for index in arrivals:
        gather.step(index)
    gather.finish()
    for d in range(1, cams):
        source = (me - d + cams) % cams
        region = attended_ref.at[:, pl.ds(pl.multiple_of(source * width, width), width)]
        pltpu.make_async_remote_copy(
            src_ref=region, dst_ref=region, send_sem=back_send.at[d - 1],
            recv_sem=back_recv.at[d - 1], device_id=cam_device(source), device_id_type=MESH_IDS,
        ).wait_recv()
    for copy in returning:
        copy.wait_send()
    own_back.wait()


def fused(query_rows, key_rows, value_rows, flag, out_weight):
    rows, features = query_rows.shape
    cams = lax.axis_size(CAM)
    width = features // cams
    shard, cols = out_weight.shape
    fsdp = lax.axis_size("z") * lax.axis_size("y_lo")
    any_spec = pl.BlockSpec(memory_space=pl.ANY)
    return pl.pallas_call(
        fused_kernel,
        out_shape=(
            jax.ShapeDtypeStruct((shard * fsdp, cols), out_weight.dtype),
            jax.ShapeDtypeStruct((rows, features), query_rows.dtype),
        ),
        in_specs=[any_spec] * 5,
        out_specs=(any_spec, any_spec),
        scratch_shapes=[
            pltpu.VMEM((cams, rows, 3 * width + 128), query_rows.dtype),
            pltpu.VMEM((cams, rows, width), query_rows.dtype),
            pltpu.SemaphoreType.DMA((SENDS,)),
            pltpu.SemaphoreType.DMA((2 * CHUNKS * len(RELATIVE),)),
            pltpu.SemaphoreType.DMA(()),
            pltpu.SemaphoreType.DMA((4 * (cams - 1),)),
            pltpu.SemaphoreType.DMA((4 * (cams - 1),)),
            pltpu.SemaphoreType.DMA((cams - 1,)),
            pltpu.SemaphoreType.DMA((cams - 1,)),
            pltpu.SemaphoreType.DMA((5,)),
        ],
        compiler_params=pltpu.CompilerParams(
            collective_id=0, has_side_effects=True, vmem_limit_bytes=60 * 1024 * 1024
        ),
    )(query_rows, key_rows, value_rows, flag, out_weight)


def local(queries, keys, values, out_weight, block_counts, row_mask):
    query_rows = queries[0]
    row_count = query_rows.shape[0]
    cam_count = lax.axis_size(CAM)
    offsets = jnp.arange(row_count, dtype=jnp.int32)
    row_valid = (row_mask[0] == 1) & (offsets // BLOCK < block_counts[0, 0])

    flag = jnp.broadcast_to(row_valid.astype(jnp.bfloat16)[:, None], (row_count, 128))
    weight_all, attended = fused(query_rows, keys[0], values[0], flag, out_weight)
    projected = jnp.dot(attended, weight_all, preferred_element_type=jnp.float32)
    result = jnp.where(row_valid[:, None], projected, jnp.float32(0.0)).astype(jnp.bfloat16)
    return result[None]


def solution(mesh):
    sub_mesh = Mesh(mesh.devices.reshape(4, 2, 2, 4, 2), CAM + FSDP)
    in_specs = (
        P(FSDP, CAM, None),
        P(FSDP, CAM, None),
        P(FSDP, CAM, None),
        P(FSDP, None),
        P(FSDP, CAM),
        P(FSDP, CAM),
    )
    out_specs = P(FSDP, CAM, None)
    return jax.shard_map(local, mesh=sub_mesh, in_specs=in_specs, out_specs=out_specs, check_vma=False)
```

```python
import functools
import math

import jax
import jax.numpy as jnp
from jax import lax
from jax.experimental import pallas as pl
from jax.experimental.pallas import tpu as pltpu
from jax.sharding import Mesh
from jax.sharding import PartitionSpec as P

HEAD_DIM = 128
BLOCK = 32

CAM = ("x", "y_hi", "core")
FSDP = ("z", "y_lo")
Y = ("y_hi", "y_lo")


MESH_IDS = pl.DeviceIdType.MESH


RELATIVE = ((-1, 0), (1, 0), (0, 1), (2, 0), (-1, 1), (1, 1), (2, 1))
ROUTES = {
    (0, 0): (("z", 1, (0, 1, 2, 3)), ("z", -1, (0, 1, 2, 3)), ("y", 1, (0, 1)), ("y", -1, (2, 3))),
    (-1, 0): (("z", 1, (0, 1)), ("y", 1, (1,)), ("y", -1, (2, 3))),
    (1, 0): (("z", -1, (2, 3)), ("y", 1, (0, 1)), ("y", -1, (2,))),
    (0, 1): (("z", 1, (0,)), ("z", -1, (3,))),
    (2, 0): (),
    (-1, 1): (("z", 1, (0, 1)),),
    (1, 1): (("z", -1, (2, 3)),),
    (2, 1): (),
}
SOURCES = {
    (-1, 0): (("z", -1),) * 4,
    (1, 0): (("z", 1),) * 4,
    (0, 1): (("y", -1),) * 2 + (("y", 1),) * 2,
    (2, 0): (("z", -1),) * 2 + (("z", 1),) * 2,
    (-1, 1): (("z", -1), ("y", -1), ("y", 1), ("y", 1)),
    (1, 1): (("y", -1), ("y", -1), ("y", 1), ("z", 1)),
    (2, 1): (("z", -1),) * 2 + (("z", 1),) * 2,
}
ARRIVALS = (
    ((-1, 0), 0), ((1, 0), 0), ((0, 1), 0), ((0, 1), 2),
    ((-1, 0), 1), ((1, 0), 1), ((0, 1), 1), ((0, 1), 3),
    ((-1, 0), 2), ((1, 0), 2), ((1, 1), 0), ((-1, 1), 2),
    ((-1, 0), 3), ((1, 0), 3), ((1, 1), 1), ((-1, 1), 1), ((1, 1), 2), ((-1, 1), 3),
    ((2, 0), 0), ((2, 0), 2), ((-1, 1), 0), ((1, 1), 3),
    ((2, 0), 1), ((2, 0), 3),
    ((2, 1), 0), ((2, 1), 2), ((2, 1), 1), ((2, 1), 3),
)
CHUNKS = 4
SENDS = sum(len(c) for routes in ROUTES.values() for _, _, c in routes) + CHUNKS * len(RELATIVE)


class WeightGather:
    def __init__(self, w_ref, out_ref, send, recv, local_sem):
        self.w_ref, self.out_ref, self.send, self.recv = w_ref, out_ref, send, recv
        self.local_sem = local_sem
        self.k = lax.axis_index("core")
        self.z = lax.axis_index("z")
        self.yl = lax.axis_index("y_lo")
        self.y = lax.axis_index("y_hi") * 2 + self.yl
        self.shard = w_ref.shape[0]
        self.half = self.shard // 2
        self.chunk = self.half // CHUNKS
        self.partner = {"core": 1 - self.k}
        self.sent = []

    def device(self, axis, step):
        if axis == "z":
            return {"z": (self.z + step) % 4}
        yy = (self.y + step) % 4
        return {"y_hi": yy // 2, "y_lo": yy % 2}

    def neighbours(self):
        return (self.device("z", 1), self.device("z", -1), self.device("y", 1), self.device("y", -1))

    def shard_of(self, rel):
        dz, flip = rel
        return ((self.z + dz) % 4) * 2 + (self.yl + flip) % 2

    def region(self, rel, kk, c):
        start = self.shard_of(rel) * self.shard + kk * self.half + c * self.chunk
        return self.out_ref.at[pl.ds(pl.multiple_of(start, self.chunk), self.chunk)]

    @staticmethod
    def seen_by(rel, axis, step):
        dz, flip = rel
        if axis == "z":
            return ((dz - step + 1) % 4 - 1, flip)
        return (dz, 1 - flip)

    @staticmethod
    def recv_slot(rel, c, from_partner):
        return (len(RELATIVE) if from_partner else 0) * CHUNKS + RELATIVE.index(rel) * CHUNKS + c

    def copy(self, src, dst, slot, dev):
        copy = pltpu.make_async_remote_copy(
            src_ref=src, dst_ref=dst, send_sem=self.send.at[len(self.sent)],
            recv_sem=self.recv.at[slot], device_id=dev, device_id_type=MESH_IDS,
        )
        copy.start()
        self.sent.append(copy)

    def start(self):
        k, shard, half, chunk = self.k, self.shard, self.half, self.chunk
        own = self.shard_of((0, 0))
        self.local_copy = pltpu.make_async_copy(
            self.w_ref, self.out_ref.at[pl.ds(pl.multiple_of(own * shard, shard), shard)],
            self.local_sem,
        )
        self.local_copy.start()
        for axis, step, chunks in ROUTES[(0, 0)]:
            for c in chunks:
                src = self.w_ref.at[pl.ds(pl.multiple_of(k * half + c * chunk, chunk), chunk)]
                slot = self.recv_slot(self.seen_by((0, 0), axis, step), c, False)
                self.copy(src, self.region((0, 0), k, c), slot, self.device(axis, step))

    def arrive(self, rel, kk, c, dev, from_partner):
        piece = self.region(rel, kk, c)
        pltpu.make_async_remote_copy(
            src_ref=piece, dst_ref=piece, send_sem=self.send.at[0],
            recv_sem=self.recv.at[self.recv_slot(rel, c, from_partner)],
            device_id=dev, device_id_type=MESH_IDS,
        ).wait_recv()

    def step(self, index):
        rel, c = ARRIVALS[index]
        axis, step = SOURCES[rel][c]
        self.arrive(rel, self.k, c, self.device(axis, step), False)
        piece = self.region(rel, self.k, c)
        for axis, step, chunks in ROUTES[rel]:
            if c in chunks:
                slot = self.recv_slot(self.seen_by(rel, axis, step), c, False)
                self.copy(piece, piece, slot, self.device(axis, step))
        self.copy(piece, piece, self.recv_slot(rel, c, True), self.partner)

    def finish(self):
        for rel in RELATIVE:
            for c in range(CHUNKS):
                self.arrive(rel, 1 - self.k, c, self.partner, True)
        assert len(self.sent) == SENDS
        for copy in self.sent:
            copy.wait_send()
        self.local_copy.wait()


def cam_device(j):
    return {"x": j // 4, "y_hi": (j // 2) % 2, "core": j % 2}


def fused_kernel(
    q_ref, k_ref, v_ref, flag_ref, w_ref, weight_ref, attended_ref,
    inbox, heads, send, recv, local_sem, a2a_send, a2a_recv, back_send, back_recv, own_sems,
):
    cams = inbox.shape[0]
    rows = inbox.shape[1]
    width = heads.shape[2]
    head_count = width // HEAD_DIM
    sources = (q_ref, k_ref, v_ref, flag_ref)
    me = (lax.axis_index("x") * 2 + lax.axis_index("y_hi")) * 2 + lax.axis_index("core")
    gather = WeightGather(w_ref, weight_ref, send, recv, local_sem)

    barrier = pltpu.get_barrier_semaphore()
    peers = [cam_device((me + d) % cams) for d in range(1, cams)]
    for dev in peers + list(gather.neighbours()):
        pl.semaphore_signal(barrier, inc=1, device_id=dev, device_id_type=MESH_IDS)
    pl.semaphore_wait(barrier, len(peers) + 4)

    gather.start()
    def block(ref, part, j):
        if part == 3:
            return ref
        return ref.at[:, pl.ds(pl.multiple_of(j * width, width), width)]

    def slot_of(ref_inbox, part, j):
        return ref_inbox.at[j, :, pl.ds(part * width, width if part < 3 else 128)]

    own_in = []
    for part, ref in enumerate(sources):
        copy = pltpu.make_async_copy(block(ref, part, me), slot_of(inbox, part, me), own_sems.at[part])
        copy.start()
        own_in.append(copy)
    outgoing = []
    for d in range(1, cams):
        peer = (me + d) % cams
        for part, ref in enumerate(sources):
            copy = pltpu.make_async_remote_copy(
                src_ref=block(ref, part, peer), dst_ref=slot_of(inbox, part, me),
                send_sem=a2a_send.at[4 * (d - 1) + part], recv_sem=a2a_recv.at[4 * (d - 1) + part],
                device_id=cam_device(peer), device_id_type=MESH_IDS,
            )
            copy.start()
            outgoing.append(copy)

    arrivals = iter(range(len(ARRIVALS)))
    for _ in range(4):
        gather.step(next(arrivals))
    for copy in own_in:
        copy.wait()
    for d in range(1, cams):
        source = (me - d + cams) % cams
        for part in range(len(sources)):
            landing = slot_of(inbox, part, source)
            pltpu.make_async_remote_copy(
                src_ref=landing, dst_ref=landing, send_sem=a2a_send.at[4 * (d - 1) + part],
                recv_sem=a2a_recv.at[4 * (d - 1) + part], device_id=cam_device(source),
                device_id_type=MESH_IDS,
            ).wait_recv()

    total = cams * rows
    flags = inbox[:, :, 3 * width : 3 * width + 128].reshape(total, 128)
    counted = lax.dot_general(
        jnp.ones((8, 128), flags.dtype), flags, (((1,), (1,)), ((), ())),
        preferred_element_type=jnp.float32,
    )
    key_ok = counted[0:1, :] > 64.0
    score_scale = 1.0 / math.sqrt(HEAD_DIM)
    group = 2
    per_segment = 2
    for h in range(head_count):
        column = h * HEAD_DIM
        key_h = inbox[:, :, width + column : width + column + HEAD_DIM].reshape(total, HEAD_DIM)
        value_h = inbox[:, :, 2 * width + column : 2 * width + column + HEAD_DIM].reshape(
            total, HEAD_DIM
        )

        def attend_group(g, carry, column=column, key_h=key_h, value_h=value_h):
            first = pl.multiple_of(g * group, group)
            query_block = inbox[pl.ds(first, group), :, column : column + HEAD_DIM].reshape(
                group * rows, HEAD_DIM
            )
            scores = lax.dot_general(
                query_block, key_h, (((1,), (1,)), ((), ())), preferred_element_type=jnp.float32
            ) * score_scale
            scores = jnp.where(key_ok, scores, jnp.float32(-1e30))
            row_top = jnp.max(scores, axis=1, keepdims=True)
            raised = jnp.exp(scores - row_top)
            weights = (raised / jnp.sum(raised, axis=1, keepdims=True)).astype(jnp.bfloat16)
            out = jnp.dot(weights, value_h, preferred_element_type=jnp.float32).astype(jnp.bfloat16)
            heads[pl.ds(first, group), :, column : column + HEAD_DIM] = out.reshape(
                group, rows, HEAD_DIM
            )
            return carry

        for segment in range(cams // group // per_segment):
            lax.fori_loop(segment * per_segment, (segment + 1) * per_segment, attend_group, 0)
            gather.step(next(arrivals))

    for copy in outgoing:
        copy.wait_send()
    own_back = pltpu.make_async_copy(
        heads.at[me], attended_ref.at[:, pl.ds(pl.multiple_of(me * width, width), width)],
        own_sems.at[4],
    )
    own_back.start()
    returning = []
    for d in range(1, cams):
        peer = (me + d) % cams
        copy = pltpu.make_async_remote_copy(
            src_ref=heads.at[peer],
            dst_ref=attended_ref.at[:, pl.ds(pl.multiple_of(me * width, width), width)],
            send_sem=back_send.at[d - 1], recv_sem=back_recv.at[d - 1],
            device_id=cam_device(peer), device_id_type=MESH_IDS,
        )
        copy.start()
        returning.append(copy)
    for index in arrivals:
        gather.step(index)
    gather.finish()
    for d in range(1, cams):
        source = (me - d + cams) % cams
        region = attended_ref.at[:, pl.ds(pl.multiple_of(source * width, width), width)]
        pltpu.make_async_remote_copy(
            src_ref=region, dst_ref=region, send_sem=back_send.at[d - 1],
            recv_sem=back_recv.at[d - 1], device_id=cam_device(source), device_id_type=MESH_IDS,
        ).wait_recv()
    for copy in returning:
        copy.wait_send()
    own_back.wait()


def fused(query_rows, key_rows, value_rows, flag, out_weight):
    rows, features = query_rows.shape
    cams = lax.axis_size(CAM)
    width = features // cams
    shard, cols = out_weight.shape
    fsdp = lax.axis_size("z") * lax.axis_size("y_lo")
    any_spec = pl.BlockSpec(memory_space=pl.ANY)
    return pl.pallas_call(
        fused_kernel,
        out_shape=(
            jax.ShapeDtypeStruct((shard * fsdp, cols), out_weight.dtype),
            jax.ShapeDtypeStruct((rows, features), query_rows.dtype),
        ),
        in_specs=[any_spec] * 5,
        out_specs=(any_spec, any_spec),
        scratch_shapes=[
            pltpu.VMEM((cams, rows, 3 * width + 128), query_rows.dtype),
            pltpu.VMEM((cams, rows, width), query_rows.dtype),
            pltpu.SemaphoreType.DMA((SENDS,)),
            pltpu.SemaphoreType.DMA((2 * CHUNKS * len(RELATIVE),)),
            pltpu.SemaphoreType.DMA(()),
            pltpu.SemaphoreType.DMA((4 * (cams - 1),)),
            pltpu.SemaphoreType.DMA((4 * (cams - 1),)),
            pltpu.SemaphoreType.DMA((cams - 1,)),
            pltpu.SemaphoreType.DMA((cams - 1,)),
            pltpu.SemaphoreType.DMA((5,)),
        ],
        compiler_params=pltpu.CompilerParams(
            collective_id=0, has_side_effects=True, vmem_limit_bytes=60 * 1024 * 1024
        ),
    )(query_rows, key_rows, value_rows, flag, out_weight)


def local(queries, keys, values, out_weight, block_counts, row_mask):
    query_rows = queries[0]
    row_count = query_rows.shape[0]
    cam_count = lax.axis_size(CAM)
    offsets = jnp.arange(row_count, dtype=jnp.int32)
    row_valid = (row_mask[0] == 1) & (offsets // BLOCK < block_counts[0, 0])

    flag = jnp.broadcast_to(row_valid.astype(jnp.bfloat16)[:, None], (row_count, 128))
    weight_all, attended = fused(query_rows, keys[0], values[0], flag, out_weight)
    projected = jnp.dot(attended, weight_all, preferred_element_type=jnp.float32)
    result = jnp.where(row_valid[:, None], projected, jnp.float32(0.0)).astype(jnp.bfloat16)
    return result[None]


def solution(mesh):
    sub_mesh = Mesh(mesh.devices.reshape(4, 2, 2, 4, 2), CAM + FSDP)
    in_specs = (
        P(FSDP, CAM, None),
        P(FSDP, CAM, None),
        P(FSDP, CAM, None),
        P(FSDP, None),
        P(FSDP, CAM),
        P(FSDP, CAM),
    )
    out_specs = P(FSDP, CAM, None)
    return jax.shard_map(local, mesh=sub_mesh, in_specs=in_specs, out_specs=out_specs, check_vma=False)
```

```python
import functools
import math

import jax
import jax.numpy as jnp
from jax import lax
from jax.experimental import pallas as pl
from jax.experimental.pallas import tpu as pltpu
from jax.sharding import Mesh
from jax.sharding import PartitionSpec as P

HEAD_DIM = 128
BLOCK = 32

CAM = ("x", "y_hi", "core")
FSDP = ("z", "y_lo")
Y = ("y_hi", "y_lo")


MESH_IDS = pl.DeviceIdType.MESH


RELATIVE = ((-1, 0), (1, 0), (0, 1), (2, 0), (-1, 1), (1, 1), (2, 1))
ROUTES = {
    (0, 0): (("z", 1, (0, 1, 2, 3)), ("z", -1, (0, 1, 2, 3)), ("y", 1, (0, 1)), ("y", -1, (2, 3))),
    (-1, 0): (("z", 1, (0, 1)), ("y", 1, (1,)), ("y", -1, (2, 3))),
    (1, 0): (("z", -1, (2, 3)), ("y", 1, (0, 1)), ("y", -1, (2,))),
    (0, 1): (("z", 1, (0,)), ("z", -1, (3,))),
    (2, 0): (),
    (-1, 1): (("z", 1, (0, 1)),),
    (1, 1): (("z", -1, (2, 3)),),
    (2, 1): (),
}
SOURCES = {
    (-1, 0): (("z", -1),) * 4,
    (1, 0): (("z", 1),) * 4,
    (0, 1): (("y", -1),) * 2 + (("y", 1),) * 2,
    (2, 0): (("z", -1),) * 2 + (("z", 1),) * 2,
    (-1, 1): (("z", -1), ("y", -1), ("y", 1), ("y", 1)),
    (1, 1): (("y", -1), ("y", -1), ("y", 1), ("z", 1)),
    (2, 1): (("z", -1),) * 2 + (("z", 1),) * 2,
}
ARRIVALS = (
    ((-1, 0), 0), ((1, 0), 0), ((0, 1), 0), ((0, 1), 2),
    ((-1, 0), 1), ((1, 0), 1), ((0, 1), 1), ((0, 1), 3),
    ((-1, 0), 2), ((1, 0), 2), ((1, 1), 0), ((-1, 1), 2),
    ((-1, 0), 3), ((1, 0), 3), ((1, 1), 1), ((-1, 1), 1), ((1, 1), 2), ((-1, 1), 3),
    ((2, 0), 0), ((2, 0), 2), ((-1, 1), 0), ((1, 1), 3),
    ((2, 0), 1), ((2, 0), 3),
    ((2, 1), 0), ((2, 1), 2), ((2, 1), 1), ((2, 1), 3),
)
CHUNKS = 4
OWN_ORDER = (
    ("y", 1, 0), ("y", -1, 2), ("z", 1, 0), ("z", -1, 0),
    ("y", 1, 1), ("y", -1, 3), ("z", 1, 1), ("z", -1, 1),
    ("z", 1, 2), ("z", -1, 2), ("z", 1, 3), ("z", -1, 3),
)
SENDS = sum(len(c) for routes in ROUTES.values() for _, _, c in routes) + CHUNKS * len(RELATIVE)


class WeightGather:
    def __init__(self, w_ref, out_ref, send, recv, local_sem):
        self.w_ref, self.out_ref, self.send, self.recv = w_ref, out_ref, send, recv
        self.local_sem = local_sem
        self.k = lax.axis_index("core")
        self.z = lax.axis_index("z")
        self.yl = lax.axis_index("y_lo")
        self.y = lax.axis_index("y_hi") * 2 + self.yl
        self.shard = w_ref.shape[0]
        self.half = self.shard // 2
        self.chunk = self.half // CHUNKS
        self.partner = {"core": 1 - self.k}
        self.sent = []

    def device(self, axis, step):
        if axis == "z":
            return {"z": (self.z + step) % 4}
        yy = (self.y + step) % 4
        return {"y_hi": yy // 2, "y_lo": yy % 2}

    def neighbours(self):
        return (self.device("z", 1), self.device("z", -1), self.device("y", 1), self.device("y", -1))

    def shard_of(self, rel):
        dz, flip = rel
        return ((self.z + dz) % 4) * 2 + (self.yl + flip) % 2

    def region(self, rel, kk, c):
        start = self.shard_of(rel) * self.shard + kk * self.half + c * self.chunk
        return self.out_ref.at[pl.ds(pl.multiple_of(start, self.chunk), self.chunk)]

    @staticmethod
    def seen_by(rel, axis, step):
        dz, flip = rel
        if axis == "z":
            return ((dz - step + 1) % 4 - 1, flip)
        return (dz, 1 - flip)

    @staticmethod
    def recv_slot(rel, c, from_partner):
        return (len(RELATIVE) if from_partner else 0) * CHUNKS + RELATIVE.index(rel) * CHUNKS + c

    def copy(self, src, dst, slot, dev):
        copy = pltpu.make_async_remote_copy(
            src_ref=src, dst_ref=dst, send_sem=self.send.at[len(self.sent)],
            recv_sem=self.recv.at[slot], device_id=dev, device_id_type=MESH_IDS,
        )
        copy.start()
        self.sent.append(copy)

    def start(self):
        k, shard, half, chunk = self.k, self.shard, self.half, self.chunk
        own = self.shard_of((0, 0))
        self.local_copy = pltpu.make_async_copy(
            self.w_ref, self.out_ref.at[pl.ds(pl.multiple_of(own * shard, shard), shard)],
            self.local_sem,
        )
        self.local_copy.start()
        for axis, step, c in OWN_ORDER:
            src = self.w_ref.at[pl.ds(pl.multiple_of(k * half + c * chunk, chunk), chunk)]
            slot = self.recv_slot(self.seen_by((0, 0), axis, step), c, False)
            self.copy(src, self.region((0, 0), k, c), slot, self.device(axis, step))

    def arrive(self, rel, kk, c, dev, from_partner):
        piece = self.region(rel, kk, c)
        pltpu.make_async_remote_copy(
            src_ref=piece, dst_ref=piece, send_sem=self.send.at[0],
            recv_sem=self.recv.at[self.recv_slot(rel, c, from_partner)],
            device_id=dev, device_id_type=MESH_IDS,
        ).wait_recv()

    def step(self, index):
        rel, c = ARRIVALS[index]
        axis, step = SOURCES[rel][c]
        self.arrive(rel, self.k, c, self.device(axis, step), False)
        piece = self.region(rel, self.k, c)
        for axis, step, chunks in ROUTES[rel]:
            if c in chunks:
                slot = self.recv_slot(self.seen_by(rel, axis, step), c, False)
                self.copy(piece, piece, slot, self.device(axis, step))
        self.copy(piece, piece, self.recv_slot(rel, c, True), self.partner)

    def finish(self):
        for rel in RELATIVE:
            for c in range(CHUNKS):
                self.arrive(rel, 1 - self.k, c, self.partner, True)
        assert len(self.sent) == SENDS
        for copy in self.sent:
            copy.wait_send()
        self.local_copy.wait()


def cam_device(j):
    return {"x": j // 4, "y_hi": (j // 2) % 2, "core": j % 2}


def fused_kernel(
    q_ref, k_ref, v_ref, flag_ref, w_ref, weight_ref, attended_ref,
    inbox, heads, send, recv, local_sem, a2a_send, a2a_recv, back_send, back_recv, own_sems,
):
    cams = inbox.shape[0]
    rows = inbox.shape[1]
    width = heads.shape[2]
    head_count = width // HEAD_DIM
    sources = (q_ref, k_ref, v_ref, flag_ref)
    me = (lax.axis_index("x") * 2 + lax.axis_index("y_hi")) * 2 + lax.axis_index("core")
    gather = WeightGather(w_ref, weight_ref, send, recv, local_sem)

    barrier = pltpu.get_barrier_semaphore()
    peers = [cam_device((me + d) % cams) for d in range(1, cams)]
    for dev in peers + list(gather.neighbours()):
        pl.semaphore_signal(barrier, inc=1, device_id=dev, device_id_type=MESH_IDS)
    pl.semaphore_wait(barrier, len(peers) + 4)

    gather.start()
    def block(ref, part, j):
        if part == 3:
            return ref
        return ref.at[:, pl.ds(pl.multiple_of(j * width, width), width)]

    def slot_of(ref_inbox, part, j):
        return ref_inbox.at[j, :, pl.ds(part * width, width if part < 3 else 128)]

    own_in = []
    for part, ref in enumerate(sources):
        copy = pltpu.make_async_copy(block(ref, part, me), slot_of(inbox, part, me), own_sems.at[part])
        copy.start()
        own_in.append(copy)
    outgoing = []
    for d in range(1, cams):
        peer = (me + d) % cams
        for part, ref in enumerate(sources):
            copy = pltpu.make_async_remote_copy(
                src_ref=block(ref, part, peer), dst_ref=slot_of(inbox, part, me),
                send_sem=a2a_send.at[4 * (d - 1) + part], recv_sem=a2a_recv.at[4 * (d - 1) + part],
                device_id=cam_device(peer), device_id_type=MESH_IDS,
            )
            copy.start()
            outgoing.append(copy)

    arrivals = iter(range(len(ARRIVALS)))
    for _ in range(4):
        gather.step(next(arrivals))
    for copy in own_in:
        copy.wait()
    for d in range(1, cams):
        source = (me - d + cams) % cams
        for part in range(len(sources)):
            landing = slot_of(inbox, part, source)
            pltpu.make_async_remote_copy(
                src_ref=landing, dst_ref=landing, send_sem=a2a_send.at[4 * (d - 1) + part],
                recv_sem=a2a_recv.at[4 * (d - 1) + part], device_id=cam_device(source),
                device_id_type=MESH_IDS,
            ).wait_recv()

    total = cams * rows
    flags = inbox[:, :, 3 * width : 3 * width + 128].reshape(total, 128)
    counted = lax.dot_general(
        jnp.ones((8, 128), flags.dtype), flags, (((1,), (1,)), ((), ())),
        preferred_element_type=jnp.float32,
    )
    key_ok = counted[0:1, :] > 64.0
    score_scale = 1.0 / math.sqrt(HEAD_DIM)
    group = 2
    per_segment = 2
    for h in range(head_count):
        column = h * HEAD_DIM
        key_h = inbox[:, :, width + column : width + column + HEAD_DIM].reshape(total, HEAD_DIM)
        value_h = inbox[:, :, 2 * width + column : 2 * width + column + HEAD_DIM].reshape(
            total, HEAD_DIM
        )

        def attend_group(g, carry, column=column, key_h=key_h, value_h=value_h):
            first = pl.multiple_of(g * group, group)
            query_block = inbox[pl.ds(first, group), :, column : column + HEAD_DIM].reshape(
                group * rows, HEAD_DIM
            )
            scores = lax.dot_general(
                query_block, key_h, (((1,), (1,)), ((), ())), preferred_element_type=jnp.float32
            ) * score_scale
            scores = jnp.where(key_ok, scores, jnp.float32(-1e30))
            row_top = jnp.max(scores, axis=1, keepdims=True)
            raised = jnp.exp(scores - row_top)
            weights = (raised / jnp.sum(raised, axis=1, keepdims=True)).astype(jnp.bfloat16)
            out = jnp.dot(weights, value_h, preferred_element_type=jnp.float32).astype(jnp.bfloat16)
            heads[pl.ds(first, group), :, column : column + HEAD_DIM] = out.reshape(
                group, rows, HEAD_DIM
            )
            return carry

        for segment in range(cams // group // per_segment):
            lax.fori_loop(segment * per_segment, (segment + 1) * per_segment, attend_group, 0)
            gather.step(next(arrivals))

    for copy in outgoing:
        copy.wait_send()
    own_back = pltpu.make_async_copy(
        heads.at[me], attended_ref.at[:, pl.ds(pl.multiple_of(me * width, width), width)],
        own_sems.at[4],
    )
    own_back.start()
    returning = []
    for d in range(1, cams):
        peer = (me + d) % cams
        copy = pltpu.make_async_remote_copy(
            src_ref=heads.at[peer],
            dst_ref=attended_ref.at[:, pl.ds(pl.multiple_of(me * width, width), width)],
            send_sem=back_send.at[d - 1], recv_sem=back_recv.at[d - 1],
            device_id=cam_device(peer), device_id_type=MESH_IDS,
        )
        copy.start()
        returning.append(copy)
    for index in arrivals:
        gather.step(index)
    gather.finish()
    for d in range(1, cams):
        source = (me - d + cams) % cams
        region = attended_ref.at[:, pl.ds(pl.multiple_of(source * width, width), width)]
        pltpu.make_async_remote_copy(
            src_ref=region, dst_ref=region, send_sem=back_send.at[d - 1],
            recv_sem=back_recv.at[d - 1], device_id=cam_device(source), device_id_type=MESH_IDS,
        ).wait_recv()
    for copy in returning:
        copy.wait_send()
    own_back.wait()


def fused(query_rows, key_rows, value_rows, flag, out_weight):
    rows, features = query_rows.shape
    cams = lax.axis_size(CAM)
    width = features // cams
    shard, cols = out_weight.shape
    fsdp = lax.axis_size("z") * lax.axis_size("y_lo")
    any_spec = pl.BlockSpec(memory_space=pl.ANY)
    return pl.pallas_call(
        fused_kernel,
        out_shape=(
            jax.ShapeDtypeStruct((shard * fsdp, cols), out_weight.dtype),
            jax.ShapeDtypeStruct((rows, features), query_rows.dtype),
        ),
        in_specs=[any_spec] * 5,
        out_specs=(any_spec, any_spec),
        scratch_shapes=[
            pltpu.VMEM((cams, rows, 3 * width + 128), query_rows.dtype),
            pltpu.VMEM((cams, rows, width), query_rows.dtype),
            pltpu.SemaphoreType.DMA((SENDS,)),
            pltpu.SemaphoreType.DMA((2 * CHUNKS * len(RELATIVE),)),
            pltpu.SemaphoreType.DMA(()),
            pltpu.SemaphoreType.DMA((4 * (cams - 1),)),
            pltpu.SemaphoreType.DMA((4 * (cams - 1),)),
            pltpu.SemaphoreType.DMA((cams - 1,)),
            pltpu.SemaphoreType.DMA((cams - 1,)),
            pltpu.SemaphoreType.DMA((5,)),
        ],
        compiler_params=pltpu.CompilerParams(
            collective_id=0, has_side_effects=True, vmem_limit_bytes=60 * 1024 * 1024
        ),
    )(query_rows, key_rows, value_rows, flag, out_weight)


def local(queries, keys, values, out_weight, block_counts, row_mask):
    query_rows = queries[0]
    row_count = query_rows.shape[0]
    cam_count = lax.axis_size(CAM)
    offsets = jnp.arange(row_count, dtype=jnp.int32)
    row_valid = (row_mask[0] == 1) & (offsets // BLOCK < block_counts[0, 0])

    flag = jnp.broadcast_to(row_valid.astype(jnp.bfloat16)[:, None], (row_count, 128))
    weight_all, attended = fused(query_rows, keys[0], values[0], flag, out_weight)
    projected = jnp.dot(attended, weight_all, preferred_element_type=jnp.float32)
    result = jnp.where(row_valid[:, None], projected, jnp.float32(0.0)).astype(jnp.bfloat16)
    return result[None]


def solution(mesh):
    sub_mesh = Mesh(mesh.devices.reshape(4, 2, 2, 4, 2), CAM + FSDP)
    in_specs = (
        P(FSDP, CAM, None),
        P(FSDP, CAM, None),
        P(FSDP, CAM, None),
        P(FSDP, None),
        P(FSDP, CAM),
        P(FSDP, CAM),
    )
    out_specs = P(FSDP, CAM, None)
    return jax.shard_map(local, mesh=sub_mesh, in_specs=in_specs, out_specs=out_specs, check_vma=False)
```

```python
import functools
import math

import jax
import jax.numpy as jnp
from jax import lax
from jax.experimental import pallas as pl
from jax.experimental.pallas import tpu as pltpu
from jax.sharding import Mesh
from jax.sharding import PartitionSpec as P

HEAD_DIM = 128
BLOCK = 32

CAM = ("x", "y_hi", "core")
FSDP = ("z", "y_lo")
Y = ("y_hi", "y_lo")


MESH_IDS = pl.DeviceIdType.MESH


RELATIVE = ((-1, 0), (1, 0), (0, 1), (2, 0), (-1, 1), (1, 1), (2, 1))
ROUTES = {
    (0, 0): (("z", 1, (0, 1, 2, 3)), ("z", -1, (0, 1, 2, 3)), ("y", 1, (0, 1)), ("y", -1, (2, 3))),
    (-1, 0): (("z", 1, (0, 1)), ("y", 1, (1,)), ("y", -1, (2, 3))),
    (1, 0): (("z", -1, (2, 3)), ("y", 1, (0, 1)), ("y", -1, (2,))),
    (0, 1): (("z", 1, (0,)), ("z", -1, (3,))),
    (2, 0): (),
    (-1, 1): (("z", 1, (0, 1)),),
    (1, 1): (("z", -1, (2, 3)),),
    (2, 1): (),
}
SOURCES = {
    (-1, 0): (("z", -1),) * 4,
    (1, 0): (("z", 1),) * 4,
    (0, 1): (("y", -1),) * 2 + (("y", 1),) * 2,
    (2, 0): (("z", -1),) * 2 + (("z", 1),) * 2,
    (-1, 1): (("z", -1), ("y", -1), ("y", 1), ("y", 1)),
    (1, 1): (("y", -1), ("y", -1), ("y", 1), ("z", 1)),
    (2, 1): (("z", -1),) * 2 + (("z", 1),) * 2,
}
ARRIVALS = (
    ((-1, 0), 0), ((1, 0), 0), ((0, 1), 0), ((0, 1), 2),
    ((-1, 0), 1), ((1, 0), 1), ((0, 1), 1), ((0, 1), 3),
    ((-1, 0), 2), ((1, 0), 2), ((1, 1), 0), ((-1, 1), 2),
    ((-1, 0), 3), ((1, 0), 3), ((1, 1), 1), ((-1, 1), 1), ((1, 1), 2), ((-1, 1), 3),
    ((2, 0), 0), ((2, 0), 2), ((-1, 1), 0), ((1, 1), 3),
    ((2, 0), 1), ((2, 0), 3),
    ((2, 1), 0), ((2, 1), 2), ((2, 1), 1), ((2, 1), 3),
)
CHUNKS = 4
OWN_ORDER = (
    ("y", 1, 0), ("y", -1, 2), ("z", 1, 0), ("z", -1, 0),
    ("y", 1, 1), ("y", -1, 3), ("z", 1, 1), ("z", -1, 1),
    ("z", 1, 2), ("z", -1, 2), ("z", 1, 3), ("z", -1, 3),
)
SENDS = sum(len(c) for routes in ROUTES.values() for _, _, c in routes) + CHUNKS * len(RELATIVE)


class WeightGather:
    def __init__(self, w_ref, out_ref, send, recv, local_sem):
        self.w_ref, self.out_ref, self.send, self.recv = w_ref, out_ref, send, recv
        self.local_sem = local_sem
        self.k = lax.axis_index("core")
        self.z = lax.axis_index("z")
        self.yl = lax.axis_index("y_lo")
        self.y = lax.axis_index("y_hi") * 2 + self.yl
        self.shard = w_ref.shape[0]
        self.half = self.shard // 2
        self.chunk = self.half // CHUNKS
        self.partner = {"core": 1 - self.k}
        self.sent = []

    def device(self, axis, step):
        if axis == "z":
            return {"z": (self.z + step) % 4}
        yy = (self.y + step) % 4
        return {"y_hi": yy // 2, "y_lo": yy % 2}

    def neighbours(self):
        return (self.device("z", 1), self.device("z", -1), self.device("y", 1), self.device("y", -1))

    def shard_of(self, rel):
        dz, flip = rel
        return ((self.z + dz) % 4) * 2 + (self.yl + flip) % 2

    def region(self, rel, kk, c):
        start = self.shard_of(rel) * self.shard + kk * self.half + c * self.chunk
        return self.out_ref.at[pl.ds(pl.multiple_of(start, self.chunk), self.chunk)]

    @staticmethod
    def seen_by(rel, axis, step):
        dz, flip = rel
        if axis == "z":
            return ((dz - step + 1) % 4 - 1, flip)
        return (dz, 1 - flip)

    @staticmethod
    def recv_slot(rel, c, from_partner):
        return (len(RELATIVE) if from_partner else 0) * CHUNKS + RELATIVE.index(rel) * CHUNKS + c

    def copy(self, src, dst, slot, dev):
        copy = pltpu.make_async_remote_copy(
            src_ref=src, dst_ref=dst, send_sem=self.send.at[len(self.sent)],
            recv_sem=self.recv.at[slot], device_id=dev, device_id_type=MESH_IDS,
        )
        copy.start()
        self.sent.append(copy)

    def start(self):
        k, shard, half, chunk = self.k, self.shard, self.half, self.chunk
        own = self.shard_of((0, 0))
        self.local_copy = pltpu.make_async_copy(
            self.w_ref, self.out_ref.at[pl.ds(pl.multiple_of(own * shard, shard), shard)],
            self.local_sem,
        )
        self.local_copy.start()
        for axis, step, c in OWN_ORDER:
            src = self.w_ref.at[pl.ds(pl.multiple_of(k * half + c * chunk, chunk), chunk)]
            slot = self.recv_slot(self.seen_by((0, 0), axis, step), c, False)
            self.copy(src, self.region((0, 0), k, c), slot, self.device(axis, step))

    def arrive(self, rel, kk, c, dev, from_partner):
        piece = self.region(rel, kk, c)
        pltpu.make_async_remote_copy(
            src_ref=piece, dst_ref=piece, send_sem=self.send.at[0],
            recv_sem=self.recv.at[self.recv_slot(rel, c, from_partner)],
            device_id=dev, device_id_type=MESH_IDS,
        ).wait_recv()

    def step(self, index):
        rel, c = ARRIVALS[index]
        axis, step = SOURCES[rel][c]
        self.arrive(rel, self.k, c, self.device(axis, step), False)
        piece = self.region(rel, self.k, c)
        for axis, step, chunks in ROUTES[rel]:
            if c in chunks:
                slot = self.recv_slot(self.seen_by(rel, axis, step), c, False)
                self.copy(piece, piece, slot, self.device(axis, step))
        self.copy(piece, piece, self.recv_slot(rel, c, True), self.partner)

    def finish(self):
        for rel in RELATIVE:
            for c in range(CHUNKS):
                self.arrive(rel, 1 - self.k, c, self.partner, True)
        assert len(self.sent) == SENDS
        for copy in self.sent:
            copy.wait_send()
        self.local_copy.wait()


def cam_device(j):
    return {"x": j // 4, "y_hi": (j // 2) % 2, "core": j % 2}


def fused_kernel(
    q_ref, k_ref, v_ref, flag_ref, w_ref, weight_ref, attended_ref,
    inbox, heads, send, recv, local_sem, a2a_send, a2a_recv, back_send, back_recv, own_sems,
):
    cams = inbox.shape[0]
    rows = inbox.shape[1]
    width = heads.shape[2]
    head_count = width // HEAD_DIM
    sources = (q_ref, k_ref, v_ref, flag_ref)
    me = (lax.axis_index("x") * 2 + lax.axis_index("y_hi")) * 2 + lax.axis_index("core")
    gather = WeightGather(w_ref, weight_ref, send, recv, local_sem)

    barrier = pltpu.get_barrier_semaphore()
    peers = [cam_device((me + d) % cams) for d in range(1, cams)]
    for dev in peers + list(gather.neighbours()):
        pl.semaphore_signal(barrier, inc=1, device_id=dev, device_id_type=MESH_IDS)
    pl.semaphore_wait(barrier, len(peers) + 4)

    gather.start()
    def block(ref, part, j):
        if part == 3:
            return ref
        return ref.at[:, pl.ds(pl.multiple_of(j * width, width), width)]

    def slot_of(ref_inbox, part, j):
        return ref_inbox.at[j, :, pl.ds(part * width, width if part < 3 else 128)]

    own_in = []
    for part, ref in enumerate(sources):
        copy = pltpu.make_async_copy(block(ref, part, me), slot_of(inbox, part, me), own_sems.at[part])
        copy.start()
        own_in.append(copy)
    outgoing = []
    for d in range(1, cams):
        peer = (me + d) % cams
        for part, ref in enumerate(sources):
            copy = pltpu.make_async_remote_copy(
                src_ref=block(ref, part, peer), dst_ref=slot_of(inbox, part, me),
                send_sem=a2a_send.at[4 * (d - 1) + part], recv_sem=a2a_recv.at[4 * (d - 1) + part],
                device_id=cam_device(peer), device_id_type=MESH_IDS,
            )
            copy.start()
            outgoing.append(copy)

    arrivals = iter(range(len(ARRIVALS)))
    for _ in range(2):
        gather.step(next(arrivals))
    for copy in own_in:
        copy.wait()
    for d in range(1, cams):
        source = (me - d + cams) % cams
        for part in range(len(sources)):
            landing = slot_of(inbox, part, source)
            pltpu.make_async_remote_copy(
                src_ref=landing, dst_ref=landing, send_sem=a2a_send.at[4 * (d - 1) + part],
                recv_sem=a2a_recv.at[4 * (d - 1) + part], device_id=cam_device(source),
                device_id_type=MESH_IDS,
            ).wait_recv()

    total = cams * rows
    flags = inbox[:, :, 3 * width : 3 * width + 128].reshape(total, 128)
    counted = lax.dot_general(
        jnp.ones((8, 128), flags.dtype), flags, (((1,), (1,)), ((), ())),
        preferred_element_type=jnp.float32,
    )
    key_ok = counted[0:1, :] > 64.0
    score_scale = 1.0 / math.sqrt(HEAD_DIM)
    group = 2
    per_segment = 2
    for h in range(head_count):
        column = h * HEAD_DIM
        key_h = inbox[:, :, width + column : width + column + HEAD_DIM].reshape(total, HEAD_DIM)
        value_h = inbox[:, :, 2 * width + column : 2 * width + column + HEAD_DIM].reshape(
            total, HEAD_DIM
        )

        def attend_group(g, carry, column=column, key_h=key_h, value_h=value_h):
            first = pl.multiple_of(g * group, group)
            query_block = inbox[pl.ds(first, group), :, column : column + HEAD_DIM].reshape(
                group * rows, HEAD_DIM
            )
            scores = lax.dot_general(
                query_block, key_h, (((1,), (1,)), ((), ())), preferred_element_type=jnp.float32
            ) * score_scale
            scores = jnp.where(key_ok, scores, jnp.float32(-1e30))
            row_top = jnp.max(scores, axis=1, keepdims=True)
            raised = jnp.exp(scores - row_top)
            weights = (raised / jnp.sum(raised, axis=1, keepdims=True)).astype(jnp.bfloat16)
            out = jnp.dot(weights, value_h, preferred_element_type=jnp.float32).astype(jnp.bfloat16)
            heads[pl.ds(first, group), :, column : column + HEAD_DIM] = out.reshape(
                group, rows, HEAD_DIM
            )
            return carry

        for segment in range(cams // group // per_segment):
            lax.fori_loop(segment * per_segment, (segment + 1) * per_segment, attend_group, 0)
            gather.step(next(arrivals))

    for copy in outgoing:
        copy.wait_send()
    own_back = pltpu.make_async_copy(
        heads.at[me], attended_ref.at[:, pl.ds(pl.multiple_of(me * width, width), width)],
        own_sems.at[4],
    )
    own_back.start()
    returning = []
    for d in range(1, cams):
        peer = (me + d) % cams
        copy = pltpu.make_async_remote_copy(
            src_ref=heads.at[peer],
            dst_ref=attended_ref.at[:, pl.ds(pl.multiple_of(me * width, width), width)],
            send_sem=back_send.at[d - 1], recv_sem=back_recv.at[d - 1],
            device_id=cam_device(peer), device_id_type=MESH_IDS,
        )
        copy.start()
        returning.append(copy)
    for index in arrivals:
        gather.step(index)
    gather.finish()
    for d in range(1, cams):
        source = (me - d + cams) % cams
        region = attended_ref.at[:, pl.ds(pl.multiple_of(source * width, width), width)]
        pltpu.make_async_remote_copy(
            src_ref=region, dst_ref=region, send_sem=back_send.at[d - 1],
            recv_sem=back_recv.at[d - 1], device_id=cam_device(source), device_id_type=MESH_IDS,
        ).wait_recv()
    for copy in returning:
        copy.wait_send()
    own_back.wait()


def fused(query_rows, key_rows, value_rows, flag, out_weight):
    rows, features = query_rows.shape
    cams = lax.axis_size(CAM)
    width = features // cams
    shard, cols = out_weight.shape
    fsdp = lax.axis_size("z") * lax.axis_size("y_lo")
    any_spec = pl.BlockSpec(memory_space=pl.ANY)
    return pl.pallas_call(
        fused_kernel,
        out_shape=(
            jax.ShapeDtypeStruct((shard * fsdp, cols), out_weight.dtype),
            jax.ShapeDtypeStruct((rows, features), query_rows.dtype),
        ),
        in_specs=[any_spec] * 5,
        out_specs=(any_spec, any_spec),
        scratch_shapes=[
            pltpu.VMEM((cams, rows, 3 * width + 128), query_rows.dtype),
            pltpu.VMEM((cams, rows, width), query_rows.dtype),
            pltpu.SemaphoreType.DMA((SENDS,)),
            pltpu.SemaphoreType.DMA((2 * CHUNKS * len(RELATIVE),)),
            pltpu.SemaphoreType.DMA(()),
            pltpu.SemaphoreType.DMA((4 * (cams - 1),)),
            pltpu.SemaphoreType.DMA((4 * (cams - 1),)),
            pltpu.SemaphoreType.DMA((cams - 1,)),
            pltpu.SemaphoreType.DMA((cams - 1,)),
            pltpu.SemaphoreType.DMA((5,)),
        ],
        compiler_params=pltpu.CompilerParams(
            collective_id=0, has_side_effects=True, vmem_limit_bytes=60 * 1024 * 1024
        ),
    )(query_rows, key_rows, value_rows, flag, out_weight)


def local(queries, keys, values, out_weight, block_counts, row_mask):
    query_rows = queries[0]
    row_count = query_rows.shape[0]
    cam_count = lax.axis_size(CAM)
    offsets = jnp.arange(row_count, dtype=jnp.int32)
    row_valid = (row_mask[0] == 1) & (offsets // BLOCK < block_counts[0, 0])

    flag = jnp.broadcast_to(row_valid.astype(jnp.bfloat16)[:, None], (row_count, 128))
    weight_all, attended = fused(query_rows, keys[0], values[0], flag, out_weight)
    projected = jnp.dot(attended, weight_all, preferred_element_type=jnp.float32)
    result = jnp.where(row_valid[:, None], projected, jnp.float32(0.0)).astype(jnp.bfloat16)
    return result[None]


def solution(mesh):
    sub_mesh = Mesh(mesh.devices.reshape(4, 2, 2, 4, 2), CAM + FSDP)
    in_specs = (
        P(FSDP, CAM, None),
        P(FSDP, CAM, None),
        P(FSDP, CAM, None),
        P(FSDP, None),
        P(FSDP, CAM),
        P(FSDP, CAM),
    )
    out_specs = P(FSDP, CAM, None)
    return jax.shard_map(local, mesh=sub_mesh, in_specs=in_specs, out_specs=out_specs, check_vma=False)
```

```python
import functools
import math

import jax
import jax.numpy as jnp
from jax import lax
from jax.experimental import pallas as pl
from jax.experimental.pallas import tpu as pltpu
from jax.sharding import Mesh
from jax.sharding import PartitionSpec as P

HEAD_DIM = 128
BLOCK = 32

CAM = ("x", "y_hi", "core")
FSDP = ("z", "y_lo")
Y = ("y_hi", "y_lo")


MESH_IDS = pl.DeviceIdType.MESH


RELATIVE = ((-1, 0), (1, 0), (0, 1), (2, 0), (-1, 1), (1, 1), (2, 1))
ROUTES = {
    (0, 0): (("z", 1, (0, 1, 2, 3)), ("z", -1, (0, 1, 2, 3)), ("y", 1, (0, 1)), ("y", -1, (2, 3))),
    (-1, 0): (("z", 1, (0, 1)), ("y", 1, (1,)), ("y", -1, (2, 3))),
    (1, 0): (("z", -1, (2, 3)), ("y", 1, (0, 1)), ("y", -1, (2,))),
    (0, 1): (("z", 1, (0,)), ("z", -1, (3,))),
    (2, 0): (),
    (-1, 1): (("z", 1, (0, 1)),),
    (1, 1): (("z", -1, (2, 3)),),
    (2, 1): (),
}
SOURCES = {
    (-1, 0): (("z", -1),) * 4,
    (1, 0): (("z", 1),) * 4,
    (0, 1): (("y", -1),) * 2 + (("y", 1),) * 2,
    (2, 0): (("z", -1),) * 2 + (("z", 1),) * 2,
    (-1, 1): (("z", -1), ("y", -1), ("y", 1), ("y", 1)),
    (1, 1): (("y", -1), ("y", -1), ("y", 1), ("z", 1)),
    (2, 1): (("z", -1),) * 2 + (("z", 1),) * 2,
}
ARRIVALS = (
    ((-1, 0), 0), ((1, 0), 0), ((0, 1), 0), ((0, 1), 2),
    ((-1, 0), 1), ((1, 0), 1), ((0, 1), 1), ((0, 1), 3),
    ((-1, 0), 2), ((1, 0), 2), ((1, 1), 0), ((-1, 1), 2),
    ((-1, 0), 3), ((1, 0), 3), ((1, 1), 1), ((-1, 1), 1), ((1, 1), 2), ((-1, 1), 3),
    ((2, 0), 0), ((2, 0), 2), ((-1, 1), 0), ((1, 1), 3),
    ((2, 0), 1), ((2, 0), 3),
    ((2, 1), 0), ((2, 1), 2), ((2, 1), 1), ((2, 1), 3),
)
CHUNKS = 4
OWN_ORDER = (
    ("y", 1, 0), ("y", -1, 2), ("z", 1, 0), ("z", -1, 0),
    ("y", 1, 1), ("y", -1, 3), ("z", 1, 1), ("z", -1, 1),
    ("z", 1, 2), ("z", -1, 2), ("z", 1, 3), ("z", -1, 3),
)
SENDS = sum(len(c) for routes in ROUTES.values() for _, _, c in routes) + CHUNKS * len(RELATIVE)


class WeightGather:
    def __init__(self, w_ref, out_ref, send, recv, local_sem):
        self.w_ref, self.out_ref, self.send, self.recv = w_ref, out_ref, send, recv
        self.local_sem = local_sem
        self.k = lax.axis_index("core")
        self.z = lax.axis_index("z")
        self.yl = lax.axis_index("y_lo")
        self.y = lax.axis_index("y_hi") * 2 + self.yl
        self.shard = w_ref.shape[0]
        self.half = self.shard // 2
        self.chunk = self.half // CHUNKS
        self.partner = {"core": 1 - self.k}
        self.sent = []

    def device(self, axis, step):
        if axis == "z":
            return {"z": (self.z + step) % 4}
        yy = (self.y + step) % 4
        return {"y_hi": yy // 2, "y_lo": yy % 2}

    def neighbours(self):
        return (self.device("z", 1), self.device("z", -1), self.device("y", 1), self.device("y", -1))

    def shard_of(self, rel):
        dz, flip = rel
        return ((self.z + dz) % 4) * 2 + (self.yl + flip) % 2

    def region(self, rel, kk, c):
        start = self.shard_of(rel) * self.shard + kk * self.half + c * self.chunk
        return self.out_ref.at[pl.ds(pl.multiple_of(start, self.chunk), self.chunk)]

    @staticmethod
    def seen_by(rel, axis, step):
        dz, flip = rel
        if axis == "z":
            return ((dz - step + 1) % 4 - 1, flip)
        return (dz, 1 - flip)

    @staticmethod
    def recv_slot(rel, c, from_partner):
        return (len(RELATIVE) if from_partner else 0) * CHUNKS + RELATIVE.index(rel) * CHUNKS + c

    def copy(self, src, dst, slot, dev):
        copy = pltpu.make_async_remote_copy(
            src_ref=src, dst_ref=dst, send_sem=self.send.at[len(self.sent)],
            recv_sem=self.recv.at[slot], device_id=dev, device_id_type=MESH_IDS,
        )
        copy.start()
        self.sent.append(copy)

    def start(self):
        k, shard, half, chunk = self.k, self.shard, self.half, self.chunk
        own = self.shard_of((0, 0))
        self.local_copy = pltpu.make_async_copy(
            self.w_ref, self.out_ref.at[pl.ds(pl.multiple_of(own * shard, shard), shard)],
            self.local_sem,
        )
        self.local_copy.start()
        for axis, step, c in OWN_ORDER:
            src = self.w_ref.at[pl.ds(pl.multiple_of(k * half + c * chunk, chunk), chunk)]
            slot = self.recv_slot(self.seen_by((0, 0), axis, step), c, False)
            self.copy(src, self.region((0, 0), k, c), slot, self.device(axis, step))

    def arrive(self, rel, kk, c, dev, from_partner):
        piece = self.region(rel, kk, c)
        pltpu.make_async_remote_copy(
            src_ref=piece, dst_ref=piece, send_sem=self.send.at[0],
            recv_sem=self.recv.at[self.recv_slot(rel, c, from_partner)],
            device_id=dev, device_id_type=MESH_IDS,
        ).wait_recv()

    def step(self, index):
        rel, c = ARRIVALS[index]
        axis, step = SOURCES[rel][c]
        self.arrive(rel, self.k, c, self.device(axis, step), False)
        piece = self.region(rel, self.k, c)
        for axis, step, chunks in ROUTES[rel]:
            if c in chunks:
                slot = self.recv_slot(self.seen_by(rel, axis, step), c, False)
                self.copy(piece, piece, slot, self.device(axis, step))
        self.copy(piece, piece, self.recv_slot(rel, c, True), self.partner)

    def finish(self):
        for rel in RELATIVE:
            for c in range(CHUNKS):
                self.arrive(rel, 1 - self.k, c, self.partner, True)
        assert len(self.sent) == SENDS
        for copy in self.sent:
            copy.wait_send()
        self.local_copy.wait()


def cam_device(j):
    return {"x": j // 4, "y_hi": (j // 2) % 2, "core": j % 2}


def fused_kernel(
    q_ref, k_ref, v_ref, flag_ref, w_ref, weight_ref, attended_ref,
    inbox, heads, send, recv, local_sem, a2a_send, a2a_recv, back_send, back_recv, own_sems,
):
    cams = inbox.shape[0]
    rows = inbox.shape[1]
    width = heads.shape[2]
    head_count = width // HEAD_DIM
    sources = (q_ref, k_ref, v_ref, flag_ref)
    me = (lax.axis_index("x") * 2 + lax.axis_index("y_hi")) * 2 + lax.axis_index("core")
    gather = WeightGather(w_ref, weight_ref, send, recv, local_sem)

    barrier = pltpu.get_barrier_semaphore()
    peers = [cam_device((me + d) % cams) for d in range(1, cams)]
    for dev in peers + list(gather.neighbours()):
        pl.semaphore_signal(barrier, inc=1, device_id=dev, device_id_type=MESH_IDS)
    pl.semaphore_wait(barrier, len(peers) + 4)

    gather.start()
    def block(ref, part, j):
        if part == 3:
            return ref
        return ref.at[:, pl.ds(pl.multiple_of(j * width, width), width)]

    def slot_of(ref_inbox, part, j):
        return ref_inbox.at[j, :, pl.ds(part * width, width if part < 3 else 128)]

    own_in = []
    for part, ref in enumerate(sources):
        copy = pltpu.make_async_copy(block(ref, part, me), slot_of(inbox, part, me), own_sems.at[part])
        copy.start()
        own_in.append(copy)
    outgoing = []
    for d in range(1, cams):
        peer = (me + d) % cams
        for part, ref in enumerate(sources):
            copy = pltpu.make_async_remote_copy(
                src_ref=block(ref, part, peer), dst_ref=slot_of(inbox, part, me),
                send_sem=a2a_send.at[4 * (d - 1) + part], recv_sem=a2a_recv.at[4 * (d - 1) + part],
                device_id=cam_device(peer), device_id_type=MESH_IDS,
            )
            copy.start()
            outgoing.append(copy)

    arrivals = iter(range(len(ARRIVALS)))
    for _ in range(6):
        gather.step(next(arrivals))
    for copy in own_in:
        copy.wait()
    for d in range(1, cams):
        source = (me - d + cams) % cams
        for part in range(len(sources)):
            landing = slot_of(inbox, part, source)
            pltpu.make_async_remote_copy(
                src_ref=landing, dst_ref=landing, send_sem=a2a_send.at[4 * (d - 1) + part],
                recv_sem=a2a_recv.at[4 * (d - 1) + part], device_id=cam_device(source),
                device_id_type=MESH_IDS,
            ).wait_recv()

    total = cams * rows
    flags = inbox[:, :, 3 * width : 3 * width + 128].reshape(total, 128)
    counted = lax.dot_general(
        jnp.ones((8, 128), flags.dtype), flags, (((1,), (1,)), ((), ())),
        preferred_element_type=jnp.float32,
    )
    key_ok = counted[0:1, :] > 64.0
    score_scale = 1.0 / math.sqrt(HEAD_DIM)
    group = 2
    per_segment = 2
    for h in range(head_count):
        column = h * HEAD_DIM
        key_h = inbox[:, :, width + column : width + column + HEAD_DIM].reshape(total, HEAD_DIM)
        value_h = inbox[:, :, 2 * width + column : 2 * width + column + HEAD_DIM].reshape(
            total, HEAD_DIM
        )

        def attend_group(g, carry, column=column, key_h=key_h, value_h=value_h):
            first = pl.multiple_of(g * group, group)
            query_block = inbox[pl.ds(first, group), :, column : column + HEAD_DIM].reshape(
                group * rows, HEAD_DIM
            )
            scores = lax.dot_general(
                query_block, key_h, (((1,), (1,)), ((), ())), preferred_element_type=jnp.float32
            ) * score_scale
            scores = jnp.where(key_ok, scores, jnp.float32(-1e30))
            row_top = jnp.max(scores, axis=1, keepdims=True)
            raised = jnp.exp(scores - row_top)
            weights = (raised / jnp.sum(raised, axis=1, keepdims=True)).astype(jnp.bfloat16)
            out = jnp.dot(weights, value_h, preferred_element_type=jnp.float32).astype(jnp.bfloat16)
            heads[pl.ds(first, group), :, column : column + HEAD_DIM] = out.reshape(
                group, rows, HEAD_DIM
            )
            return carry

        for segment in range(cams // group // per_segment):
            lax.fori_loop(segment * per_segment, (segment + 1) * per_segment, attend_group, 0)
            gather.step(next(arrivals))

    for copy in outgoing:
        copy.wait_send()
    own_back = pltpu.make_async_copy(
        heads.at[me], attended_ref.at[:, pl.ds(pl.multiple_of(me * width, width), width)],
        own_sems.at[4],
    )
    own_back.start()
    returning = []
    for d in range(1, cams):
        peer = (me + d) % cams
        copy = pltpu.make_async_remote_copy(
            src_ref=heads.at[peer],
            dst_ref=attended_ref.at[:, pl.ds(pl.multiple_of(me * width, width), width)],
            send_sem=back_send.at[d - 1], recv_sem=back_recv.at[d - 1],
            device_id=cam_device(peer), device_id_type=MESH_IDS,
        )
        copy.start()
        returning.append(copy)
    for index in arrivals:
        gather.step(index)
    gather.finish()
    for d in range(1, cams):
        source = (me - d + cams) % cams
        region = attended_ref.at[:, pl.ds(pl.multiple_of(source * width, width), width)]
        pltpu.make_async_remote_copy(
            src_ref=region, dst_ref=region, send_sem=back_send.at[d - 1],
            recv_sem=back_recv.at[d - 1], device_id=cam_device(source), device_id_type=MESH_IDS,
        ).wait_recv()
    for copy in returning:
        copy.wait_send()
    own_back.wait()


def fused(query_rows, key_rows, value_rows, flag, out_weight):
    rows, features = query_rows.shape
    cams = lax.axis_size(CAM)
    width = features // cams
    shard, cols = out_weight.shape
    fsdp = lax.axis_size("z") * lax.axis_size("y_lo")
    any_spec = pl.BlockSpec(memory_space=pl.ANY)
    return pl.pallas_call(
        fused_kernel,
        out_shape=(
            jax.ShapeDtypeStruct((shard * fsdp, cols), out_weight.dtype),
            jax.ShapeDtypeStruct((rows, features), query_rows.dtype),
        ),
        in_specs=[any_spec] * 5,
        out_specs=(any_spec, any_spec),
        scratch_shapes=[
            pltpu.VMEM((cams, rows, 3 * width + 128), query_rows.dtype),
            pltpu.VMEM((cams, rows, width), query_rows.dtype),
            pltpu.SemaphoreType.DMA((SENDS,)),
            pltpu.SemaphoreType.DMA((2 * CHUNKS * len(RELATIVE),)),
            pltpu.SemaphoreType.DMA(()),
            pltpu.SemaphoreType.DMA((4 * (cams - 1),)),
            pltpu.SemaphoreType.DMA((4 * (cams - 1),)),
            pltpu.SemaphoreType.DMA((cams - 1,)),
            pltpu.SemaphoreType.DMA((cams - 1,)),
            pltpu.SemaphoreType.DMA((5,)),
        ],
        compiler_params=pltpu.CompilerParams(
            collective_id=0, has_side_effects=True, vmem_limit_bytes=60 * 1024 * 1024
        ),
    )(query_rows, key_rows, value_rows, flag, out_weight)


def local(queries, keys, values, out_weight, block_counts, row_mask):
    query_rows = queries[0]
    row_count = query_rows.shape[0]
    cam_count = lax.axis_size(CAM)
    offsets = jnp.arange(row_count, dtype=jnp.int32)
    row_valid = (row_mask[0] == 1) & (offsets // BLOCK < block_counts[0, 0])

    flag = jnp.broadcast_to(row_valid.astype(jnp.bfloat16)[:, None], (row_count, 128))
    weight_all, attended = fused(query_rows, keys[0], values[0], flag, out_weight)
    projected = jnp.dot(attended, weight_all, preferred_element_type=jnp.float32)
    result = jnp.where(row_valid[:, None], projected, jnp.float32(0.0)).astype(jnp.bfloat16)
    return result[None]


def solution(mesh):
    sub_mesh = Mesh(mesh.devices.reshape(4, 2, 2, 4, 2), CAM + FSDP)
    in_specs = (
        P(FSDP, CAM, None),
        P(FSDP, CAM, None),
        P(FSDP, CAM, None),
        P(FSDP, None),
        P(FSDP, CAM),
        P(FSDP, CAM),
    )
    out_specs = P(FSDP, CAM, None)
    return jax.shard_map(local, mesh=sub_mesh, in_specs=in_specs, out_specs=out_specs, check_vma=False)
```

```python
import functools
import math

import jax
import jax.numpy as jnp
from jax import lax
from jax.experimental import pallas as pl
from jax.experimental.pallas import tpu as pltpu
from jax.sharding import Mesh
from jax.sharding import PartitionSpec as P

HEAD_DIM = 128
BLOCK = 32

CAM = ("x", "y_hi", "core")
FSDP = ("z", "y_lo")
Y = ("y_hi", "y_lo")


MESH_IDS = pl.DeviceIdType.MESH


RELATIVE = ((-1, 0), (1, 0), (0, 1), (2, 0), (-1, 1), (1, 1), (2, 1))
ROUTES = {
    (0, 0): (("z", 1, (0, 1, 2, 3)), ("z", -1, (0, 1, 2, 3)), ("y", 1, (0, 1)), ("y", -1, (2, 3))),
    (-1, 0): (("z", 1, (0, 1)), ("y", 1, (1,)), ("y", -1, (2, 3))),
    (1, 0): (("z", -1, (2, 3)), ("y", 1, (0, 1)), ("y", -1, (2,))),
    (0, 1): (("z", 1, (0,)), ("z", -1, (3,))),
    (2, 0): (),
    (-1, 1): (("z", 1, (0, 1)),),
    (1, 1): (("z", -1, (2, 3)),),
    (2, 1): (),
}
SOURCES = {
    (-1, 0): (("z", -1),) * 4,
    (1, 0): (("z", 1),) * 4,
    (0, 1): (("y", -1),) * 2 + (("y", 1),) * 2,
    (2, 0): (("z", -1),) * 2 + (("z", 1),) * 2,
    (-1, 1): (("z", -1), ("y", -1), ("y", 1), ("y", 1)),
    (1, 1): (("y", -1), ("y", -1), ("y", 1), ("z", 1)),
    (2, 1): (("z", -1),) * 2 + (("z", 1),) * 2,
}
ARRIVALS = (
    ((-1, 0), 0), ((1, 0), 0), ((0, 1), 0), ((0, 1), 2),
    ((-1, 0), 1), ((1, 0), 1), ((0, 1), 1), ((0, 1), 3),
    ((-1, 0), 2), ((1, 0), 2), ((1, 1), 0), ((-1, 1), 2),
    ((-1, 0), 3), ((1, 0), 3), ((1, 1), 1), ((-1, 1), 1), ((1, 1), 2), ((-1, 1), 3),
    ((2, 0), 0), ((2, 0), 2), ((-1, 1), 0), ((1, 1), 3),
    ((2, 0), 1), ((2, 0), 3),
    ((2, 1), 0), ((2, 1), 2), ((2, 1), 1), ((2, 1), 3),
)
CHUNKS = 4
OWN_ORDER = (
    ("y", 1, 0), ("y", -1, 2), ("z", 1, 0), ("z", -1, 0),
    ("y", 1, 1), ("y", -1, 3), ("z", 1, 1), ("z", -1, 1),
    ("z", 1, 2), ("z", -1, 2), ("z", 1, 3), ("z", -1, 3),
)
SENDS = sum(len(c) for routes in ROUTES.values() for _, _, c in routes) + CHUNKS * len(RELATIVE)


class WeightGather:
    def __init__(self, w_ref, out_ref, send, recv, local_sem):
        self.w_ref, self.out_ref, self.send, self.recv = w_ref, out_ref, send, recv
        self.local_sem = local_sem
        self.k = lax.axis_index("core")
        self.z = lax.axis_index("z")
        self.yl = lax.axis_index("y_lo")
        self.y = lax.axis_index("y_hi") * 2 + self.yl
        self.shard = w_ref.shape[0]
        self.half = self.shard // 2
        self.chunk = self.half // CHUNKS
        self.partner = {"core": 1 - self.k}
        self.sent = []

    def device(self, axis, step):
        if axis == "z":
            return {"z": (self.z + step) % 4}
        yy = (self.y + step) % 4
        return {"y_hi": yy // 2, "y_lo": yy % 2}

    def neighbours(self):
        return (self.device("z", 1), self.device("z", -1), self.device("y", 1), self.device("y", -1))

    def shard_of(self, rel):
        dz, flip = rel
        return ((self.z + dz) % 4) * 2 + (self.yl + flip) % 2

    def region(self, rel, kk, c):
        start = self.shard_of(rel) * self.shard + kk * self.half + c * self.chunk
        return self.out_ref.at[pl.ds(pl.multiple_of(start, self.chunk), self.chunk)]

    @staticmethod
    def seen_by(rel, axis, step):
        dz, flip = rel
        if axis == "z":
            return ((dz - step + 1) % 4 - 1, flip)
        return (dz, 1 - flip)

    @staticmethod
    def recv_slot(rel, c, from_partner):
        return (len(RELATIVE) if from_partner else 0) * CHUNKS + RELATIVE.index(rel) * CHUNKS + c

    def copy(self, src, dst, slot, dev):
        copy = pltpu.make_async_remote_copy(
            src_ref=src, dst_ref=dst, send_sem=self.send.at[len(self.sent)],
            recv_sem=self.recv.at[slot], device_id=dev, device_id_type=MESH_IDS,
        )
        copy.start()
        self.sent.append(copy)

    def start(self):
        k, shard, half, chunk = self.k, self.shard, self.half, self.chunk
        own = self.shard_of((0, 0))
        self.local_copy = pltpu.make_async_copy(
            self.w_ref, self.out_ref.at[pl.ds(pl.multiple_of(own * shard, shard), shard)],
            self.local_sem,
        )
        self.local_copy.start()
        for axis, step, c in OWN_ORDER:
            src = self.w_ref.at[pl.ds(pl.multiple_of(k * half + c * chunk, chunk), chunk)]
            slot = self.recv_slot(self.seen_by((0, 0), axis, step), c, False)
            self.copy(src, self.region((0, 0), k, c), slot, self.device(axis, step))

    def arrive(self, rel, kk, c, dev, from_partner):
        piece = self.region(rel, kk, c)
        pltpu.make_async_remote_copy(
            src_ref=piece, dst_ref=piece, send_sem=self.send.at[0],
            recv_sem=self.recv.at[self.recv_slot(rel, c, from_partner)],
            device_id=dev, device_id_type=MESH_IDS,
        ).wait_recv()

    def step(self, index):
        rel, c = ARRIVALS[index]
        axis, step = SOURCES[rel][c]
        self.arrive(rel, self.k, c, self.device(axis, step), False)
        piece = self.region(rel, self.k, c)
        for axis, step, chunks in ROUTES[rel]:
            if c in chunks:
                slot = self.recv_slot(self.seen_by(rel, axis, step), c, False)
                self.copy(piece, piece, slot, self.device(axis, step))
        self.copy(piece, piece, self.recv_slot(rel, c, True), self.partner)

    def finish(self):
        for rel in RELATIVE:
            for c in range(CHUNKS):
                self.arrive(rel, 1 - self.k, c, self.partner, True)
        assert len(self.sent) == SENDS
        for copy in self.sent:
            copy.wait_send()
        self.local_copy.wait()


def cam_device(j):
    return {"x": j // 4, "y_hi": (j // 2) % 2, "core": j % 2}


def fused_kernel(
    q_ref, k_ref, v_ref, flag_ref, w_ref, weight_ref, attended_ref,
    inbox, heads, send, recv, local_sem, a2a_send, a2a_recv, back_send, back_recv, own_sems,
):
    cams = inbox.shape[0]
    rows = inbox.shape[1]
    width = heads.shape[2]
    head_count = width // HEAD_DIM
    sources = (q_ref, k_ref, v_ref, flag_ref)
    me = (lax.axis_index("x") * 2 + lax.axis_index("y_hi")) * 2 + lax.axis_index("core")
    gather = WeightGather(w_ref, weight_ref, send, recv, local_sem)

    barrier = pltpu.get_barrier_semaphore()
    peers = [cam_device((me + d) % cams) for d in range(1, cams)]
    for dev in peers + list(gather.neighbours()):
        pl.semaphore_signal(barrier, inc=1, device_id=dev, device_id_type=MESH_IDS)
    pl.semaphore_wait(barrier, len(peers) + 4)

    gather.start()
    def block(ref, part, j):
        if part == 3:
            return ref
        return ref.at[:, pl.ds(pl.multiple_of(j * width, width), width)]

    def slot_of(ref_inbox, part, j):
        return ref_inbox.at[j, :, pl.ds(part * width, width if part < 3 else 128)]

    own_in = []
    for part, ref in enumerate(sources):
        copy = pltpu.make_async_copy(block(ref, part, me), slot_of(inbox, part, me), own_sems.at[part])
        copy.start()
        own_in.append(copy)
    outgoing = []
    for d in range(1, cams):
        peer = (me + d) % cams
        for part, ref in enumerate(sources):
            copy = pltpu.make_async_remote_copy(
                src_ref=block(ref, part, peer), dst_ref=slot_of(inbox, part, me),
                send_sem=a2a_send.at[4 * (d - 1) + part], recv_sem=a2a_recv.at[4 * (d - 1) + part],
                device_id=cam_device(peer), device_id_type=MESH_IDS,
            )
            copy.start()
            outgoing.append(copy)

    arrivals = iter(range(len(ARRIVALS)))
    for _ in range(8):
        gather.step(next(arrivals))
    for copy in own_in:
        copy.wait()
    for d in range(1, cams):
        source = (me - d + cams) % cams
        for part in range(len(sources)):
            landing = slot_of(inbox, part, source)
            pltpu.make_async_remote_copy(
                src_ref=landing, dst_ref=landing, send_sem=a2a_send.at[4 * (d - 1) + part],
                recv_sem=a2a_recv.at[4 * (d - 1) + part], device_id=cam_device(source),
                device_id_type=MESH_IDS,
            ).wait_recv()

    total = cams * rows
    flags = inbox[:, :, 3 * width : 3 * width + 128].reshape(total, 128)
    counted = lax.dot_general(
        jnp.ones((8, 128), flags.dtype), flags, (((1,), (1,)), ((), ())),
        preferred_element_type=jnp.float32,
    )
    key_ok = counted[0:1, :] > 64.0
    score_scale = 1.0 / math.sqrt(HEAD_DIM)
    group = 2
    per_segment = 2
    for h in range(head_count):
        column = h * HEAD_DIM
        key_h = inbox[:, :, width + column : width + column + HEAD_DIM].reshape(total, HEAD_DIM)
        value_h = inbox[:, :, 2 * width + column : 2 * width + column + HEAD_DIM].reshape(
            total, HEAD_DIM
        )

        def attend_group(g, carry, column=column, key_h=key_h, value_h=value_h):
            first = pl.multiple_of(g * group, group)
            query_block = inbox[pl.ds(first, group), :, column : column + HEAD_DIM].reshape(
                group * rows, HEAD_DIM
            )
            scores = lax.dot_general(
                query_block, key_h, (((1,), (1,)), ((), ())), preferred_element_type=jnp.float32
            ) * score_scale
            scores = jnp.where(key_ok, scores, jnp.float32(-1e30))
            row_top = jnp.max(scores, axis=1, keepdims=True)
            raised = jnp.exp(scores - row_top)
            weights = (raised / jnp.sum(raised, axis=1, keepdims=True)).astype(jnp.bfloat16)
            out = jnp.dot(weights, value_h, preferred_element_type=jnp.float32).astype(jnp.bfloat16)
            heads[pl.ds(first, group), :, column : column + HEAD_DIM] = out.reshape(
                group, rows, HEAD_DIM
            )
            return carry

        for segment in range(cams // group // per_segment):
            lax.fori_loop(segment * per_segment, (segment + 1) * per_segment, attend_group, 0)
            gather.step(next(arrivals))

    for copy in outgoing:
        copy.wait_send()
    own_back = pltpu.make_async_copy(
        heads.at[me], attended_ref.at[:, pl.ds(pl.multiple_of(me * width, width), width)],
        own_sems.at[4],
    )
    own_back.start()
    returning = []
    for d in range(1, cams):
        peer = (me + d) % cams
        copy = pltpu.make_async_remote_copy(
            src_ref=heads.at[peer],
            dst_ref=attended_ref.at[:, pl.ds(pl.multiple_of(me * width, width), width)],
            send_sem=back_send.at[d - 1], recv_sem=back_recv.at[d - 1],
            device_id=cam_device(peer), device_id_type=MESH_IDS,
        )
        copy.start()
        returning.append(copy)
    for index in arrivals:
        gather.step(index)
    gather.finish()
    for d in range(1, cams):
        source = (me - d + cams) % cams
        region = attended_ref.at[:, pl.ds(pl.multiple_of(source * width, width), width)]
        pltpu.make_async_remote_copy(
            src_ref=region, dst_ref=region, send_sem=back_send.at[d - 1],
            recv_sem=back_recv.at[d - 1], device_id=cam_device(source), device_id_type=MESH_IDS,
        ).wait_recv()
    for copy in returning:
        copy.wait_send()
    own_back.wait()


def fused(query_rows, key_rows, value_rows, flag, out_weight):
    rows, features = query_rows.shape
    cams = lax.axis_size(CAM)
    width = features // cams
    shard, cols = out_weight.shape
    fsdp = lax.axis_size("z") * lax.axis_size("y_lo")
    any_spec = pl.BlockSpec(memory_space=pl.ANY)
    return pl.pallas_call(
        fused_kernel,
        out_shape=(
            jax.ShapeDtypeStruct((shard * fsdp, cols), out_weight.dtype),
            jax.ShapeDtypeStruct((rows, features), query_rows.dtype),
        ),
        in_specs=[any_spec] * 5,
        out_specs=(any_spec, any_spec),
        scratch_shapes=[
            pltpu.VMEM((cams, rows, 3 * width + 128), query_rows.dtype),
            pltpu.VMEM((cams, rows, width), query_rows.dtype),
            pltpu.SemaphoreType.DMA((SENDS,)),
            pltpu.SemaphoreType.DMA((2 * CHUNKS * len(RELATIVE),)),
            pltpu.SemaphoreType.DMA(()),
            pltpu.SemaphoreType.DMA((4 * (cams - 1),)),
            pltpu.SemaphoreType.DMA((4 * (cams - 1),)),
            pltpu.SemaphoreType.DMA((cams - 1,)),
            pltpu.SemaphoreType.DMA((cams - 1,)),
            pltpu.SemaphoreType.DMA((5,)),
        ],
        compiler_params=pltpu.CompilerParams(
            collective_id=0, has_side_effects=True, vmem_limit_bytes=60 * 1024 * 1024
        ),
    )(query_rows, key_rows, value_rows, flag, out_weight)


def local(queries, keys, values, out_weight, block_counts, row_mask):
    query_rows = queries[0]
    row_count = query_rows.shape[0]
    cam_count = lax.axis_size(CAM)
    offsets = jnp.arange(row_count, dtype=jnp.int32)
    row_valid = (row_mask[0] == 1) & (offsets // BLOCK < block_counts[0, 0])

    flag = jnp.broadcast_to(row_valid.astype(jnp.bfloat16)[:, None], (row_count, 128))
    weight_all, attended = fused(query_rows, keys[0], values[0], flag, out_weight)
    projected = jnp.dot(attended, weight_all, preferred_element_type=jnp.float32)
    result = jnp.where(row_valid[:, None], projected, jnp.float32(0.0)).astype(jnp.bfloat16)
    return result[None]


def solution(mesh):
    sub_mesh = Mesh(mesh.devices.reshape(4, 2, 2, 4, 2), CAM + FSDP)
    in_specs = (
        P(FSDP, CAM, None),
        P(FSDP, CAM, None),
        P(FSDP, CAM, None),
        P(FSDP, None),
        P(FSDP, CAM),
        P(FSDP, CAM),
    )
    out_specs = P(FSDP, CAM, None)
    return jax.shard_map(local, mesh=sub_mesh, in_specs=in_specs, out_specs=out_specs, check_vma=False)
```

```python
import functools
import math

import jax
import jax.numpy as jnp
from jax import lax
from jax.experimental import pallas as pl
from jax.experimental.pallas import tpu as pltpu
from jax.sharding import Mesh
from jax.sharding import PartitionSpec as P

HEAD_DIM = 128
BLOCK = 32

CAM = ("x", "y_hi", "core")
FSDP = ("z", "y_lo")
Y = ("y_hi", "y_lo")


MESH_IDS = pl.DeviceIdType.MESH


RELATIVE = ((-1, 0), (1, 0), (0, 1), (2, 0), (-1, 1), (1, 1), (2, 1))
ROUTES = {
    (0, 0): (("z", 1, (0, 1, 2, 3)), ("z", -1, (0, 1, 2, 3)), ("y", 1, (0, 1)), ("y", -1, (2, 3))),
    (-1, 0): (("z", 1, (0, 1)), ("y", 1, (1,)), ("y", -1, (2, 3))),
    (1, 0): (("z", -1, (2, 3)), ("y", 1, (0, 1)), ("y", -1, (2,))),
    (0, 1): (("z", 1, (0,)), ("z", -1, (3,))),
    (2, 0): (),
    (-1, 1): (("z", 1, (0, 1)),),
    (1, 1): (("z", -1, (2, 3)),),
    (2, 1): (),
}
SOURCES = {
    (-1, 0): (("z", -1),) * 4,
    (1, 0): (("z", 1),) * 4,
    (0, 1): (("y", -1),) * 2 + (("y", 1),) * 2,
    (2, 0): (("z", -1),) * 2 + (("z", 1),) * 2,
    (-1, 1): (("z", -1), ("y", -1), ("y", 1), ("y", 1)),
    (1, 1): (("y", -1), ("y", -1), ("y", 1), ("z", 1)),
    (2, 1): (("z", -1),) * 2 + (("z", 1),) * 2,
}
ARRIVALS = (
    ((-1, 0), 0), ((1, 0), 0), ((0, 1), 0), ((0, 1), 2),
    ((-1, 0), 1), ((1, 0), 1), ((0, 1), 1), ((0, 1), 3),
    ((-1, 0), 2), ((1, 0), 2), ((1, 1), 0), ((-1, 1), 2),
    ((-1, 0), 3), ((1, 0), 3), ((1, 1), 1), ((-1, 1), 1), ((1, 1), 2), ((-1, 1), 3),
    ((2, 0), 0), ((2, 0), 2), ((-1, 1), 0), ((1, 1), 3),
    ((2, 0), 1), ((2, 0), 3),
    ((2, 1), 0), ((2, 1), 2), ((2, 1), 1), ((2, 1), 3),
)
CHUNKS = 4
OWN_ORDER = (
    ("y", 1, 0), ("y", -1, 2), ("z", 1, 0), ("z", -1, 0),
    ("y", 1, 1), ("y", -1, 3), ("z", 1, 1), ("z", -1, 1),
    ("z", 1, 2), ("z", -1, 2), ("z", 1, 3), ("z", -1, 3),
)
SENDS = sum(len(c) for routes in ROUTES.values() for _, _, c in routes) + CHUNKS * len(RELATIVE)


class WeightGather:
    def __init__(self, w_ref, out_ref, send, recv, local_sem):
        self.w_ref, self.out_ref, self.send, self.recv = w_ref, out_ref, send, recv
        self.local_sem = local_sem
        self.k = lax.axis_index("core")
        self.z = lax.axis_index("z")
        self.yl = lax.axis_index("y_lo")
        self.y = lax.axis_index("y_hi") * 2 + self.yl
        self.shard = w_ref.shape[0]
        self.half = self.shard // 2
        self.chunk = self.half // CHUNKS
        self.partner = {"core": 1 - self.k}
        self.sent = []

    def device(self, axis, step):
        if axis == "z":
            return {"z": (self.z + step) % 4}
        yy = (self.y + step) % 4
        return {"y_hi": yy // 2, "y_lo": yy % 2}

    def neighbours(self):
        return (self.device("z", 1), self.device("z", -1), self.device("y", 1), self.device("y", -1))

    def shard_of(self, rel):
        dz, flip = rel
        return ((self.z + dz) % 4) * 2 + (self.yl + flip) % 2

    def region(self, rel, kk, c):
        start = self.shard_of(rel) * self.shard + kk * self.half + c * self.chunk
        return self.out_ref.at[pl.ds(pl.multiple_of(start, self.chunk), self.chunk)]

    @staticmethod
    def seen_by(rel, axis, step):
        dz, flip = rel
        if axis == "z":
            return ((dz - step + 1) % 4 - 1, flip)
        return (dz, 1 - flip)

    @staticmethod
    def recv_slot(rel, c, from_partner):
        return (len(RELATIVE) if from_partner else 0) * CHUNKS + RELATIVE.index(rel) * CHUNKS + c

    def copy(self, src, dst, slot, dev):
        copy = pltpu.make_async_remote_copy(
            src_ref=src, dst_ref=dst, send_sem=self.send.at[len(self.sent)],
            recv_sem=self.recv.at[slot], device_id=dev, device_id_type=MESH_IDS,
        )
        copy.start()
        self.sent.append(copy)

    def start(self):
        k, shard, half, chunk = self.k, self.shard, self.half, self.chunk
        own = self.shard_of((0, 0))
        self.local_copy = pltpu.make_async_copy(
            self.w_ref, self.out_ref.at[pl.ds(pl.multiple_of(own * shard, shard), shard)],
            self.local_sem,
        )
        self.local_copy.start()
        for axis, step, c in OWN_ORDER:
            src = self.w_ref.at[pl.ds(pl.multiple_of(k * half + c * chunk, chunk), chunk)]
            slot = self.recv_slot(self.seen_by((0, 0), axis, step), c, False)
            self.copy(src, self.region((0, 0), k, c), slot, self.device(axis, step))

    def arrive(self, rel, kk, c, dev, from_partner):
        piece = self.region(rel, kk, c)
        pltpu.make_async_remote_copy(
            src_ref=piece, dst_ref=piece, send_sem=self.send.at[0],
            recv_sem=self.recv.at[self.recv_slot(rel, c, from_partner)],
            device_id=dev, device_id_type=MESH_IDS,
        ).wait_recv()

    def step(self, index):
        rel, c = ARRIVALS[index]
        axis, step = SOURCES[rel][c]
        self.arrive(rel, self.k, c, self.device(axis, step), False)
        piece = self.region(rel, self.k, c)
        for axis, step, chunks in ROUTES[rel]:
            if c in chunks:
                slot = self.recv_slot(self.seen_by(rel, axis, step), c, False)
                self.copy(piece, piece, slot, self.device(axis, step))
        self.copy(piece, piece, self.recv_slot(rel, c, True), self.partner)

    def finish(self):
        for rel in RELATIVE:
            for c in range(CHUNKS):
                self.arrive(rel, 1 - self.k, c, self.partner, True)
        assert len(self.sent) == SENDS
        for copy in self.sent:
            copy.wait_send()
        self.local_copy.wait()


def cam_device(j):
    return {"x": j // 4, "y_hi": (j // 2) % 2, "core": j % 2}


def fused_kernel(
    q_ref, k_ref, v_ref, flag_ref, w_ref, weight_ref, attended_ref,
    inbox, heads, send, recv, local_sem, a2a_send, a2a_recv, back_send, back_recv, own_sems,
):
    cams = inbox.shape[0]
    rows = inbox.shape[1]
    width = heads.shape[2]
    head_count = width // HEAD_DIM
    sources = (q_ref, k_ref, v_ref, flag_ref)
    me = (lax.axis_index("x") * 2 + lax.axis_index("y_hi")) * 2 + lax.axis_index("core")
    gather = WeightGather(w_ref, weight_ref, send, recv, local_sem)

    barrier = pltpu.get_barrier_semaphore()
    peers = [cam_device((me + d) % cams) for d in range(1, cams)]
    for dev in peers + list(gather.neighbours()):
        pl.semaphore_signal(barrier, inc=1, device_id=dev, device_id_type=MESH_IDS)
    pl.semaphore_wait(barrier, len(peers) + 4)

    gather.start()
    def block(ref, part, j):
        if part == 3:
            return ref
        return ref.at[:, pl.ds(pl.multiple_of(j * width, width), width)]

    def slot_of(ref_inbox, part, j):
        return ref_inbox.at[j, :, pl.ds(part * width, width if part < 3 else 128)]

    own_in = []
    for part, ref in enumerate(sources):
        copy = pltpu.make_async_copy(block(ref, part, me), slot_of(inbox, part, me), own_sems.at[part])
        copy.start()
        own_in.append(copy)
    outgoing = []
    for d in range(1, cams):
        peer = (me + d) % cams
        for part, ref in enumerate(sources):
            copy = pltpu.make_async_remote_copy(
                src_ref=block(ref, part, peer), dst_ref=slot_of(inbox, part, me),
                send_sem=a2a_send.at[4 * (d - 1) + part], recv_sem=a2a_recv.at[4 * (d - 1) + part],
                device_id=cam_device(peer), device_id_type=MESH_IDS,
            )
            copy.start()
            outgoing.append(copy)

    arrivals = iter(range(len(ARRIVALS)))
    for _ in range(10):
        gather.step(next(arrivals))
    for copy in own_in:
        copy.wait()
    for d in range(1, cams):
        source = (me - d + cams) % cams
        for part in range(len(sources)):
            landing = slot_of(inbox, part, source)
            pltpu.make_async_remote_copy(
                src_ref=landing, dst_ref=landing, send_sem=a2a_send.at[4 * (d - 1) + part],
                recv_sem=a2a_recv.at[4 * (d - 1) + part], device_id=cam_device(source),
                device_id_type=MESH_IDS,
            ).wait_recv()

    total = cams * rows
    flags = inbox[:, :, 3 * width : 3 * width + 128].reshape(total, 128)
    counted = lax.dot_general(
        jnp.ones((8, 128), flags.dtype), flags, (((1,), (1,)), ((), ())),
        preferred_element_type=jnp.float32,
    )
    key_ok = counted[0:1, :] > 64.0
    score_scale = 1.0 / math.sqrt(HEAD_DIM)
    group = 2
    per_segment = 2
    for h in range(head_count):
        column = h * HEAD_DIM
        key_h = inbox[:, :, width + column : width + column + HEAD_DIM].reshape(total, HEAD_DIM)
        value_h = inbox[:, :, 2 * width + column : 2 * width + column + HEAD_DIM].reshape(
            total, HEAD_DIM
        )

        def attend_group(g, carry, column=column, key_h=key_h, value_h=value_h):
            first = pl.multiple_of(g * group, group)
            query_block = inbox[pl.ds(first, group), :, column : column + HEAD_DIM].reshape(
                group * rows, HEAD_DIM
            )
            scores = lax.dot_general(
                query_block, key_h, (((1,), (1,)), ((), ())), preferred_element_type=jnp.float32
            ) * score_scale
            scores = jnp.where(key_ok, scores, jnp.float32(-1e30))
            row_top = jnp.max(scores, axis=1, keepdims=True)
            raised = jnp.exp(scores - row_top)
            weights = (raised / jnp.sum(raised, axis=1, keepdims=True)).astype(jnp.bfloat16)
            out = jnp.dot(weights, value_h, preferred_element_type=jnp.float32).astype(jnp.bfloat16)
            heads[pl.ds(first, group), :, column : column + HEAD_DIM] = out.reshape(
                group, rows, HEAD_DIM
            )
            return carry

        for segment in range(cams // group // per_segment):
            lax.fori_loop(segment * per_segment, (segment + 1) * per_segment, attend_group, 0)
            gather.step(next(arrivals))

    for copy in outgoing:
        copy.wait_send()
    own_back = pltpu.make_async_copy(
        heads.at[me], attended_ref.at[:, pl.ds(pl.multiple_of(me * width, width), width)],
        own_sems.at[4],
    )
    own_back.start()
    returning = []
    for d in range(1, cams):
        peer = (me + d) % cams
        copy = pltpu.make_async_remote_copy(
            src_ref=heads.at[peer],
            dst_ref=attended_ref.at[:, pl.ds(pl.multiple_of(me * width, width), width)],
            send_sem=back_send.at[d - 1], recv_sem=back_recv.at[d - 1],
            device_id=cam_device(peer), device_id_type=MESH_IDS,
        )
        copy.start()
        returning.append(copy)
    for index in arrivals:
        gather.step(index)
    gather.finish()
    for d in range(1, cams):
        source = (me - d + cams) % cams
        region = attended_ref.at[:, pl.ds(pl.multiple_of(source * width, width), width)]
        pltpu.make_async_remote_copy(
            src_ref=region, dst_ref=region, send_sem=back_send.at[d - 1],
            recv_sem=back_recv.at[d - 1], device_id=cam_device(source), device_id_type=MESH_IDS,
        ).wait_recv()
    for copy in returning:
        copy.wait_send()
    own_back.wait()


def fused(query_rows, key_rows, value_rows, flag, out_weight):
    rows, features = query_rows.shape
    cams = lax.axis_size(CAM)
    width = features // cams
    shard, cols = out_weight.shape
    fsdp = lax.axis_size("z") * lax.axis_size("y_lo")
    any_spec = pl.BlockSpec(memory_space=pl.ANY)
    return pl.pallas_call(
        fused_kernel,
        out_shape=(
            jax.ShapeDtypeStruct((shard * fsdp, cols), out_weight.dtype),
            jax.ShapeDtypeStruct((rows, features), query_rows.dtype),
        ),
        in_specs=[any_spec] * 5,
        out_specs=(any_spec, any_spec),
        scratch_shapes=[
            pltpu.VMEM((cams, rows, 3 * width + 128), query_rows.dtype),
            pltpu.VMEM((cams, rows, width), query_rows.dtype),
            pltpu.SemaphoreType.DMA((SENDS,)),
            pltpu.SemaphoreType.DMA((2 * CHUNKS * len(RELATIVE),)),
            pltpu.SemaphoreType.DMA(()),
            pltpu.SemaphoreType.DMA((4 * (cams - 1),)),
            pltpu.SemaphoreType.DMA((4 * (cams - 1),)),
            pltpu.SemaphoreType.DMA((cams - 1,)),
            pltpu.SemaphoreType.DMA((cams - 1,)),
            pltpu.SemaphoreType.DMA((5,)),
        ],
        compiler_params=pltpu.CompilerParams(
            collective_id=0, has_side_effects=True, vmem_limit_bytes=60 * 1024 * 1024
        ),
    )(query_rows, key_rows, value_rows, flag, out_weight)


def local(queries, keys, values, out_weight, block_counts, row_mask):
    query_rows = queries[0]
    row_count = query_rows.shape[0]
    cam_count = lax.axis_size(CAM)
    offsets = jnp.arange(row_count, dtype=jnp.int32)
    row_valid = (row_mask[0] == 1) & (offsets // BLOCK < block_counts[0, 0])

    flag = jnp.broadcast_to(row_valid.astype(jnp.bfloat16)[:, None], (row_count, 128))
    weight_all, attended = fused(query_rows, keys[0], values[0], flag, out_weight)
    projected = jnp.dot(attended, weight_all, preferred_element_type=jnp.float32)
    result = jnp.where(row_valid[:, None], projected, jnp.float32(0.0)).astype(jnp.bfloat16)
    return result[None]


def solution(mesh):
    sub_mesh = Mesh(mesh.devices.reshape(4, 2, 2, 4, 2), CAM + FSDP)
    in_specs = (
        P(FSDP, CAM, None),
        P(FSDP, CAM, None),
        P(FSDP, CAM, None),
        P(FSDP, None),
        P(FSDP, CAM),
        P(FSDP, CAM),
    )
    out_specs = P(FSDP, CAM, None)
    return jax.shard_map(local, mesh=sub_mesh, in_specs=in_specs, out_specs=out_specs, check_vma=False)
```

```python
import functools
import math

import jax
import jax.numpy as jnp
from jax import lax
from jax.experimental import pallas as pl
from jax.experimental.pallas import tpu as pltpu
from jax.sharding import Mesh
from jax.sharding import PartitionSpec as P

HEAD_DIM = 128
BLOCK = 32

CAM = ("x", "y_hi", "core")
FSDP = ("z", "y_lo")
Y = ("y_hi", "y_lo")


MESH_IDS = pl.DeviceIdType.MESH


RELATIVE = ((-1, 0), (1, 0), (0, 1), (2, 0), (-1, 1), (1, 1), (2, 1))
ROUTES = {
    (0, 0): (("z", 1, (0, 1, 2, 3)), ("z", -1, (0, 1, 2, 3)), ("y", 1, (0, 1)), ("y", -1, (2, 3))),
    (-1, 0): (("z", 1, (0, 1)), ("y", 1, (1,)), ("y", -1, (2, 3))),
    (1, 0): (("z", -1, (2, 3)), ("y", 1, (0, 1)), ("y", -1, (2,))),
    (0, 1): (("z", 1, (0,)), ("z", -1, (3,))),
    (2, 0): (),
    (-1, 1): (("z", 1, (0, 1)),),
    (1, 1): (("z", -1, (2, 3)),),
    (2, 1): (),
}
SOURCES = {
    (-1, 0): (("z", -1),) * 4,
    (1, 0): (("z", 1),) * 4,
    (0, 1): (("y", -1),) * 2 + (("y", 1),) * 2,
    (2, 0): (("z", -1),) * 2 + (("z", 1),) * 2,
    (-1, 1): (("z", -1), ("y", -1), ("y", 1), ("y", 1)),
    (1, 1): (("y", -1), ("y", -1), ("y", 1), ("z", 1)),
    (2, 1): (("z", -1),) * 2 + (("z", 1),) * 2,
}
ARRIVALS = (
    ((-1, 0), 0), ((1, 0), 0), ((0, 1), 0), ((0, 1), 2),
    ((-1, 0), 1), ((1, 0), 1), ((0, 1), 1), ((0, 1), 3),
    ((-1, 0), 2), ((1, 0), 2), ((1, 1), 0), ((-1, 1), 2),
    ((-1, 0), 3), ((1, 0), 3), ((1, 1), 1), ((-1, 1), 1), ((1, 1), 2), ((-1, 1), 3),
    ((2, 0), 0), ((2, 0), 2), ((-1, 1), 0), ((1, 1), 3),
    ((2, 0), 1), ((2, 0), 3),
    ((2, 1), 0), ((2, 1), 2), ((2, 1), 1), ((2, 1), 3),
)
CHUNKS = 4
OWN_ORDER = (
    ("y", 1, 0), ("y", -1, 2), ("z", 1, 0), ("z", -1, 0),
    ("y", 1, 1), ("y", -1, 3), ("z", 1, 1), ("z", -1, 1),
    ("z", 1, 2), ("z", -1, 2), ("z", 1, 3), ("z", -1, 3),
)
SENDS = sum(len(c) for routes in ROUTES.values() for _, _, c in routes) + CHUNKS * len(RELATIVE)


class WeightGather:
    def __init__(self, w_ref, out_ref, send, recv, local_sem):
        self.w_ref, self.out_ref, self.send, self.recv = w_ref, out_ref, send, recv
        self.local_sem = local_sem
        self.k = lax.axis_index("core")
        self.z = lax.axis_index("z")
        self.yl = lax.axis_index("y_lo")
        self.y = lax.axis_index("y_hi") * 2 + self.yl
        self.shard = w_ref.shape[0]
        self.half = self.shard // 2
        self.chunk = self.half // CHUNKS
        self.partner = {"core": 1 - self.k}
        self.sent = []

    def device(self, axis, step):
        if axis == "z":
            return {"z": (self.z + step) % 4}
        yy = (self.y + step) % 4
        return {"y_hi": yy // 2, "y_lo": yy % 2}

    def neighbours(self):
        return (self.device("z", 1), self.device("z", -1), self.device("y", 1), self.device("y", -1))

    def shard_of(self, rel):
        dz, flip = rel
        return ((self.z + dz) % 4) * 2 + (self.yl + flip) % 2

    def region(self, rel, kk, c):
        start = self.shard_of(rel) * self.shard + kk * self.half + c * self.chunk
        return self.out_ref.at[pl.ds(pl.multiple_of(start, self.chunk), self.chunk)]

    @staticmethod
    def seen_by(rel, axis, step):
        dz, flip = rel
        if axis == "z":
            return ((dz - step + 1) % 4 - 1, flip)
        return (dz, 1 - flip)

    @staticmethod
    def recv_slot(rel, c, from_partner):
        return (len(RELATIVE) if from_partner else 0) * CHUNKS + RELATIVE.index(rel) * CHUNKS + c

    def copy(self, src, dst, slot, dev):
        copy = pltpu.make_async_remote_copy(
            src_ref=src, dst_ref=dst, send_sem=self.send.at[len(self.sent)],
            recv_sem=self.recv.at[slot], device_id=dev, device_id_type=MESH_IDS,
        )
        copy.start()
        self.sent.append(copy)

    def start(self):
        k, shard, half, chunk = self.k, self.shard, self.half, self.chunk
        own = self.shard_of((0, 0))
        self.local_copy = pltpu.make_async_copy(
            self.w_ref, self.out_ref.at[pl.ds(pl.multiple_of(own * shard, shard), shard)],
            self.local_sem,
        )
        self.local_copy.start()
        for axis, step, c in OWN_ORDER:
            src = self.w_ref.at[pl.ds(pl.multiple_of(k * half + c * chunk, chunk), chunk)]
            slot = self.recv_slot(self.seen_by((0, 0), axis, step), c, False)
            self.copy(src, self.region((0, 0), k, c), slot, self.device(axis, step))

    def arrive(self, rel, kk, c, dev, from_partner):
        piece = self.region(rel, kk, c)
        pltpu.make_async_remote_copy(
            src_ref=piece, dst_ref=piece, send_sem=self.send.at[0],
            recv_sem=self.recv.at[self.recv_slot(rel, c, from_partner)],
            device_id=dev, device_id_type=MESH_IDS,
        ).wait_recv()

    def step(self, index):
        rel, c = ARRIVALS[index]
        axis, step = SOURCES[rel][c]
        self.arrive(rel, self.k, c, self.device(axis, step), False)
        piece = self.region(rel, self.k, c)
        for axis, step, chunks in ROUTES[rel]:
            if c in chunks:
                slot = self.recv_slot(self.seen_by(rel, axis, step), c, False)
                self.copy(piece, piece, slot, self.device(axis, step))
        self.copy(piece, piece, self.recv_slot(rel, c, True), self.partner)

    def finish(self):
        for rel in RELATIVE:
            for c in range(CHUNKS):
                self.arrive(rel, 1 - self.k, c, self.partner, True)
        assert len(self.sent) == SENDS
        for copy in self.sent:
            copy.wait_send()
        self.local_copy.wait()


def cam_device(j):
    return {"x": j // 4, "y_hi": (j // 2) % 2, "core": j % 2}


def fused_kernel(
    q_ref, k_ref, v_ref, flag_ref, w_ref, weight_ref, attended_ref,
    inbox, heads, send, recv, local_sem, a2a_send, a2a_recv, back_send, back_recv, own_sems,
):
    cams = inbox.shape[0]
    rows = inbox.shape[1]
    width = heads.shape[2]
    head_count = width // HEAD_DIM
    sources = (q_ref, k_ref, v_ref, flag_ref)
    me = (lax.axis_index("x") * 2 + lax.axis_index("y_hi")) * 2 + lax.axis_index("core")
    gather = WeightGather(w_ref, weight_ref, send, recv, local_sem)

    barrier = pltpu.get_barrier_semaphore()
    peers = [cam_device((me + d) % cams) for d in range(1, cams)]
    for dev in peers + list(gather.neighbours()):
        pl.semaphore_signal(barrier, inc=1, device_id=dev, device_id_type=MESH_IDS)
    pl.semaphore_wait(barrier, len(peers) + 4)

    gather.start()
    def block(ref, part, j):
        if part == 3:
            return ref
        return ref.at[:, pl.ds(pl.multiple_of(j * width, width), width)]

    def slot_of(ref_inbox, part, j):
        return ref_inbox.at[j, :, pl.ds(part * width, width if part < 3 else 128)]

    own_in = []
    for part, ref in enumerate(sources):
        copy = pltpu.make_async_copy(block(ref, part, me), slot_of(inbox, part, me), own_sems.at[part])
        copy.start()
        own_in.append(copy)
    outgoing = []
    for d in range(1, cams):
        peer = (me + d) % cams
        for part, ref in enumerate(sources):
            copy = pltpu.make_async_remote_copy(
                src_ref=block(ref, part, peer), dst_ref=slot_of(inbox, part, me),
                send_sem=a2a_send.at[4 * (d - 1) + part], recv_sem=a2a_recv.at[4 * (d - 1) + part],
                device_id=cam_device(peer), device_id_type=MESH_IDS,
            )
            copy.start()
            outgoing.append(copy)

    arrivals = iter(range(len(ARRIVALS)))
    for _ in range(12):
        gather.step(next(arrivals))
    for copy in own_in:
        copy.wait()
    for d in range(1, cams):
        source = (me - d + cams) % cams
        for part in range(len(sources)):
            landing = slot_of(inbox, part, source)
            pltpu.make_async_remote_copy(
                src_ref=landing, dst_ref=landing, send_sem=a2a_send.at[4 * (d - 1) + part],
                recv_sem=a2a_recv.at[4 * (d - 1) + part], device_id=cam_device(source),
                device_id_type=MESH_IDS,
            ).wait_recv()

    total = cams * rows
    flags = inbox[:, :, 3 * width : 3 * width + 128].reshape(total, 128)
    counted = lax.dot_general(
        jnp.ones((8, 128), flags.dtype), flags, (((1,), (1,)), ((), ())),
        preferred_element_type=jnp.float32,
    )
    key_ok = counted[0:1, :] > 64.0
    score_scale = 1.0 / math.sqrt(HEAD_DIM)
    group = 2
    per_segment = 2
    for h in range(head_count):
        column = h * HEAD_DIM
        key_h = inbox[:, :, width + column : width + column + HEAD_DIM].reshape(total, HEAD_DIM)
        value_h = inbox[:, :, 2 * width + column : 2 * width + column + HEAD_DIM].reshape(
            total, HEAD_DIM
        )

        def attend_group(g, carry, column=column, key_h=key_h, value_h=value_h):
            first = pl.multiple_of(g * group, group)
            query_block = inbox[pl.ds(first, group), :, column : column + HEAD_DIM].reshape(
                group * rows, HEAD_DIM
            )
            scores = lax.dot_general(
                query_block, key_h, (((1,), (1,)), ((), ())), preferred_element_type=jnp.float32
            ) * score_scale
            scores = jnp.where(key_ok, scores, jnp.float32(-1e30))
            row_top = jnp.max(scores, axis=1, keepdims=True)
            raised = jnp.exp(scores - row_top)
            weights = (raised / jnp.sum(raised, axis=1, keepdims=True)).astype(jnp.bfloat16)
            out = jnp.dot(weights, value_h, preferred_element_type=jnp.float32).astype(jnp.bfloat16)
            heads[pl.ds(first, group), :, column : column + HEAD_DIM] = out.reshape(
                group, rows, HEAD_DIM
            )
            return carry

        for segment in range(cams // group // per_segment):
            lax.fori_loop(segment * per_segment, (segment + 1) * per_segment, attend_group, 0)
            gather.step(next(arrivals))

    for copy in outgoing:
        copy.wait_send()
    own_back = pltpu.make_async_copy(
        heads.at[me], attended_ref.at[:, pl.ds(pl.multiple_of(me * width, width), width)],
        own_sems.at[4],
    )
    own_back.start()
    returning = []
    for d in range(1, cams):
        peer = (me + d) % cams
        copy = pltpu.make_async_remote_copy(
            src_ref=heads.at[peer],
            dst_ref=attended_ref.at[:, pl.ds(pl.multiple_of(me * width, width), width)],
            send_sem=back_send.at[d - 1], recv_sem=back_recv.at[d - 1],
            device_id=cam_device(peer), device_id_type=MESH_IDS,
        )
        copy.start()
        returning.append(copy)
    for index in arrivals:
        gather.step(index)
    gather.finish()
    for d in range(1, cams):
        source = (me - d + cams) % cams
        region = attended_ref.at[:, pl.ds(pl.multiple_of(source * width, width), width)]
        pltpu.make_async_remote_copy(
            src_ref=region, dst_ref=region, send_sem=back_send.at[d - 1],
            recv_sem=back_recv.at[d - 1], device_id=cam_device(source), device_id_type=MESH_IDS,
        ).wait_recv()
    for copy in returning:
        copy.wait_send()
    own_back.wait()


def fused(query_rows, key_rows, value_rows, flag, out_weight):
    rows, features = query_rows.shape
    cams = lax.axis_size(CAM)
    width = features // cams
    shard, cols = out_weight.shape
    fsdp = lax.axis_size("z") * lax.axis_size("y_lo")
    any_spec = pl.BlockSpec(memory_space=pl.ANY)
    return pl.pallas_call(
        fused_kernel,
        out_shape=(
            jax.ShapeDtypeStruct((shard * fsdp, cols), out_weight.dtype),
            jax.ShapeDtypeStruct((rows, features), query_rows.dtype),
        ),
        in_specs=[any_spec] * 5,
        out_specs=(any_spec, any_spec),
        scratch_shapes=[
            pltpu.VMEM((cams, rows, 3 * width + 128), query_rows.dtype),
            pltpu.VMEM((cams, rows, width), query_rows.dtype),
            pltpu.SemaphoreType.DMA((SENDS,)),
            pltpu.SemaphoreType.DMA((2 * CHUNKS * len(RELATIVE),)),
            pltpu.SemaphoreType.DMA(()),
            pltpu.SemaphoreType.DMA((4 * (cams - 1),)),
            pltpu.SemaphoreType.DMA((4 * (cams - 1),)),
            pltpu.SemaphoreType.DMA((cams - 1,)),
            pltpu.SemaphoreType.DMA((cams - 1,)),
            pltpu.SemaphoreType.DMA((5,)),
        ],
        compiler_params=pltpu.CompilerParams(
            collective_id=0, has_side_effects=True, vmem_limit_bytes=60 * 1024 * 1024
        ),
    )(query_rows, key_rows, value_rows, flag, out_weight)


def local(queries, keys, values, out_weight, block_counts, row_mask):
    query_rows = queries[0]
    row_count = query_rows.shape[0]
    cam_count = lax.axis_size(CAM)
    offsets = jnp.arange(row_count, dtype=jnp.int32)
    row_valid = (row_mask[0] == 1) & (offsets // BLOCK < block_counts[0, 0])

    flag = jnp.broadcast_to(row_valid.astype(jnp.bfloat16)[:, None], (row_count, 128))
    weight_all, attended = fused(query_rows, keys[0], values[0], flag, out_weight)
    projected = jnp.dot(attended, weight_all, preferred_element_type=jnp.float32)
    result = jnp.where(row_valid[:, None], projected, jnp.float32(0.0)).astype(jnp.bfloat16)
    return result[None]


def solution(mesh):
    sub_mesh = Mesh(mesh.devices.reshape(4, 2, 2, 4, 2), CAM + FSDP)
    in_specs = (
        P(FSDP, CAM, None),
        P(FSDP, CAM, None),
        P(FSDP, CAM, None),
        P(FSDP, None),
        P(FSDP, CAM),
        P(FSDP, CAM),
    )
    out_specs = P(FSDP, CAM, None)
    return jax.shard_map(local, mesh=sub_mesh, in_specs=in_specs, out_specs=out_specs, check_vma=False)
```
